128 devices in a mesh: region: 8 (over x, core), species: 16 (over z, y).
Axes of the slice: x: 4, y: 4, z: 4, core: 2. Of those that a mesh axis runs over, the one named last changes fastest.
Arguments:
- concentrations: float32 [256, 1024, 256], P('species', 'region'), may hold values from 0.05 to 5
- diffusion: float32 [256], P('species'), may hold values from 0.02 to 0.08
- courant_x: float32 [1024, 256], P('region'), may hold values from -0.2 to 0.2
- courant_y: float32 [1024, 256], P('region'), may hold values from -0.2 to 0.2
- log_rate: float32 [4, 768], replicated, may hold values from -3 to 0
- reactants: int32 [256, 768], replicated, may hold values from 0 to 1, as said below
- products: int32 [768, 256], replicated, may hold values from 0 to 1, as said below
- block_class: int32 [2048], P(('region', 'species')), may hold values from 0 to 3, as said below
- send_slot: int32 [2048], P(('region', 'species')), may hold values from -1 to 15, as said below
Outputs:
- reacted: float32 [256, 1024, 256], P('species', 'region')
The draws below stay inside these ranges and needn't reach their ends.
Inputs may be any that keep to these rules, and one draw needn't show every extreme that they name: `send_slot`: block n lies on the device with region index n // 256 and species index (n // 16) % 16. A value t >= 0 marks a stiff block and names slot t % 2 of region t // 2; -1 marks the others. Among the blocks of one species index every value from 0 to 15 occurs exactly once; for each species index one device holds exactly 8 marked blocks, and no device holds more. The marked blocks of one device name different regions. `block_class`: A block marked in send_slot has class 3; every other block has a lower class. `reactants`: every column has one or two ones, in different rows. `products`: every row has one or two ones, in different columns.
All inputs are finite; a program needn't handle non-finite values.
Results may differ from the reference program's by a relative error of at most 0.0003.
Values sent between devices are 32-bit elements; how exact they have to be, the bound alone decides.
No kernel may reach another device: no remote copies, remote signals or barrier semaphores. Data moves between devices by JAX's collectives and lax.ppermute only.
A program may use at most 128 MiB of HBM per device.

```python
import math
import jax
import jax.numpy as jnp
from jax import lax

SPECIES = 256
REACT = 768
CX = 128
NY = 256
STEPS = 3
ITERS = 2
SUB = 2
CLASSES = 4
QUEUE = 2
STIFF_MOST = 8
NX = 1024
N_REGION = 8
N_SPECIES = 16


def stiff_plan(key):
    blocks_dev = CX * NY // (128 * N_SPECIES)
    total = N_REGION * QUEUE
    base = jax.random.fold_in(key, 7001)
    keys = jax.random.split(base, 5)
    heaviest = jax.random.randint(keys[0], (N_SPECIES,), 0, N_REGION)
    others = jax.random.randint(keys[1], (N_SPECIES, total), 0, N_REGION - 1)
    units = jnp.arange(total)
    region_of = jnp.where(units[None, :] < STIFF_MOST, heaviest[:, None], (heaviest[:, None] + 1 + others) % N_REGION)
    earlier = units[None, :, None] > units[None, None, :]
    same_region = region_of[:, :, None] == region_of[:, None, :]
    ranks = jnp.sum((same_region & earlier).astype(jnp.int32), axis=2)
    scores = jax.random.randint(keys[2], (N_SPECIES, N_REGION, blocks_dev), 0, 2 ** 20)
    orders = jnp.argsort(scores * blocks_dev + jnp.arange(blocks_dev), axis=-1).astype(jnp.int32)
    groups = jnp.broadcast_to(jnp.arange(N_SPECIES)[:, None], (N_SPECIES, total))
    block_of = orders[groups, region_of, ranks]
    sorted_units = jnp.argsort(region_of * total + units[None, :], axis=-1).astype(jnp.int32)
    position = jnp.argsort(sorted_units, axis=-1).astype(jnp.int32)
    rotation = jax.random.randint(keys[3], (N_SPECIES, 1), 0, N_REGION)
    label_scores = jax.random.randint(keys[4], (N_SPECIES, N_REGION), 0, 2 ** 20)
    labels = jnp.argsort(label_scores * N_REGION + jnp.arange(N_REGION)[None, :], axis=-1).astype(jnp.int32)
    target = jnp.take_along_axis(labels, (position + rotation) % N_REGION, axis=1)
    slot_of = (target * QUEUE + position // N_REGION).astype(jnp.int32)
    return (region_of, groups, block_of, slot_of)


def draw_send_slot(key, part):
    blocks_dev = CX * NY // (128 * N_SPECIES)
    region_of, groups, block_of, slot_of = stiff_plan(key)
    layout = jnp.full((N_REGION, N_SPECIES, blocks_dev), -1, jnp.int32)
    layout = layout.at[region_of, groups, block_of].set(slot_of)
    return layout.reshape(-1)


def draw_block_class(key, part):
    blocks_dev = CX * NY // (128 * N_SPECIES)
    region_of, groups, block_of, slot_of = stiff_plan(key)
    lower = jax.random.randint(jax.random.fold_in(key, 7002), (N_REGION, N_SPECIES, blocks_dev), 0, CLASSES - 1)
    layout = lower.at[region_of, groups, block_of].set(CLASSES - 1)
    return layout.reshape(-1).astype(jnp.int32)


def pair_table(key, salt):
    keys = jax.random.split(jax.random.fold_in(key, salt), 3)
    first_pick = jax.random.randint(keys[0], (REACT,), 0, SPECIES)
    offset = jax.random.randint(keys[1], (REACT,), 1, SPECIES)
    second_pick = (first_pick + offset) % SPECIES
    doubled = jax.random.randint(keys[2], (REACT,), 0, 2)
    species_ids = jnp.arange(SPECIES)[:, None]
    chosen = (species_ids == first_pick[None, :]) | (species_ids == second_pick[None, :]) & (doubled[None, :] == 1)
    return chosen.astype(jnp.int32)


def draw_reactants(key, part):
    return pair_table(key, 7101)


def draw_products(key, part):
    return pair_table(key, 7201).T


def block_levels(own_key, shape, cuts, low, largest):
    gain = 1.0
    for dim, parts in cuts:
        heights = jax.random.uniform(jax.random.fold_in(jax.random.fold_in(own_key, 6), dim), (parts,), jnp.float32, low / len(cuts), largest / len(cuts))
        gain = gain * jnp.repeat(jnp.exp(heights), shape[dim] // parts).reshape((-1,) + (1,) * (len(shape) - 1 - dim))
    return gain


def setup_inputs(seed: int = 0) -> dict:
    seeds = jax.random.split(jax.random.key(seed), 10)
    concentrations = jnp.clip(jnp.exp(math.log(5.0) - 4.6051702 * jax.random.uniform(seeds[0], (SPECIES, NX, NY), jnp.float32) ** block_levels(seeds[0], (SPECIES, NX, NY), ((0, 16), (1, 8)), -0.2, 0.2)), 0.05, 5.0)
    diffusion = jnp.clip(0.02 + 0.06 * jax.random.uniform(seeds[1], (SPECIES,), jnp.float32) ** block_levels(seeds[1], (SPECIES,), ((0, 16),), -0.2, 0.2), 0.02, 0.08)
    courant_x = jnp.clip(jax.random.uniform(seeds[2], (NX, NY), jnp.float32, -0.2, 0.2) * block_levels(seeds[2], (NX, NY), ((0, 8),), -0.4, 0.0), -0.2, 0.2)
    courant_y = jnp.clip(jax.random.uniform(seeds[3], (NX, NY), jnp.float32, -0.2, 0.2) * block_levels(seeds[3], (NX, NY), ((0, 8),), -0.4, 0.0), -0.2, 0.2)
    log_rate = jnp.clip(jax.random.uniform(seeds[4], (CLASSES, REACT), jnp.float32, -3.0, 0.0), -3.0, 0.0)
    reactants = draw_reactants(jax.random.fold_in(seeds[9], 71), 0)
    products = draw_products(jax.random.fold_in(seeds[9], 71), 0)
    block_class = draw_block_class(jax.random.fold_in(seeds[9], 71), 0)
    send_slot = draw_send_slot(jax.random.fold_in(seeds[9], 71), 0)
    return {"concentrations": concentrations, "diffusion": diffusion, "courant_x": courant_x, "courant_y": courant_y, "log_rate": log_rate, "reactants": reactants, "products": products, "block_class": block_class, "send_slot": send_slot}


floor_value = 0.05
highest = lax.Precision.HIGHEST


def minmod(first_diff, second):
    signed = jnp.sign(first_diff)
    return signed * jnp.maximum(0.0, jnp.minimum(jnp.abs(first_diff), signed * second))


def face_flux(field, courant, diffuse, axis_index):
    length = field.shape[axis_index]
    behind = lax.slice_in_dim(field, 0, length - 3, axis=axis_index)
    center = lax.slice_in_dim(field, 1, length - 2, axis=axis_index)
    forward = lax.slice_in_dim(field, 2, length - 1, axis=axis_index)
    beyond = lax.slice_in_dim(field, 3, length, axis=axis_index)
    upwind = center + 0.5 * (1.0 - courant) * minmod(center - behind, forward - center)
    downwind = forward - 0.5 * (1.0 + courant) * minmod(forward - center, beyond - forward)
    return courant * jnp.where(courant >= 0.0, upwind, downwind) - diffuse * (forward - center)


def substep(padded, wind_rows, cross_rows, diffuse):
    height = padded.shape[1]
    row_faces = 0.5 * (wind_rows[1:height - 2] + wind_rows[2:height - 1])
    flux_rows = face_flux(padded, row_faces[None], diffuse, 1)
    interior = padded[:, 2:height - 2]
    widened = jnp.pad(interior, ((0, 0), (0, 0), (2, 2)))
    cross_pad = jnp.pad(cross_rows, ((0, 0), (2, 2)))
    extent = cross_pad.shape[1]
    across = 0.5 * (cross_pad[:, 1:extent - 2] + cross_pad[:, 2:extent - 1])
    flux_cols = face_flux(widened, across[None], diffuse, 2)
    return interior - (flux_rows[:, 1:] - flux_rows[:, :-1]) - (flux_cols[:, :, 1:] - flux_cols[:, :, :-1])


def backward_euler(anchor, rate_logs, reactant_coef, product_coef, stride):
    iterate = anchor
    for iteration in range(ITERS):
        summed = lax.dot_general(reactant_coef, jnp.log(iterate), (((0,), (0,)), ((), ())), precision=highest, preferred_element_type=jnp.float32)
        reaction_rates = jnp.exp(rate_logs + summed)
        making = lax.dot_general(product_coef, reaction_rates, (((0,), (0,)), ((), ())), precision=highest, preferred_element_type=jnp.float32)
        losing = jnp.dot(reactant_coef, reaction_rates, precision=highest, preferred_element_type=jnp.float32)
        iterate = (anchor + stride * making) / (1.0 + stride * losing / iterate)
    return iterate


def stiff_steps(anchor, rate_logs, reactant_coef, product_coef):
    iterate = anchor
    for counter in range(SUB):
        iterate = backward_euler(iterate, rate_logs, reactant_coef, product_coef, 1.0 / SUB)
    return iterate


def reference(concentrations, diffusion, courant_x, courant_y, log_rate, reactants, products, block_class, send_slot):
    group_size = SPECIES // N_SPECIES
    wind_pad = jnp.pad(courant_x, ((2, 2), (0, 0)))

    def transport(pieces):
        concentration, spread = pieces
        diffuse = spread[:, None, None]
        for counter in range(STEPS):
            concentration = substep(jnp.pad(concentration, ((0, 0), (2, 2), (0, 0))), wind_pad, courant_y, diffuse)
        return concentration

    advected = lax.map(transport, (concentrations.reshape(N_SPECIES, group_size, NX, NY), diffusion.reshape(N_SPECIES, group_size)))
    piece_cells = CX * NY // N_SPECIES
    piece_count = NX * NY // piece_cells
    pieces_conc = advected.reshape(SPECIES, piece_count, piece_cells).transpose(1, 0, 2)
    cell_class = jnp.repeat(block_class, 128).reshape(piece_count, piece_cells)
    stiff_flags = jnp.repeat(send_slot >= 0, 128).reshape(piece_count, piece_cells)
    reactant_coef = reactants.astype(jnp.float32)
    product_coef = products.astype(jnp.float32)
    rate_table = log_rate.T

    def react(pieces):
        values, classes, flags = pieces
        anchor = jnp.maximum(values, floor_value)
        rate_logs = rate_table[:, classes]
        single_step = backward_euler(anchor, rate_logs, reactant_coef, product_coef, 1.0)
        multi_step = stiff_steps(anchor, rate_logs, reactant_coef, product_coef)
        return jnp.where(flags[None, :], multi_step, single_step)

    reacted = lax.map(react, (pieces_conc, cell_class, stiff_flags))
    return reacted.transpose(1, 0, 2).reshape(SPECIES, NX, NY)
```

```python
import functools

import jax
import jax.numpy as jnp
from jax import lax
from jax.experimental import pallas as pl
from jax.experimental.pallas import tpu as pltpu
from jax.sharding import PartitionSpec as P

STEPS = 3
ITERS = 2
SUB = 2
FLOOR = 0.05
EDGE = 8
DEEP = 2 * STEPS
LANES = 128
TILE = 4
bf16 = jnp.bfloat16
f32 = jnp.float32


def median0(p, r):
    return jnp.maximum(jnp.minimum(p, r), jnp.minimum(jnp.maximum(p, r), 0.0))


def shift_left(pair, lane):
    a, b = (pltpu.roll(v, LANES - 1, 1) for v in pair)
    last = lane == LANES - 1
    return jnp.where(last, b, a), jnp.where(last, 0.0, b)


def shift_right(pair, first, lane):
    a, b = (pltpu.roll(v, 1, 1) for v in pair)
    head = lane == 0
    return jnp.where(head, first, a), jnp.where(head, a, b)


def halves(v):
    return v[:, :LANES], v[:, LANES:]


def face_coefs(a):
    size = jnp.abs(a)
    return 0.5 * size * (1.0 - size)


def store_coefs(cx, cy, coef):
    ax = 0.5 * (cx + jnp.concatenate([cx[1:], cx[:1]], axis=0))
    edge = lax.broadcasted_iota(jnp.int32, cy.shape, 1) == 2 * LANES - 1
    ay = 0.5 * (cy + jnp.where(edge, 0.0, jnp.concatenate([cy[:, 1:], cy[:, :1]], axis=1)))
    al = 0.5 * cy[:, :LANES]
    al_weight = jnp.where(al < 0.0, face_coefs(al), 0.0)
    pairs = [halves(v) for v in (ax, face_coefs(ax), ay, face_coefs(ay))]
    pairs.append((jnp.minimum(al, 0.0), al_weight))
    for k, pair in enumerate(pairs):
        coef[2 * k] = pair[0]
        coef[2 * k + 1] = pair[1]


def one_flux(q, qn, d, m, mn, a, e, nu):
    up = a >= 0.0
    return a * jnp.where(up, q, qn) + e * jnp.where(up, m, mn) - nu * d


def sweep(load, store, coef, nu, lo, hi, unroll, keep=None):
    group = nu.shape[0]
    lane = lax.broadcasted_iota(jnp.int32, (group, LANES), 1)

    def spread(which, row):
        return tuple(coef[2 * which + k, pl.ds(row, group, stride=0), :] for k in (0, 1))

    def x_flux(row, q, qn, d, m, mn):
        a, e = spread(0, row), spread(1, row)
        return tuple(one_flux(q[i], qn[i], d[i], m[i], mn[i], a[i], e[i], nu) for i in (0, 1))

    def diff(q, qn):
        return tuple(y - x for x, y in zip(q, qn))

    def limited(p, r):
        return tuple(median0(x, y) for x, y in zip(p, r))

    qa, qb, qc, qd = (load(lo + k) for k in (-2, -1, 0, 1))
    da, db, dc = diff(qa, qb), diff(qb, qc), diff(qc, qd)
    mb, mc = limited(da, db), limited(db, dc)
    behind = x_flux(lo - 1, qb, qc, db, mb, mc)

    def row_step(row, carry):
        q, qn, d, m, behind = carry
        qnn = load(row + 2)
        dn = diff(qn, qnn)
        mn = limited(d, dn)
        fx = x_flux(row, q, qn, d, m, mn)
        right = shift_left(q, lane)
        g = diff(q, right)
        s = limited(shift_right(g, q[0], lane), g)
        sn = shift_left(s, lane)
        a, e = spread(2, row), spread(3, row)
        fy = tuple(one_flux(q[i], right[i], g[i], s[i], sn[i], a[i], e[i], nu) for i in (0, 1))
        la, le = spread(4, row)
        fl = shift_right(fy, (la - nu) * q[0] + le * s[0], lane)
        new = tuple(q[i] - (fx[i] - behind[i]) - (fy[i] - fl[i]) for i in (0, 1))
        if keep is not None:
            scale = keep(row)
            new = tuple(v * scale for v in new)
        store(row, new)
        return qn, qnn, dn, mn, fx

    def steps(i, carry):
        for k in range(unroll):
            carry = row_step(lo + i * unroll + k, carry)
        return carry

    count = hi - lo
    carry = lax.fori_loop(0, count // unroll, steps, (qc, qd, dc, mc, behind))
    for row in range(lo + count // unroll * unroll, hi):
        carry = row_step(row, carry)


def buffer_access(buf):
    def load(row):
        return buf[row, :, :LANES], buf[row, :, LANES:]

    def store(row, pair):
        buf[row, :, :LANES] = pair[0]
        buf[row, :, LANES:] = pair[1]

    return load, store


def interior_kernel(conc0, conc1, cx, cy, diffuse, left, right, coef, one, two):
    group = diffuse.shape[0]
    rows = cx.shape[0]
    nu = jnp.broadcast_to(diffuse[...], (group, LANES))
    store_coefs(cx[...], cy[...], coef)
    load1, store1 = buffer_access(one)
    load2, store2 = buffer_access(two)

    def load0(row):
        return tuple(c[pl.ds(row, group, stride=rows), :] for c in (conc0, conc1))

    def store3(row, pair):
        left[row] = pair[0]
        right[row] = pair[1]

    sweep(load0, store1, coef, nu, 2, rows - 2, 4)
    sweep(load1, store2, coef, nu, 4, rows - 4, 4)
    sweep(load2, store3, coef, nu, 6, rows - 6, 4)


def edge_kernel(
    place,
    conc0,
    conc1,
    cx,
    cy,
    before0,
    before1,
    after0,
    after1,
    diffuse,
    left_in,
    right_in,
    left,
    right,
    coef,
    one,
    two,
    three,
):
    group = diffuse.shape[0]
    top = pl.program_id(0) == 0
    nu = jnp.broadcast_to(diffuse[...], (group, LANES))
    own = 2 * EDGE
    slab = own + EDGE

    def fill(first, halo, halo_first):
        for side, (conc, rim) in enumerate(zip((conc0, conc1), halo)):
            lanes = slice(side * LANES, (side + 1) * LANES)
            for k in range(own):
                one[first + k, :, lanes] = conc[:, k, :]
            for k in range(EDGE):
                one[halo_first + k, :, lanes] = rim[pl.ds(k, group, stride=EDGE), :]
        winds = jnp.concatenate([h[group * EDGE :] for h in halo], axis=1)
        rim = winds[:EDGE], winds[EDGE:]
        order = (lambda a, b: (a, b)) if halo_first else (lambda a, b: (b, a))
        store_coefs(
            jnp.concatenate(order(cx[...], rim[0]), axis=0),
            jnp.concatenate(order(cy[...], rim[1]), axis=0),
            coef,
        )

    @pl.when(top)
    def _():
        fill(EDGE, (before0, before1), 0)

    @pl.when(jnp.logical_not(top))
    def _():
        fill(0, (after0, after1), own)

    open_top = jnp.logical_and(top, place[0] == 0)
    open_end = jnp.logical_and(jnp.logical_not(top), place[0] == place[1] - 1)

    def keep(row):
        out = jnp.logical_or(
            jnp.logical_and(open_top, row < EDGE), jnp.logical_and(open_end, row >= own)
        )
        return jnp.where(out, 0.0, 1.0)

    load1, store1 = buffer_access(one)
    load2, store2 = buffer_access(two)
    load3, store3 = buffer_access(three)
    sweep(load1, store2, coef, nu, 4, slab - 4, 4, keep)
    sweep(load2, store3, coef, nu, 6, slab - 6, 4, keep)
    sweep(load3, store1, coef, nu, 8, slab - 8, 4)
    left[...] = left_in[...]
    right[...] = right_in[...]

    @pl.when(top)
    def _():
        for k in range(DEEP):
            left[k] = one[EDGE + k, :, :LANES]
            right[k] = one[EDGE + k, :, LANES:]

    @pl.when(jnp.logical_not(top))
    def _():
        for k in range(EDGE - DEEP, EDGE):
            left[k] = one[EDGE + k, :, :LANES]
            right[k] = one[EDGE + k, :, LANES:]


def split(x):
    high = x.astype(bf16)
    return high, (x - high.astype(f32)).astype(bf16)


def table_dot(table, x):
    high, low = split(x)
    return jnp.dot(table, high, preferred_element_type=f32) + jnp.dot(
        table, low, preferred_element_type=f32
    )


def euler(state, logs, step, reac, both):
    species = state.shape[0]
    g = state
    for _ in range(ITERS):
        rates = jnp.exp(logs + table_dot(reac, jnp.log(g)))
        made_lost = table_dot(both, rates)
        g = (state + step * made_lost[:species]) / (1.0 + step * made_lost[species:] / g)
    return g


def chemistry_kernel(classes, slots, x, log_table, reac, both, out, result, listed):
    peers, blocks, group, _ = x.shape
    species = peers * group
    count = jnp.int32(0)
    for b in range(blocks):
        listed[count] = b
        count = count + (slots[b] >= 0).astype(jnp.int32)

    def tile(chosen, first):
        states, logs, lengths = [], [], []
        for b in chosen:
            if first:
                states.append(jnp.maximum(x[:, b].reshape(species, LANES), FLOOR))
                length = jnp.where(slots[b] >= 0, 1.0 / SUB, 1.0)
            else:
                states.append(result[b])
                length = 1.0 / SUB
            lengths.append(jnp.full((1, LANES), length, f32))
            logs.append(log_table[classes[b]])
        g = euler(
            jnp.concatenate(states, axis=1),
            jnp.concatenate(logs, axis=1),
            jnp.concatenate(lengths, axis=1),
            reac[...],
            both[...],
        )
        for i, b in enumerate(chosen):
            piece = g[:, i * LANES : (i + 1) * LANES]
            result[b] = piece
            for k in range(0, species, 8):
                out[pl.ds(k * blocks + b, 8, stride=blocks), :] = piece[k : k + 8]

    @pl.loop(0, blocks // TILE)
    def _(i):
        tile([i * TILE + j for j in range(TILE)], True)

    for _ in range(SUB - 1):

        @pl.loop(0, (count + TILE - 1) // TILE)
        def _(i):
            tile([listed[jnp.minimum(i * TILE + j, count - 1)] for j in range(TILE)], False)


def chemistry(x, classes, slots, log_table, reac, both):
    peers, blocks, group, _ = x.shape
    species = peers * group
    vmem = pl.BlockSpec(memory_space=pltpu.VMEM)
    smem = pl.BlockSpec(memory_space=pltpu.SMEM)
    return pl.pallas_call(
        chemistry_kernel,
        out_shape=jax.ShapeDtypeStruct((species * blocks, LANES), f32),
        in_specs=[smem, smem, vmem, vmem, vmem, vmem],
        out_specs=vmem,
        scratch_shapes=[
            pltpu.VMEM((blocks, species, LANES), f32),
            pltpu.SMEM((blocks,), jnp.int32),
        ],
        compiler_params=pltpu.CompilerParams(vmem_limit_bytes=40 << 20),
        name="chemistry",
    )(classes, slots, x, log_table, reac, both)


def per_device(
    concentrations,
    diffusion,
    courant_x,
    courant_y,
    log_rate,
    reactants,
    products,
    block_class,
    send_slot,
):
    group, rows, columns = concentrations.shape
    species, reactions = reactants.shape
    peers = species // group
    regions = lax.axis_size("region")
    up = [(i, (i + 1) % regions) for i in range(regions - 1)]
    down = [(j, i) for i, j in up]
    winds = jnp.stack([courant_x, courant_y])
    last = jnp.concatenate([concentrations[:, rows - EDGE :], winds[:, rows - EDGE :]], axis=0)
    leading = jnp.concatenate([concentrations[:, :EDGE], winds[:, :EDGE]], axis=0)
    before = lax.ppermute(last, "region", up)
    after = lax.ppermute(leading, "region", down)
    diffuse = diffusion[:, None]
    vmem = pl.BlockSpec(memory_space=pltpu.VMEM)
    half = jax.ShapeDtypeStruct((rows, group, LANES), f32)
    row_buffer = pltpu.VMEM((rows, group, columns), f32)
    left, right = pl.pallas_call(
        interior_kernel,
        out_shape=(half, half),
        grid=(1,),
        in_specs=[
            pl.BlockSpec((group * rows, LANES), lambda i: (0, 0)),
            pl.BlockSpec((group * rows, LANES), lambda i: (0, 1)),
            vmem,
            vmem,
            vmem,
        ],
        out_specs=(vmem, vmem),
        scratch_shapes=[pltpu.VMEM((10, rows, LANES), f32), row_buffer, row_buffer],
        compiler_params=pltpu.CompilerParams(vmem_limit_bytes=40 << 20),
        name="interior",
    )(*[concentrations.reshape(group * rows, columns)] * 2, courant_x, courant_y, diffuse)

    place = jnp.stack([lax.axis_index("region"), jnp.int32(regions)]).astype(jnp.int32)
    own = 2 * EDGE
    far = rows // own - 1
    far_out = rows // EDGE - 1
    slab_buffer = pltpu.VMEM((own + EDGE, group, columns), f32)

    def conc_spec(side):
        return pl.BlockSpec((group, own, LANES), lambda i: (0, i * far, side))

    def halo_spec(side):
        return pl.BlockSpec(((group + 2) * EDGE, LANES), lambda i: (0, side))

    wind_spec = pl.BlockSpec((own, columns), lambda i: (i * far, 0))
    half_spec = pl.BlockSpec((EDGE, group, LANES), lambda i: (i * far_out, 0, 0))
    left, right = pl.pallas_call(
        edge_kernel,
        grid=(2,),
        out_shape=(half, half),
        in_specs=[
            pl.BlockSpec(memory_space=pltpu.SMEM),
            conc_spec(0),
            conc_spec(1),
            wind_spec,
            wind_spec,
            halo_spec(0),
            halo_spec(1),
            halo_spec(0),
            halo_spec(1),
            pl.BlockSpec((group, 1), lambda i: (0, 0)),
            half_spec,
            half_spec,
        ],
        out_specs=(half_spec, half_spec),
        scratch_shapes=[pltpu.VMEM((10, own + EDGE, LANES), f32)] + [slab_buffer] * 3,
        input_output_aliases={10: 0, 11: 1},
        name="edges",
    )(
        place,
        concentrations,
        concentrations,
        courant_x,
        courant_y,
        *[before.reshape((group + 2) * EDGE, columns)] * 2,
        *[after.reshape((group + 2) * EDGE, columns)] * 2,
        diffuse,
        left,
        right,
    )

    reac = reactants.T.astype(bf16)
    both = jnp.concatenate([products.T, reactants], axis=0).astype(bf16)
    log_table = jnp.broadcast_to(log_rate[:, :, None], log_rate.shape + (LANES,))
    blocks = rows // peers
    classes = block_class.reshape(blocks, 2)
    slots = send_slot.reshape(blocks, 2)
    done = []
    for side, part in enumerate((left, right)):
        mine = lax.all_to_all(part, "species", split_axis=0, concat_axis=0, tiled=True)
        reacted = chemistry(
            mine.reshape(peers, blocks, group, LANES),
            classes[:, side],
            slots[:, side],
            log_table,
            reac,
            both,
        )
        done.append(
            lax.all_to_all(
                reacted.reshape(peers, group, blocks, LANES),
                "species",
                split_axis=0,
                concat_axis=0,
                tiled=True,
            )
        )
    whole = jnp.concatenate(done, axis=3)
    return whole.transpose(1, 0, 2, 3).reshape(group, rows, columns)


def solution(mesh):
    in_specs = (
        P("species", "region", None),
        P("species"),
        P("region", None),
        P("region", None),
        P(),
        P(),
        P(),
        P(("region", "species")),
        P(("region", "species")),
    )
    out_specs = P("species", "region", None)
    return jax.shard_map(
        per_device, mesh=mesh, in_specs=in_specs, out_specs=out_specs, check_vma=False
    )
```

```python
import functools

import jax
import jax.numpy as jnp
from jax import lax
from jax.experimental import pallas as pl
from jax.experimental.pallas import tpu as pltpu
from jax.sharding import PartitionSpec as P

STEPS = 3
ITERS = 2
SUB = 2
FLOOR = 0.05
EDGE = 8
LANES = 128
TILE = 4
bf16 = jnp.bfloat16
f32 = jnp.float32


def median0(p, r):
    return jnp.maximum(jnp.minimum(p, r), jnp.minimum(jnp.maximum(p, r), 0.0))


def shift_left(pair, lane):
    a, b = (pltpu.roll(v, LANES - 1, 1) for v in pair)
    last = lane == LANES - 1
    return jnp.where(last, b, a), jnp.where(last, 0.0, b)


def shift_right(pair, first, lane):
    a, b = (pltpu.roll(v, 1, 1) for v in pair)
    head = lane == 0
    return jnp.where(head, first, a), jnp.where(head, a, b)


def halves(v):
    return v[:, :LANES], v[:, LANES:]


def face_coefs(a):
    size = jnp.abs(a)
    return 0.5 * size * (1.0 - size)


def store_coefs(cx, cy, coef):
    ax = 0.5 * (cx + jnp.concatenate([cx[1:], cx[:1]], axis=0))
    edge = lax.broadcasted_iota(jnp.int32, cy.shape, 1) == 2 * LANES - 1
    ay = 0.5 * (cy + jnp.where(edge, 0.0, jnp.concatenate([cy[:, 1:], cy[:, :1]], axis=1)))
    al = 0.5 * cy[:, :LANES]
    al_weight = jnp.where(al < 0.0, face_coefs(al), 0.0)
    pairs = [halves(v) for v in (ax, face_coefs(ax), ay, face_coefs(ay))]
    pairs.append((jnp.minimum(al, 0.0), al_weight))
    for k, pair in enumerate(pairs):
        coef[2 * k] = pair[0]
        coef[2 * k + 1] = pair[1]


def one_flux(q, qn, d, m, mn, a, e, nu):
    up = a >= 0.0
    return a * jnp.where(up, q, qn) + e * jnp.where(up, m, mn) - nu * d


def sweep(load, store, coef, nu, lo, hi, unroll, keep=None):
    group = nu.shape[0]
    lane = lax.broadcasted_iota(jnp.int32, (group, LANES), 1)

    def spread(which, row):
        return tuple(coef[2 * which + k, pl.ds(row, group, stride=0), :] for k in (0, 1))

    def x_flux(row, q, qn, d, m, mn):
        a, e = spread(0, row), spread(1, row)
        return tuple(one_flux(q[i], qn[i], d[i], m[i], mn[i], a[i], e[i], nu) for i in (0, 1))

    def diff(q, qn):
        return tuple(y - x for x, y in zip(q, qn))

    def limited(p, r):
        return tuple(median0(x, y) for x, y in zip(p, r))

    qa, qb, qc, qd = (load(lo + k) for k in (-2, -1, 0, 1))
    da, db, dc = diff(qa, qb), diff(qb, qc), diff(qc, qd)
    mb, mc = limited(da, db), limited(db, dc)
    behind = x_flux(lo - 1, qb, qc, db, mb, mc)

    def row_step(row, carry):
        q, qn, d, m, behind = carry
        qnn = load(row + 2)
        dn = diff(qn, qnn)
        mn = limited(d, dn)
        fx = x_flux(row, q, qn, d, m, mn)
        right = shift_left(q, lane)
        g = diff(q, right)
        s = limited(shift_right(g, q[0], lane), g)
        sn = shift_left(s, lane)
        a, e = spread(2, row), spread(3, row)
        fy = tuple(one_flux(q[i], right[i], g[i], s[i], sn[i], a[i], e[i], nu) for i in (0, 1))
        la, le = spread(4, row)
        fl = shift_right(fy, (la - nu) * q[0] + le * s[0], lane)
        new = tuple(q[i] - (fx[i] - behind[i]) - (fy[i] - fl[i]) for i in (0, 1))
        if keep is not None:
            scale = keep(row)
            new = tuple(v * scale for v in new)
        store(row, new)
        return qn, qnn, dn, mn, fx

    def steps(i, carry):
        for k in range(unroll):
            carry = row_step(lo + i * unroll + k, carry)
        return carry

    count = hi - lo
    carry = lax.fori_loop(0, count // unroll, steps, (qc, qd, dc, mc, behind))
    for row in range(lo + count // unroll * unroll, hi):
        carry = row_step(row, carry)


def buffer_access(buf):
    def load(row):
        return buf[row, :, :LANES], buf[row, :, LANES:]

    def store(row, pair):
        buf[row, :, :LANES] = pair[0]
        buf[row, :, LANES:] = pair[1]

    return load, store


def start_all(copies):
    for copy in copies:
        copy.start()


def wait_all(copies):
    for copy in copies:
        copy.wait()


def spread_species(diffuse, group):
    lane = lax.broadcasted_iota(jnp.int32, (group, LANES), 0)
    nu = jnp.zeros((group, LANES), f32)
    for k in range(group):
        nu = jnp.where(lane == k, diffuse[k], nu)
    return nu


def raw_access(block):
    group, rows, _ = block.shape[1:]
    flat = [block.at[k].reshape(group * rows, LANES) for k in (0, 1)]

    def load(row):
        return tuple(part[pl.ds(row, group, stride=rows), :] for part in flat)

    return load


def three_sweeps(load, store, coef, nu, one, two, rows, unrolls, keep=None):
    load1, store1 = buffer_access(one)
    load2, store2 = buffer_access(two)
    sweep(load, store1, coef, nu, 4, rows - 4, unrolls[0], keep)
    sweep(load1, store2, coef, nu, 6, rows - 6, unrolls[1], keep)
    sweep(load2, store, coef, nu, 8, rows - 8, unrolls[2])


def store_grouped(out, base):
    def store(row, pair):
        at = row - EDGE
        place, inner = base + lax.shift_right_logical(at, 3), lax.bitwise_and(at, 7)
        out[place, 0, inner] = pair[0]
        out[place, 1, inner] = pair[1]

    return store


def middle_kernel(diffuse, conc, cx, cy, out, raw, wx, wy, coef, one, two, sems):
    group, rows = raw.shape[1:3]
    first = conc.shape[1] // 4 - EDGE
    copies = [
        pltpu.make_async_copy(src.at[pl.ds(first, rows)], dst, sems.at[k])
        for k, (src, dst) in enumerate(((cx, wx), (cy, wy)))
    ]
    copies += [
        pltpu.make_async_copy(
            conc.at[:, pl.ds(first, rows), pl.ds(k * LANES, LANES)], raw.at[k], sems.at[2 + k]
        )
        for k in (0, 1)
    ]
    start_all(copies)
    nu = spread_species(diffuse, group)
    wait_all(copies[:2])
    store_coefs(wx[...], wy[...], coef)
    wait_all(copies[2:])
    three_sweeps(
        raw_access(raw), store_grouped(out, 0), coef, nu, one, two, rows, (18, 17, 16)
    )


def edge_kernel(
    diffuse, place, conc, cx, cy, before, after, out, raw, wx, wy, coef, one, two, sems
):
    group, rows = raw.shape[2:4]
    total = conc.shape[1]
    own = rows - EDGE
    copies = []

    def copy(src, dst):
        copies.append(pltpu.make_async_copy(src, dst, sems.at[len(copies)]))

    for slab, halo, own_first, own_at, halo_at in (
        (0, before, 0, EDGE, 0),
        (1, after, total - own, 0, own),
    ):
        for k, (wind, dst) in enumerate(((cx, wx), (cy, wy))):
            copy(wind.at[pl.ds(own_first, own)], dst.at[slab, pl.ds(own_at, own)])
            copy(halo.at[group + k], dst.at[slab, pl.ds(halo_at, EDGE)])
        for k in (0, 1):
            lanes = pl.ds(k * LANES, LANES)
            dst = raw.at[slab, k]
            copy(conc.at[:, pl.ds(own_first, own), lanes], dst.at[:, pl.ds(own_at, own)])
            copy(halo.at[pl.ds(0, group), :, lanes], dst.at[:, pl.ds(halo_at, EDGE)])
    start_all(copies)
    nu = spread_species(diffuse, group)
    wait_all(copies)

    @pl.loop(0, 2)
    def _(slab):
        store_coefs(wx[slab], wy[slab], coef)
        open_top = jnp.logical_and(slab == 0, place[0] == 0)
        open_end = jnp.logical_and(slab == 1, place[0] == place[1] - 1)

        def keep(row):
            outside = jnp.logical_or(
                jnp.logical_and(open_top, row < EDGE), jnp.logical_and(open_end, row >= own)
            )
            return jnp.where(outside, 0.0, 1.0)

        three_sweeps(
            raw_access(raw.at[slab]),
            store_grouped(out, slab * 4),
            coef,
            nu,
            one,
            two,
            rows,
            (10, 12, 16),
            keep,
        )


def split(x):
    high = x.astype(bf16)
    return high, (x - high.astype(f32)).astype(bf16)


def table_dot(table, x):
    high, low = split(x)
    return jnp.dot(table, high, preferred_element_type=f32) + jnp.dot(
        table, low, preferred_element_type=f32
    )


def euler(state, logs, step, reac, both):
    species = state.shape[0]
    g = state
    for _ in range(ITERS):
        rates = jnp.exp(logs + table_dot(reac, jnp.log(g)))
        made_lost = table_dot(both, rates)
        g = (state + step * made_lost[:species]) / (1.0 + step * made_lost[species:] / g)
    return g


def chemistry_kernel(info, start, x, log_table, reac, both, out, result, answer, listed, sem):
    peers, blocks, group, _ = x.shape
    species = peers * group
    codes = [info[start[0] + 2 * b] for b in range(blocks)]
    count = jnp.int32(0)
    for b in range(blocks):
        listed[1, b] = lax.bitwise_and(codes[b], 3)
        listed[2, b] = lax.shift_right_logical(codes[b], 2)
        listed[0, count] = b
        count = count + lax.shift_right_logical(codes[b], 2)

    def tile(chosen, first):
        states, logs, lengths = [], [], []
        for b in chosen:
            if first:
                states.append(jnp.maximum(x[:, b].reshape(species, LANES), FLOOR))
                length = jnp.where(listed[2, b] > 0, 1.0 / SUB, 1.0)
            else:
                states.append(result[b])
                length = 1.0 / SUB
            lengths.append(jnp.full((1, LANES), length, f32))
            logs.append(log_table[listed[1, b]])
        g = euler(
            jnp.concatenate(states, axis=1),
            jnp.concatenate(logs, axis=1),
            jnp.concatenate(lengths, axis=1),
            reac[...],
            both[...],
        )
        for i, b in enumerate(chosen):
            piece = g[:, i * LANES : (i + 1) * LANES]
            result[b] = piece
            for k in range(0, species, 8):
                answer[pl.ds(k * blocks + b, 8, stride=blocks), :] = piece[k : k + 8]

    @pl.loop(0, blocks // TILE)
    def _(i):
        tile([i * TILE + j for j in range(TILE)], True)

    for _ in range(SUB - 1):

        @pl.loop(0, (count + TILE - 1) // TILE)
        def _(i):
            tile([listed[0, jnp.minimum(i * TILE + j, count - 1)] for j in range(TILE)], False)


    copy = pltpu.make_async_copy(answer, out, sem)
    copy.start()
    copy.wait()


def chemistry(x, info, start, log_table, reac, both):
    peers, blocks, group, _ = x.shape
    species = peers * group
    vmem = pl.BlockSpec(memory_space=pltpu.VMEM)
    smem = pl.BlockSpec(memory_space=pltpu.SMEM)
    return pl.pallas_call(
        chemistry_kernel,
        out_shape=jax.ShapeDtypeStruct((species * blocks, LANES), f32),
        in_specs=[smem, smem, vmem, vmem, vmem, vmem],
        out_specs=pl.BlockSpec(memory_space=pltpu.HBM),
        scratch_shapes=[
            pltpu.VMEM((blocks, species, LANES), f32),
            pltpu.VMEM((species * blocks, LANES), f32),
            pltpu.SMEM((3, blocks), jnp.int32),
            pltpu.SemaphoreType.DMA,
        ],
        compiler_params=pltpu.CompilerParams(vmem_limit_bytes=20 << 20),
        name="chemistry",
    )(info, start, x, log_table, reac, both)


def per_device(
    concentrations,
    diffusion,
    courant_x,
    courant_y,
    log_rate,
    reactants,
    products,
    block_class,
    send_slot,
):
    group, rows, columns = concentrations.shape
    species, reactions = reactants.shape
    peers = species // group
    regions = lax.axis_size("region")
    up = [(i, (i + 1) % regions) for i in range(regions - 1)]
    down = [(j, i) for i, j in up]
    hbm = pl.BlockSpec(memory_space=pltpu.HBM)
    smem = pl.BlockSpec(memory_space=pltpu.SMEM)
    places = rows // (2 * EDGE)
    part = jax.ShapeDtypeStruct((places, 2, EDGE, group, LANES), f32)

    def buffers(slab_rows):
        row_buffer = pltpu.VMEM((slab_rows, group, columns), f32)
        return [pltpu.VMEM((10, slab_rows, LANES), f32), row_buffer, row_buffer]

    code = block_class + 4 * (send_slot >= 0).astype(jnp.int32)
    info = lax.all_gather(code, "species", tiled=True)

    slab_rows = rows // 2 + 2 * EDGE
    middle = pl.pallas_call(
        middle_kernel,
        out_shape=part,
        in_specs=[smem, hbm, hbm, hbm],
        out_specs=pl.BlockSpec(memory_space=pltpu.VMEM),
        scratch_shapes=[
            pltpu.VMEM((2, group, slab_rows, LANES), f32),
            pltpu.VMEM((slab_rows, columns), f32),
            pltpu.VMEM((slab_rows, columns), f32),
            *buffers(slab_rows),
            pltpu.SemaphoreType.DMA((4,)),
        ],
        compiler_params=pltpu.CompilerParams(vmem_limit_bytes=16 << 20),
        name="middle",
    )(diffusion, concentrations, courant_x, courant_y)

    winds = jnp.stack([courant_x, courant_y])
    last = jnp.concatenate([concentrations[:, rows - EDGE :], winds[:, rows - EDGE :]], axis=0)
    leading = jnp.concatenate([concentrations[:, :EDGE], winds[:, :EDGE]], axis=0)
    before = lax.ppermute(last, "region", up)
    after = lax.ppermute(leading, "region", down)
    place = jnp.stack([lax.axis_index("region"), jnp.int32(regions)]).astype(jnp.int32)
    slab_rows = rows // 4 + 2 * EDGE
    edges = pl.pallas_call(
        edge_kernel,
        out_shape=part,
        in_specs=[smem, smem, hbm, hbm, hbm, hbm, hbm],
        out_specs=pl.BlockSpec(memory_space=pltpu.VMEM),
        scratch_shapes=[
            pltpu.VMEM((2, 2, group, slab_rows, LANES), f32),
            pltpu.VMEM((2, slab_rows, columns), f32),
            pltpu.VMEM((2, slab_rows, columns), f32),
            *buffers(slab_rows),
            pltpu.SemaphoreType.DMA((16,)),
        ],
        compiler_params=pltpu.CompilerParams(vmem_limit_bytes=16 << 20),
        name="edges",
    )(diffusion, place, concentrations, courant_x, courant_y, before, after)

    reac = reactants.T.astype(bf16)
    both = jnp.concatenate([products.T, reactants], axis=0).astype(bf16)
    log_table = jnp.broadcast_to(log_rate[:, :, None], log_rate.shape + (LANES,))
    mine = lax.axis_index("species").astype(jnp.int32)
    lower, parity = mine // 2, mine % 2
    done = []
    for slab, source in (
        (middle, lower + peers // 4),
        (edges, lower + jnp.where(lower < peers // 4, 0, peers // 2)),
    ):
        gathered = lax.all_to_all(
            slab.reshape(peers, EDGE, group, LANES), "species", split_axis=0, concat_axis=0, tiled=True
        )
        start = (source * 2 * EDGE + parity).reshape(1)
        reacted = chemistry(gathered, info, start, log_table, reac, both)
        done.append(
            lax.all_to_all(
                reacted.reshape(peers, group, EDGE, LANES),
                "species",
                split_axis=0,
                concat_axis=0,
                tiled=True,
            )
        )
    tiles = [v.reshape(places, 2, group, EDGE, LANES) for v in done]
    whole = jnp.concatenate([tiles[1][: places // 2], tiles[0], tiles[1][places // 2 :]], axis=0)
    return whole.transpose(2, 0, 3, 1, 4).reshape(group, rows, columns)


def solution(mesh):
    in_specs = (
        P("species", "region", None),
        P("species"),
        P("region", None),
        P("region", None),
        P(),
        P(),
        P(),
        P(("region", "species")),
        P(("region", "species")),
    )
    out_specs = P("species", "region", None)
    return jax.shard_map(
        per_device, mesh=mesh, in_specs=in_specs, out_specs=out_specs, check_vma=False
    )
```

```python
import functools

import jax
import jax.numpy as jnp
from jax import lax
from jax.experimental import pallas as pl
from jax.experimental.pallas import tpu as pltpu
from jax.sharding import PartitionSpec as P

STEPS = 3
ITERS = 2
SUB = 2
FLOOR = 0.05
EDGE = 8
LANES = 128
TILE = 4
bf16 = jnp.bfloat16
f32 = jnp.float32


def median0(p, r):
    return jnp.maximum(jnp.minimum(p, r), jnp.minimum(jnp.maximum(p, r), 0.0))


def shift_left(pair, lane):
    a, b = (pltpu.roll(v, LANES - 1, 1) for v in pair)
    last = lane == LANES - 1
    return jnp.where(last, b, a), jnp.where(last, 0.0, b)


def shift_right(pair, first, lane):
    a, b = (pltpu.roll(v, 1, 1) for v in pair)
    head = lane == 0
    return jnp.where(head, first, a), jnp.where(head, a, b)


def halves(v):
    return v[:, :LANES], v[:, LANES:]


def face_coefs(a):
    size = jnp.abs(a)
    return 0.5 * size * (1.0 - size)


def store_coefs(cx, cy, coef):
    ax = 0.5 * (cx + jnp.concatenate([cx[1:], cx[:1]], axis=0))
    edge = lax.broadcasted_iota(jnp.int32, cy.shape, 1) == 2 * LANES - 1
    ay = 0.5 * (cy + jnp.where(edge, 0.0, jnp.concatenate([cy[:, 1:], cy[:, :1]], axis=1)))
    al = 0.5 * cy[:, :LANES]
    al_weight = jnp.where(al < 0.0, face_coefs(al), 0.0)
    pairs = [halves(v) for v in (ax, face_coefs(ax), ay, face_coefs(ay))]
    pairs.append((jnp.minimum(al, 0.0), al_weight))
    for k, pair in enumerate(pairs):
        coef[2 * k] = pair[0]
        coef[2 * k + 1] = pair[1]


def one_flux(q, qn, d, m, mn, a, e, nu):
    up = a >= 0.0
    return a * jnp.where(up, q, qn) + e * jnp.where(up, m, mn) - nu * d


def sweep(load, store, coef, nu, lo, hi, unroll, keep=None):
    group = nu.shape[0]
    lane = lax.broadcasted_iota(jnp.int32, (group, LANES), 1)

    def spread(which, row):
        return tuple(coef[2 * which + k, pl.ds(row, group, stride=0), :] for k in (0, 1))

    def x_flux(row, q, qn, d, m, mn):
        a, e = spread(0, row), spread(1, row)
        return tuple(one_flux(q[i], qn[i], d[i], m[i], mn[i], a[i], e[i], nu) for i in (0, 1))

    def diff(q, qn):
        return tuple(y - x for x, y in zip(q, qn))

    def limited(p, r):
        return tuple(median0(x, y) for x, y in zip(p, r))

    qa, qb, qc, qd = (load(lo + k) for k in (-2, -1, 0, 1))
    da, db, dc = diff(qa, qb), diff(qb, qc), diff(qc, qd)
    mb, mc = limited(da, db), limited(db, dc)
    behind = x_flux(lo - 1, qb, qc, db, mb, mc)

    def row_step(row, carry):
        q, qn, d, m, behind = carry
        qnn = load(row + 2)
        dn = diff(qn, qnn)
        mn = limited(d, dn)
        fx = x_flux(row, q, qn, d, m, mn)
        right = shift_left(q, lane)
        g = diff(q, right)
        s = limited(shift_right(g, q[0], lane), g)
        sn = shift_left(s, lane)
        a, e = spread(2, row), spread(3, row)
        fy = tuple(one_flux(q[i], right[i], g[i], s[i], sn[i], a[i], e[i], nu) for i in (0, 1))
        la, le = spread(4, row)
        fl = shift_right(fy, (la - nu) * q[0] + le * s[0], lane)
        new = tuple(q[i] - (fx[i] - behind[i]) - (fy[i] - fl[i]) for i in (0, 1))
        if keep is not None:
            scale = keep(row)
            new = tuple(v * scale for v in new)
        store(row, new)
        return qn, qnn, dn, mn, fx

    def steps(i, carry):
        for k in range(unroll):
            carry = row_step(lo + i * unroll + k, carry)
        return carry

    count = hi - lo
    carry = lax.fori_loop(0, count // unroll, steps, (qc, qd, dc, mc, behind))
    for row in range(lo + count // unroll * unroll, hi):
        carry = row_step(row, carry)


def buffer_access(buf):
    def load(row):
        return buf[row, :, :LANES], buf[row, :, LANES:]

    def store(row, pair):
        buf[row, :, :LANES] = pair[0]
        buf[row, :, LANES:] = pair[1]

    return load, store


def start_all(copies):
    for copy in copies:
        copy.start()


def wait_all(copies):
    for copy in copies:
        copy.wait()


def spread_species(diffuse, group):
    lane = lax.broadcasted_iota(jnp.int32, (group, LANES), 0)
    nu = jnp.zeros((group, LANES), f32)
    for k in range(group):
        nu = jnp.where(lane == k, diffuse[k], nu)
    return nu


def raw_access(block):
    group, rows, _ = block.shape[1:]
    flat = [block.at[k].reshape(group * rows, LANES) for k in (0, 1)]

    def load(row):
        return tuple(part[pl.ds(row, group, stride=rows), :] for part in flat)

    return load


def three_sweeps(load, store, coef, nu, one, two, rows, unrolls, keep=None):
    load1, store1 = buffer_access(one)
    load2, store2 = buffer_access(two)
    sweep(load, store1, coef, nu, 4, rows - 4, unrolls[0], keep)
    sweep(load1, store2, coef, nu, 6, rows - 6, unrolls[1], keep)
    sweep(load2, store, coef, nu, 8, rows - 8, unrolls[2])


def store_grouped(out, base, group):
    def store(row, pair):
        at = row - EDGE
        place = 2 * (base + lax.shift_right_logical(at, 3))
        line = pl.multiple_of(lax.bitwise_and(at, EDGE - 1) * group, group)
        out[place, pl.ds(line, group), :] = pair[0]
        out[place + 1, pl.ds(line, group), :] = pair[1]

    return store


def middle_kernel(diffuse, classes, slots, conc, cx, cy, out, raw, wx, wy, coef, one, two, sems):
    group, rows = raw.shape[1:3]
    first = conc.shape[1] // 4 - EDGE
    copies = [
        pltpu.make_async_copy(src.at[pl.ds(first, rows)], dst, sems.at[k])
        for k, (src, dst) in enumerate(((cx, wx), (cy, wy)))
    ]
    copies += [
        pltpu.make_async_copy(
            conc.at[:, pl.ds(first, rows), pl.ds(k * LANES, LANES)], raw.at[k], sems.at[2 + k]
        )
        for k in (0, 1)
    ]
    start_all(copies)
    nu = spread_species(diffuse, group)
    lane = lax.broadcasted_iota(jnp.int32, (EDGE, LANES), 1)
    codes = jnp.zeros((EDGE, LANES), f32)
    for k in range(classes.shape[0]):
        code = classes[k] + jnp.where(slots[k] >= 0, 4, 0)
        codes = jnp.where(lane == k, code.astype(f32), codes)
    for k in range(out.shape[0]):
        out[k, EDGE * group :, :] = codes
    wait_all(copies[:2])
    store_coefs(wx[...], wy[...], coef)
    wait_all(copies[2:])
    three_sweeps(
        raw_access(raw), store_grouped(out, 0, group), coef, nu, one, two, rows, (18, 17, 16)
    )


def edge_kernel(
    diffuse, place, conc, cx, cy, before, after, out, raw, wx, wy, coef, one, two, sems
):
    group, rows = raw.shape[2:4]
    total = conc.shape[1]
    own = rows - EDGE
    copies = []

    def copy(src, dst):
        copies.append(pltpu.make_async_copy(src, dst, sems.at[len(copies)]))

    for slab, halo, own_first, own_at, halo_at in (
        (0, before, 0, EDGE, 0),
        (1, after, total - own, 0, own),
    ):
        for k, (wind, dst) in enumerate(((cx, wx), (cy, wy))):
            copy(wind.at[pl.ds(own_first, own)], dst.at[slab, pl.ds(own_at, own)])
            copy(halo.at[group + k], dst.at[slab, pl.ds(halo_at, EDGE)])
        for k in (0, 1):
            lanes = pl.ds(k * LANES, LANES)
            dst = raw.at[slab, k]
            copy(conc.at[:, pl.ds(own_first, own), lanes], dst.at[:, pl.ds(own_at, own)])
            copy(halo.at[pl.ds(0, group), :, lanes], dst.at[:, pl.ds(halo_at, EDGE)])
    start_all(copies)
    nu = spread_species(diffuse, group)
    wait_all(copies)

    @pl.loop(0, 2)
    def _(slab):
        store_coefs(wx[slab], wy[slab], coef)
        open_top = jnp.logical_and(slab == 0, place[0] == 0)
        open_end = jnp.logical_and(slab == 1, place[0] == place[1] - 1)

        def keep(row):
            outside = jnp.logical_or(
                jnp.logical_and(open_top, row < EDGE), jnp.logical_and(open_end, row >= own)
            )
            return jnp.where(outside, 0.0, 1.0)

        three_sweeps(
            raw_access(raw.at[slab]),
            store_grouped(out, slab * 4, group),
            coef,
            nu,
            one,
            two,
            rows,
            (10, 12, 16),
            keep,
        )


def split(x):
    high = x.astype(bf16)
    return high, (x - high.astype(f32)).astype(bf16)


def table_dot(table, x):
    high, low = split(x)
    return jnp.dot(table, high, preferred_element_type=f32) + jnp.dot(
        table, low, preferred_element_type=f32
    )


def euler(state, logs, step, reac, both):
    species = state.shape[0]
    g = state
    for _ in range(ITERS):
        rates = jnp.exp(logs + table_dot(reac, jnp.log(g)))
        made_lost = table_dot(both, rates)
        g = (state + step * made_lost[:species]) / (1.0 + step * made_lost[species:] / g)
    return g


def first_line(block, group):
    return block * group if isinstance(block, int) else pl.multiple_of(block * group, group)


def chemistry_kernel(info, start, x, log_table, reac, both, out, result, answer, listed, sem):
    peers, blocks = x.shape[0], EDGE
    species = reac.shape[1]
    group = species // peers
    codes = [info[start[0] + 2 * b] for b in range(blocks)]
    count = jnp.int32(0)
    for b in range(blocks):
        listed[1, b] = lax.bitwise_and(codes[b], 3)
        listed[2, b] = lax.shift_right_logical(codes[b], 2)
        listed[0, count] = b
        count = count + lax.shift_right_logical(codes[b], 2)

    def tile(chosen, first):
        states, logs, lengths = [], [], []
        for b in chosen:
            if first:
                states.append(jnp.maximum(x[:, pl.ds(first_line(b, group), group), :].reshape(species, LANES), FLOOR))
                length = jnp.where(listed[2, b] > 0, 1.0 / SUB, 1.0)
            else:
                states.append(result[b])
                length = 1.0 / SUB
            lengths.append(jnp.full((1, LANES), length, f32))
            logs.append(log_table[listed[1, b]])
        g = euler(
            jnp.concatenate(states, axis=1),
            jnp.concatenate(logs, axis=1),
            jnp.concatenate(lengths, axis=1),
            reac[...],
            both[...],
        )
        for i, b in enumerate(chosen):
            piece = g[:, i * LANES : (i + 1) * LANES]
            result[b] = piece
            for k in range(0, species, 8):
                answer[pl.ds(k * blocks + b, 8, stride=blocks), :] = piece[k : k + 8]

    @pl.loop(0, blocks // TILE)
    def _(i):
        tile([i * TILE + j for j in range(TILE)], True)

    for _ in range(SUB - 1):

        @pl.loop(0, (count + TILE - 1) // TILE)
        def _(i):
            tile([listed[0, jnp.minimum(i * TILE + j, count - 1)] for j in range(TILE)], False)


    copy = pltpu.make_async_copy(answer, out, sem)
    copy.start()
    copy.wait()


def chemistry(x, info, start, log_table, reac, both):
    species, blocks = reac.shape[1], EDGE
    vmem = pl.BlockSpec(memory_space=pltpu.VMEM)
    smem = pl.BlockSpec(memory_space=pltpu.SMEM)
    return pl.pallas_call(
        chemistry_kernel,
        out_shape=pltpu.HBM((species * blocks, LANES), f32),
        in_specs=[smem, smem, vmem, vmem, vmem, vmem],
        out_specs=pl.BlockSpec(memory_space=pltpu.HBM),
        scratch_shapes=[
            pltpu.VMEM((blocks, species, LANES), f32),
            pltpu.VMEM((species * blocks, LANES), f32),
            pltpu.SMEM((3, blocks), jnp.int32),
            pltpu.SemaphoreType.DMA,
        ],
        compiler_params=pltpu.CompilerParams(vmem_limit_bytes=20 << 20),
        cost_estimate=pl.CostEstimate(
            flops=24 * species * reac.shape[0] * 2 * blocks * LANES,
            transcendentals=4 * (species + reac.shape[0]) * blocks * LANES,
            bytes_accessed=8 << 20,
        ),
        name="chemistry",
    )(info, start, x, log_table, reac, both)


def per_device(
    concentrations,
    diffusion,
    courant_x,
    courant_y,
    log_rate,
    reactants,
    products,
    block_class,
    send_slot,
):
    group, rows, columns = concentrations.shape
    species, reactions = reactants.shape
    peers = species // group
    regions = lax.axis_size("region")
    up = [(i, (i + 1) % regions) for i in range(regions - 1)]
    down = [(j, i) for i, j in up]
    hbm = pl.BlockSpec(memory_space=pltpu.HBM)
    smem = pl.BlockSpec(memory_space=pltpu.SMEM)
    places = rows // (2 * EDGE)
    lines = EDGE * group

    def buffers(slab_rows):
        row_buffer = pltpu.VMEM((slab_rows, group, columns), f32)
        return [pltpu.VMEM((10, slab_rows, LANES), f32), row_buffer, row_buffer]

    def in_hbm(*arrays):
        return [pltpu.with_memory_space_constraint(v, pltpu.HBM) for v in arrays]

    fields = in_hbm(concentrations, courant_x, courant_y)
    slab_rows = rows // 2 + 2 * EDGE
    middle = pl.pallas_call(
        middle_kernel,
        grid=(1,),
        out_shape=pltpu.HBM((peers, lines + EDGE, LANES), f32),
        in_specs=[smem, smem, smem, hbm, hbm, hbm],
        out_specs=pl.BlockSpec((peers, lines + EDGE, LANES), lambda i: (0, 0, 0)),
        scratch_shapes=[
            pltpu.VMEM((2, group, slab_rows, LANES), f32),
            pltpu.VMEM((slab_rows, columns), f32),
            pltpu.VMEM((slab_rows, columns), f32),
            *buffers(slab_rows),
            pltpu.SemaphoreType.DMA((4,)),
        ],
        compiler_params=pltpu.CompilerParams(vmem_limit_bytes=16 << 20),
        name="middle",
    )(diffusion, block_class, send_slot, *fields)

    winds = jnp.stack([courant_x, courant_y])
    last = jnp.concatenate([concentrations[:, rows - EDGE :], winds[:, rows - EDGE :]], axis=0)
    leading = jnp.concatenate([concentrations[:, :EDGE], winds[:, :EDGE]], axis=0)
    before = lax.ppermute(last, "region", up)
    after = lax.ppermute(leading, "region", down)
    before, after, _ = lax.optimization_barrier((before, after, middle))
    place = jnp.stack([lax.axis_index("region"), jnp.int32(regions)]).astype(jnp.int32)
    slab_rows = rows // 4 + 2 * EDGE
    edges = pl.pallas_call(
        edge_kernel,
        grid=(1,),
        out_shape=pltpu.HBM((peers, lines, LANES), f32),
        in_specs=[smem, smem, hbm, hbm, hbm, hbm, hbm],
        out_specs=pl.BlockSpec((peers, lines, LANES), lambda i: (0, 0, 0)),
        scratch_shapes=[
            pltpu.VMEM((2, 2, group, slab_rows, LANES), f32),
            pltpu.VMEM((2, slab_rows, columns), f32),
            pltpu.VMEM((2, slab_rows, columns), f32),
            *buffers(slab_rows),
            pltpu.SemaphoreType.DMA((16,)),
        ],
        compiler_params=pltpu.CompilerParams(vmem_limit_bytes=16 << 20),
        name="edges",
    )(diffusion, place, *fields, before, after)

    reac = reactants.T.astype(bf16)
    both = jnp.concatenate([products.T, reactants], axis=0).astype(bf16)
    log_table = jnp.broadcast_to(log_rate[:, :, None], log_rate.shape + (LANES,))
    mine = lax.axis_index("species").astype(jnp.int32)
    lower, parity = mine // 2, mine % 2
    done = []
    exchange = functools.partial(
        lax.all_to_all, axis_name="species", split_axis=0, concat_axis=0, tiled=True
    )
    info = None
    for slab, source in (
        (middle, lower + peers // 4),
        (edges, lower + jnp.where(lower < peers // 4, 0, peers // 2)),
    ):
        gathered = exchange(slab)
        if info is None:
            info = gathered[:, lines, : 2 * EDGE].astype(jnp.int32).reshape(-1)
        start = (source * 2 * EDGE + parity).reshape(1)
        if done:
            start, _ = lax.optimization_barrier((start, reacted))
        reacted = chemistry(gathered, info, start, log_table, reac, both)
        done.append(exchange(reacted.reshape(peers, group, EDGE, LANES)))
    tiles = [v.reshape(places, 2, group, EDGE, LANES) for v in done]
    whole = jnp.concatenate([tiles[1][: places // 2], tiles[0], tiles[1][places // 2 :]], axis=0)
    return whole.transpose(2, 0, 3, 1, 4).reshape(group, rows, columns)


def solution(mesh):
    in_specs = (
        P("species", "region", None),
        P("species"),
        P("region", None),
        P("region", None),
        P(),
        P(),
        P(),
        P(("region", "species")),
        P(("region", "species")),
    )
    out_specs = P("species", "region", None)
    return jax.shard_map(
        per_device, mesh=mesh, in_specs=in_specs, out_specs=out_specs, check_vma=False
    )
```

```python
import functools

import jax
import jax.numpy as jnp
from jax import lax
from jax.experimental import pallas as pl
from jax.experimental.pallas import tpu as pltpu
from jax.sharding import PartitionSpec as P

STEPS = 3
ITERS = 2
SUB = 2
FLOOR = 0.05
EDGE = 8
LANES = 128
TILE = 4
bf16 = jnp.bfloat16
f32 = jnp.float32


def median0(p, r):
    return jnp.maximum(jnp.minimum(p, r), jnp.minimum(jnp.maximum(p, r), 0.0))


def shift_left(pair, lane):
    a, b = (pltpu.roll(v, LANES - 1, 1) for v in pair)
    last = lane == LANES - 1
    return jnp.where(last, b, a), jnp.where(last, 0.0, b)


def shift_right(pair, first, lane):
    a, b = (pltpu.roll(v, 1, 1) for v in pair)
    head = lane == 0
    return jnp.where(head, first, a), jnp.where(head, a, b)


def halves(v):
    return v[:, :LANES], v[:, LANES:]


def face_coefs(a):
    size = jnp.abs(a)
    return 0.5 * size * (1.0 - size)


def store_coefs(cx, cy, coef):
    ax = 0.5 * (cx + jnp.concatenate([cx[1:], cx[:1]], axis=0))
    edge = lax.broadcasted_iota(jnp.int32, cy.shape, 1) == 2 * LANES - 1
    ay = 0.5 * (cy + jnp.where(edge, 0.0, jnp.concatenate([cy[:, 1:], cy[:, :1]], axis=1)))
    al = 0.5 * cy[:, :LANES]
    al_weight = jnp.where(al < 0.0, face_coefs(al), 0.0)
    pairs = [halves(v) for v in (ax, face_coefs(ax), ay, face_coefs(ay))]
    pairs.append((jnp.minimum(al, 0.0), al_weight))
    for k, pair in enumerate(pairs):
        coef[2 * k] = pair[0]
        coef[2 * k + 1] = pair[1]


def one_flux(q, qn, d, m, mn, a, e, nu):
    up = a >= 0.0
    return a * jnp.where(up, q, qn) + e * jnp.where(up, m, mn) - nu * d


def sweep(load, store, coef, nu, lo, hi, unroll, keep=None):
    group = nu.shape[0]
    lane = lax.broadcasted_iota(jnp.int32, (group, LANES), 1)

    def spread(which, row):
        return tuple(coef[2 * which + k, pl.ds(row, group, stride=0), :] for k in (0, 1))

    def x_flux(row, q, qn, d, m, mn):
        a, e = spread(0, row), spread(1, row)
        return tuple(one_flux(q[i], qn[i], d[i], m[i], mn[i], a[i], e[i], nu) for i in (0, 1))

    def diff(q, qn):
        return tuple(y - x for x, y in zip(q, qn))

    def limited(p, r):
        return tuple(median0(x, y) for x, y in zip(p, r))

    qa, qb, qc, qd = (load(lo + k) for k in (-2, -1, 0, 1))
    da, db, dc = diff(qa, qb), diff(qb, qc), diff(qc, qd)
    mb, mc = limited(da, db), limited(db, dc)
    behind = x_flux(lo - 1, qb, qc, db, mb, mc)

    def row_step(row, carry):
        q, qn, d, m, behind = carry
        qnn = load(row + 2)
        dn = diff(qn, qnn)
        mn = limited(d, dn)
        fx = x_flux(row, q, qn, d, m, mn)
        right = shift_left(q, lane)
        g = diff(q, right)
        s = limited(shift_right(g, q[0], lane), g)
        sn = shift_left(s, lane)
        a, e = spread(2, row), spread(3, row)
        fy = tuple(one_flux(q[i], right[i], g[i], s[i], sn[i], a[i], e[i], nu) for i in (0, 1))
        la, le = spread(4, row)
        fl = shift_right(fy, (la - nu) * q[0] + le * s[0], lane)
        new = tuple(q[i] - (fx[i] - behind[i]) - (fy[i] - fl[i]) for i in (0, 1))
        if keep is not None:
            scale = keep(row)
            new = tuple(v * scale for v in new)
        store(row, new)
        return qn, qnn, dn, mn, fx

    def steps(i, carry):
        for k in range(unroll):
            carry = row_step(lo + i * unroll + k, carry)
        return carry

    count = hi - lo
    carry = lax.fori_loop(0, count // unroll, steps, (qc, qd, dc, mc, behind))
    for row in range(lo + count // unroll * unroll, hi):
        carry = row_step(row, carry)


def buffer_access(buf):
    def load(row):
        return buf[row, :, :LANES], buf[row, :, LANES:]

    def store(row, pair):
        buf[row, :, :LANES] = pair[0]
        buf[row, :, LANES:] = pair[1]

    return load, store


def start_all(copies):
    for copy in copies:
        copy.start()


def wait_all(copies):
    for copy in copies:
        copy.wait()


def spread_species(diffuse, group):
    lane = lax.broadcasted_iota(jnp.int32, (group, LANES), 0)
    nu = jnp.zeros((group, LANES), f32)
    for k in range(group):
        nu = jnp.where(lane == k, diffuse[k], nu)
    return nu


def raw_access(block):
    group, rows, _ = block.shape[1:]
    flat = [block.at[k].reshape(group * rows, LANES) for k in (0, 1)]

    def load(row):
        return tuple(part[pl.ds(row, group, stride=rows), :] for part in flat)

    return load


def three_sweeps(load, store, coef, nu, one, two, rows, unrolls, keep=None):
    load1, store1 = buffer_access(one)
    load2, store2 = buffer_access(two)
    sweep(load, store1, coef, nu, 4, rows - 4, unrolls[0], keep)
    sweep(load1, store2, coef, nu, 6, rows - 6, unrolls[1], keep)
    sweep(load2, store, coef, nu, 8, rows - 8, unrolls[2])


def store_grouped(out, base, group):
    def store(row, pair):
        at = row - EDGE
        place = 2 * (base + lax.shift_right_logical(at, 3))
        line = pl.multiple_of(lax.bitwise_and(at, EDGE - 1) * group, group)
        out[place, pl.ds(line, group), :] = pair[0]
        out[place + 1, pl.ds(line, group), :] = pair[1]

    return store


def middle_kernel(
    diffuse_in,
    classes_in,
    slots_in,
    conc,
    cx,
    cy,
    out,
    last,
    leading,
    diffuse,
    classes,
    slots,
    raw,
    wx,
    wy,
    coef,
    one,
    two,
    sems,
):
    group, rows = raw.shape[1:3]
    total = conc.shape[1]
    first = total // 4 - EDGE
    pairs = [(cx.at[pl.ds(first, rows)], wx), (cy.at[pl.ds(first, rows)], wy)]
    pairs += [
        (conc.at[:, pl.ds(first, rows), pl.ds(k * LANES, LANES)], raw.at[k]) for k in (0, 1)
    ]
    pairs += [(diffuse_in, diffuse), (classes_in, classes), (slots_in, slots)]
    for rim, at in ((last, total - EDGE), (leading, 0)):
        pairs.append((conc.at[:, pl.ds(at, EDGE)], rim.at[pl.ds(0, group)]))
        pairs.append((cx.at[pl.ds(at, EDGE)], rim.at[group]))
        pairs.append((cy.at[pl.ds(at, EDGE)], rim.at[group + 1]))
    copies = [pltpu.make_async_copy(*pair, sems.at[k]) for k, pair in enumerate(pairs)]
    start_all(copies)
    wait_all(copies[4:7])
    nu = spread_species(diffuse, group)
    lane = lax.broadcasted_iota(jnp.int32, (EDGE, LANES), 1)
    codes = jnp.zeros((EDGE, LANES), f32)
    for k in range(classes.shape[0]):
        code = classes[k] + jnp.where(slots[k] >= 0, 4, 0)
        codes = jnp.where(lane == k, code.astype(f32), codes)
    for k in range(out.shape[0]):
        out[k, EDGE * group :, :] = codes
    wait_all(copies[:2])
    store_coefs(wx[...], wy[...], coef)
    wait_all(copies[2:4])
    three_sweeps(
        raw_access(raw), store_grouped(out, 0, group), coef, nu, one, two, rows, (18, 17, 16)
    )
    wait_all(copies[7:])


def edge_kernel(
    place, diffuse_in, conc, cx, cy, before, after, out, diffuse, raw, wx, wy, coef, one, two, sems
):
    group, rows = raw.shape[2:4]
    total = conc.shape[1]
    own = rows - EDGE
    copies = []

    def copy(src, dst):
        copies.append(pltpu.make_async_copy(src, dst, sems.at[len(copies)]))

    copy(diffuse_in, diffuse)
    for slab, halo, own_first, own_at, halo_at in (
        (0, before, 0, EDGE, 0),
        (1, after, total - own, 0, own),
    ):
        for k, (wind, dst) in enumerate(((cx, wx), (cy, wy))):
            copy(wind.at[pl.ds(own_first, own)], dst.at[slab, pl.ds(own_at, own)])
            copy(halo.at[group + k], dst.at[slab, pl.ds(halo_at, EDGE)])
        for k in (0, 1):
            lanes = pl.ds(k * LANES, LANES)
            dst = raw.at[slab, k]
            copy(conc.at[:, pl.ds(own_first, own), lanes], dst.at[:, pl.ds(own_at, own)])
            copy(halo.at[pl.ds(0, group), :, lanes], dst.at[:, pl.ds(halo_at, EDGE)])
    start_all(copies)
    wait_all(copies)
    nu = spread_species(diffuse, group)

    @pl.loop(0, 2)
    def _(slab):
        store_coefs(wx[slab], wy[slab], coef)
        open_top = jnp.logical_and(slab == 0, place[0] == 0)
        open_end = jnp.logical_and(slab == 1, place[0] == place[1] - 1)

        def keep(row):
            outside = jnp.logical_or(
                jnp.logical_and(open_top, row < EDGE), jnp.logical_and(open_end, row >= own)
            )
            return jnp.where(outside, 0.0, 1.0)

        three_sweeps(
            raw_access(raw.at[slab]),
            store_grouped(out, slab * 4, group),
            coef,
            nu,
            one,
            two,
            rows,
            (10, 12, 16),
            keep,
        )


def split(x):
    high = x.astype(bf16)
    return high, (x - high.astype(f32)).astype(bf16)


def table_dot(table, x):
    high, low = split(x)
    return jnp.dot(table, high, preferred_element_type=f32) + jnp.dot(
        table, low, preferred_element_type=f32
    )


def euler(state, logs, step, reac, both):
    species = state.shape[0]
    g = state
    for _ in range(ITERS):
        rates = jnp.exp(logs + table_dot(reac, jnp.log(g)))
        made_lost = table_dot(both, rates)
        g = (state + step * made_lost[:species]) / (1.0 + step * made_lost[species:] / g)
    return g


def first_line(block, group):
    return block * group if isinstance(block, int) else pl.multiple_of(block * group, group)


def table_kernel(log_rate, reactants, products, log_table, reac, both):
    species, reactions = reactants.shape
    reactant = reactants[...].astype(f32)
    reac[...] = reactant.T.astype(bf16)
    both[:species] = products[...].astype(f32).T.astype(bf16)
    both[species:] = reactant.astype(bf16)
    for k in range(log_rate.shape[0]):
        log_table[k] = jnp.broadcast_to(log_rate[k : k + 1, :], (LANES, reactions)).T


def tables_of(log_rate, reactants, products):
    species, reactions = reactants.shape
    vmem = pl.BlockSpec(memory_space=pltpu.VMEM)
    return pl.pallas_call(
        table_kernel,
        out_shape=[
            jax.ShapeDtypeStruct((log_rate.shape[0], reactions, LANES), f32),
            jax.ShapeDtypeStruct((reactions, species), bf16),
            jax.ShapeDtypeStruct((2 * species, reactions), bf16),
        ],
        in_specs=[vmem] * 3,
        out_specs=[vmem] * 3,
        compiler_params=pltpu.CompilerParams(vmem_limit_bytes=20 << 20),
        name="tables",
    )(log_rate, reactants, products)


def chemistry_kernel(info, start, x, log_table, reac, both, out, result, answer, listed, sem):
    peers, blocks = x.shape[0], EDGE
    species = reac.shape[1]
    group = species // peers
    codes = [info[start[0] + 2 * b] for b in range(blocks)]
    count = jnp.int32(0)
    for b in range(blocks):
        listed[1, b] = lax.bitwise_and(codes[b], 3)
        listed[2, b] = lax.shift_right_logical(codes[b], 2)
        listed[0, count] = b
        count = count + lax.shift_right_logical(codes[b], 2)

    def tile(chosen, first):
        states, logs, lengths = [], [], []
        for b in chosen:
            if first:
                states.append(jnp.maximum(x[:, pl.ds(first_line(b, group), group), :].reshape(species, LANES), FLOOR))
                length = jnp.where(listed[2, b] > 0, 1.0 / SUB, 1.0)
            else:
                states.append(result[b])
                length = 1.0 / SUB
            lengths.append(jnp.full((1, LANES), length, f32))
            logs.append(log_table[listed[1, b]])
        g = euler(
            jnp.concatenate(states, axis=1),
            jnp.concatenate(logs, axis=1),
            jnp.concatenate(lengths, axis=1),
            reac[...],
            both[...],
        )
        for i, b in enumerate(chosen):
            piece = g[:, i * LANES : (i + 1) * LANES]
            result[b] = piece
            for k in range(0, species, 8):
                answer[pl.ds(k * blocks + b, 8, stride=blocks), :] = piece[k : k + 8]

    @pl.loop(0, blocks // TILE)
    def _(i):
        tile([i * TILE + j for j in range(TILE)], True)

    for _ in range(SUB - 1):

        @pl.loop(0, (count + TILE - 1) // TILE)
        def _(i):
            tile([listed[0, jnp.minimum(i * TILE + j, count - 1)] for j in range(TILE)], False)


    copy = pltpu.make_async_copy(answer, out, sem)
    copy.start()
    copy.wait()


def chemistry(x, info, start, log_table, reac, both):
    species, blocks = reac.shape[1], EDGE
    vmem = pl.BlockSpec(memory_space=pltpu.VMEM)
    smem = pl.BlockSpec(memory_space=pltpu.SMEM)
    return pl.pallas_call(
        chemistry_kernel,
        out_shape=pltpu.HBM((species * blocks, LANES), f32),
        in_specs=[smem, smem, vmem, vmem, vmem, vmem],
        out_specs=pl.BlockSpec(memory_space=pltpu.HBM),
        scratch_shapes=[
            pltpu.VMEM((blocks, species, LANES), f32),
            pltpu.VMEM((species * blocks, LANES), f32),
            pltpu.SMEM((3, blocks), jnp.int32),
            pltpu.SemaphoreType.DMA,
        ],
        compiler_params=pltpu.CompilerParams(vmem_limit_bytes=20 << 20),
        name="chemistry",
    )(info, start, x, log_table, reac, both)


def place_kernel(groups, parts, *rest):
    whole, sems = rest[-2:]
    copies = [
        pltpu.make_async_copy(
            parts.at[2 * k + side],
            whole.at[:, pl.ds(at * EDGE, EDGE), pl.ds(side * LANES, LANES)],
            sems.at[2 * k + side],
        )
        for k, at in enumerate(groups)
        for side in (0, 1)
    ]
    start_all(copies)
    wait_all(copies)


def place_rows(parts, groups, rows, *whole):
    peers, group = parts.shape[:2]
    hbm = pl.BlockSpec(memory_space=pltpu.HBM)
    return pl.pallas_call(
        functools.partial(place_kernel, groups),
        out_shape=pltpu.HBM((group, rows, 2 * LANES), f32),
        in_specs=[pl.BlockSpec(memory_space=pltpu.VMEM)] + [hbm] * len(whole),
        out_specs=hbm,
        scratch_shapes=[pltpu.SemaphoreType.DMA((peers,))],
        input_output_aliases={1: 0} if whole else {},
        name="place",
    )(parts, *whole)


def per_device(
    concentrations,
    diffusion,
    courant_x,
    courant_y,
    log_rate,
    reactants,
    products,
    block_class,
    send_slot,
):
    group, rows, columns = concentrations.shape
    species, reactions = reactants.shape
    peers = species // group
    regions = lax.axis_size("region")
    up = [(i, (i + 1) % regions) for i in range(regions - 1)]
    down = [(j, i) for i, j in up]
    hbm = pl.BlockSpec(memory_space=pltpu.HBM)
    smem = pl.BlockSpec(memory_space=pltpu.SMEM)
    vmem = pl.BlockSpec(memory_space=pltpu.VMEM)
    places = rows // (2 * EDGE)
    lines = EDGE * group

    def buffers(slab_rows):
        row_buffer = pltpu.VMEM((slab_rows, group, columns), f32)
        return [pltpu.VMEM((10, slab_rows, LANES), f32), row_buffer, row_buffer]

    def in_hbm(*arrays):
        return [pltpu.with_memory_space_constraint(v, pltpu.HBM) for v in arrays]

    fields = in_hbm(concentrations, courant_x, courant_y)
    slab_rows = rows // 2 + 2 * EDGE
    rim = pltpu.HBM((group + 2, EDGE, columns), f32)
    middle, last, leading = pl.pallas_call(
        middle_kernel,
        grid=(1,),
        out_shape=(pltpu.HBM((peers, lines + EDGE, LANES), f32), rim, rim),
        in_specs=[hbm] * 6,
        out_specs=(pl.BlockSpec((peers, lines + EDGE, LANES), lambda i: (0, 0, 0)), hbm, hbm),
        scratch_shapes=[
            pltpu.SMEM((group,), f32),
            pltpu.SMEM((2 * EDGE,), jnp.int32),
            pltpu.SMEM((2 * EDGE,), jnp.int32),
            pltpu.VMEM((2, group, slab_rows, LANES), f32),
            pltpu.VMEM((slab_rows, columns), f32),
            pltpu.VMEM((slab_rows, columns), f32),
            *buffers(slab_rows),
            pltpu.SemaphoreType.DMA((13,)),
        ],
        compiler_params=pltpu.CompilerParams(vmem_limit_bytes=16 << 20),
        name="middle",
    )(*in_hbm(diffusion, block_class, send_slot), *fields)

    before = lax.ppermute(last, "region", up)
    after = lax.ppermute(leading, "region", down)
    place = jnp.stack([lax.axis_index("region"), jnp.int32(regions)]).astype(jnp.int32)
    slab_rows = rows // 4 + 2 * EDGE
    edges = pl.pallas_call(
        edge_kernel,
        grid=(1,),
        out_shape=pltpu.HBM((peers, lines, LANES), f32),
        in_specs=[smem] + [hbm] * 4 + [vmem] * 2,
        out_specs=pl.BlockSpec((peers, lines, LANES), lambda i: (0, 0, 0)),
        scratch_shapes=[
            pltpu.SMEM((group,), f32),
            pltpu.VMEM((2, 2, group, slab_rows, LANES), f32),
            pltpu.VMEM((2, slab_rows, columns), f32),
            pltpu.VMEM((2, slab_rows, columns), f32),
            *buffers(slab_rows),
            pltpu.SemaphoreType.DMA((17,)),
        ],
        compiler_params=pltpu.CompilerParams(vmem_limit_bytes=16 << 20),
        name="edges",
    )(place, *in_hbm(diffusion), *fields, before, after)

    tables = tables_of(log_rate, reactants, products)
    mine = lax.axis_index("species").astype(jnp.int32)
    lower, parity = mine // 2, mine % 2
    done = []
    exchange = functools.partial(
        lax.all_to_all, axis_name="species", split_axis=0, concat_axis=0, tiled=True
    )
    info = None
    for slab, source in (
        (middle, lower + peers // 4),
        (edges, lower + jnp.where(lower < peers // 4, 0, peers // 2)),
    ):
        gathered = exchange(slab)
        if info is None:
            info = gathered[:, lines, : 2 * EDGE].astype(jnp.int32).reshape(-1)
        start = (source * 2 * EDGE + parity).reshape(1)
        reacted = chemistry(gathered, info, start, *tables)
        done.append(exchange(reacted.reshape(peers, group, EDGE, LANES)))
    quarter = places // 2
    filled = place_rows(done[0], range(quarter, 3 * quarter), rows)
    sides = (*range(quarter), *range(3 * quarter, 4 * quarter))
    return place_rows(done[1], sides, rows, filled)


def solution(mesh):
    in_specs = (
        P("species", "region", None),
        P("species"),
        P("region", None),
        P("region", None),
        P(),
        P(),
        P(),
        P(("region", "species")),
        P(("region", "species")),
    )
    out_specs = P("species", "region", None)
    return jax.shard_map(
        per_device, mesh=mesh, in_specs=in_specs, out_specs=out_specs, check_vma=False
    )
```

```python
import functools

import jax
import jax.numpy as jnp
from jax import lax
from jax.experimental import pallas as pl
from jax.experimental.pallas import tpu as pltpu
from jax.sharding import PartitionSpec as P

STEPS = 3
ITERS = 2
SUB = 2
FLOOR = 0.05
EDGE = 8
LANES = 128
TILE = 4
bf16 = jnp.bfloat16
f32 = jnp.float32


def median0(p, r):
    return jnp.maximum(jnp.minimum(p, r), jnp.minimum(jnp.maximum(p, r), 0.0))


def shift_left(pair, lane):
    a, b = (pltpu.roll(v, LANES - 1, 1) for v in pair)
    last = lane == LANES - 1
    return jnp.where(last, b, a), jnp.where(last, 0.0, b)


def shift_right(pair, first, lane):
    a, b = (pltpu.roll(v, 1, 1) for v in pair)
    head = lane == 0
    return jnp.where(head, first, a), jnp.where(head, a, b)


def halves(v):
    return v[:, :LANES], v[:, LANES:]


def face_coefs(a):
    size = jnp.abs(a)
    return 0.5 * size * (1.0 - size)


def store_coefs(cx, cy, coef):
    ax = 0.5 * (cx + jnp.concatenate([cx[1:], cx[:1]], axis=0))
    edge = lax.broadcasted_iota(jnp.int32, cy.shape, 1) == 2 * LANES - 1
    ay = 0.5 * (cy + jnp.where(edge, 0.0, jnp.concatenate([cy[:, 1:], cy[:, :1]], axis=1)))
    al = 0.5 * cy[:, :LANES]
    al_weight = jnp.where(al < 0.0, face_coefs(al), 0.0)
    pairs = [halves(v) for v in (ax, face_coefs(ax), ay, face_coefs(ay))]
    pairs.append((jnp.minimum(al, 0.0), al_weight))
    for k, pair in enumerate(pairs):
        coef[2 * k] = pair[0]
        coef[2 * k + 1] = pair[1]


def one_flux(q, qn, d, m, mn, a, e, nu):
    up = a >= 0.0
    return a * jnp.where(up, q, qn) + e * jnp.where(up, m, mn) - nu * d


def sweep(load, store, coef, nu, lo, hi, unroll, keep=None):
    group = nu.shape[0]
    lane = lax.broadcasted_iota(jnp.int32, (group, LANES), 1)

    def spread(which, row):
        return tuple(coef[2 * which + k, pl.ds(row, group, stride=0), :] for k in (0, 1))

    def x_flux(row, q, qn, d, m, mn):
        a, e = spread(0, row), spread(1, row)
        return tuple(one_flux(q[i], qn[i], d[i], m[i], mn[i], a[i], e[i], nu) for i in (0, 1))

    def diff(q, qn):
        return tuple(y - x for x, y in zip(q, qn))

    def limited(p, r):
        return tuple(median0(x, y) for x, y in zip(p, r))

    qa, qb, qc, qd = (load(lo + k) for k in (-2, -1, 0, 1))
    da, db, dc = diff(qa, qb), diff(qb, qc), diff(qc, qd)
    mb, mc = limited(da, db), limited(db, dc)
    behind = x_flux(lo - 1, qb, qc, db, mb, mc)

    def row_step(row, carry):
        q, qn, d, m, behind = carry
        qnn = load(row + 2)
        dn = diff(qn, qnn)
        mn = limited(d, dn)
        fx = x_flux(row, q, qn, d, m, mn)
        right = shift_left(q, lane)
        g = diff(q, right)
        s = limited(shift_right(g, q[0], lane), g)
        sn = shift_left(s, lane)
        a, e = spread(2, row), spread(3, row)
        fy = tuple(one_flux(q[i], right[i], g[i], s[i], sn[i], a[i], e[i], nu) for i in (0, 1))
        la, le = spread(4, row)
        fl = shift_right(fy, (la - nu) * q[0] + le * s[0], lane)
        new = tuple(q[i] - (fx[i] - behind[i]) - (fy[i] - fl[i]) for i in (0, 1))
        if keep is not None:
            scale = keep(row)
            new = tuple(v * scale for v in new)
        store(row, new)
        return qn, qnn, dn, mn, fx

    def steps(i, carry):
        for k in range(unroll):
            carry = row_step(lo + i * unroll + k, carry)
        return carry

    count = hi - lo
    carry = lax.fori_loop(0, count // unroll, steps, (qc, qd, dc, mc, behind))
    for row in range(lo + count // unroll * unroll, hi):
        carry = row_step(row, carry)


def buffer_access(buf):
    def load(row):
        return buf[row, :, :LANES], buf[row, :, LANES:]

    def store(row, pair):
        buf[row, :, :LANES] = pair[0]
        buf[row, :, LANES:] = pair[1]

    return load, store


def start_all(copies):
    for copy in copies:
        copy.start()


def wait_all(copies):
    for copy in copies:
        copy.wait()


def spread_species(diffuse, group):
    lane = lax.broadcasted_iota(jnp.int32, (group, LANES), 0)
    nu = jnp.zeros((group, LANES), f32)
    for k in range(group):
        nu = jnp.where(lane == k, diffuse[k], nu)
    return nu


def raw_access(block):
    group, rows, _ = block.shape[1:]
    flat = [block.at[k].reshape(group * rows, LANES) for k in (0, 1)]

    def load(row):
        return tuple(part[pl.ds(row, group, stride=rows), :] for part in flat)

    return load


def three_sweeps(load, store, coef, nu, one, two, rows, unrolls, keep=None):
    load1, store1 = buffer_access(one)
    load2, store2 = buffer_access(two)
    sweep(load, store1, coef, nu, 4, rows - 4, unrolls[0], keep)
    sweep(load1, store2, coef, nu, 6, rows - 6, unrolls[1], keep)
    sweep(load2, store, coef, nu, 8, rows - 8, unrolls[2])


def store_grouped(out, base, group):
    def store(row, pair):
        at = row - EDGE
        line = pl.multiple_of((base + lax.shift_right_logical(at, 3)) * group, group)
        peer = 2 * lax.bitwise_and(at, EDGE - 1)
        out[peer, pl.ds(line, group), :] = pair[0]
        out[peer + 1, pl.ds(line, group), :] = pair[1]

    return store


def middle_kernel(
    diffuse_in,
    classes_in,
    slots_in,
    conc,
    cx,
    cy,
    out,
    last,
    leading,
    diffuse,
    classes,
    slots,
    raw,
    wx,
    wy,
    coef,
    one,
    two,
    sems,
):
    group, rows = raw.shape[1:3]
    total = conc.shape[1]
    first = total // 4 - EDGE
    pairs = [(cx.at[pl.ds(first, rows)], wx), (cy.at[pl.ds(first, rows)], wy)]
    pairs += [
        (conc.at[:, pl.ds(first, rows), pl.ds(k * LANES, LANES)], raw.at[k]) for k in (0, 1)
    ]
    pairs += [(diffuse_in, diffuse), (classes_in, classes), (slots_in, slots)]
    for rim, at in ((last, total - EDGE), (leading, 0)):
        pairs.append((conc.at[:, pl.ds(at, EDGE)], rim.at[pl.ds(0, group)]))
        pairs.append((cx.at[pl.ds(at, EDGE)], rim.at[group]))
        pairs.append((cy.at[pl.ds(at, EDGE)], rim.at[group + 1]))
    copies = [pltpu.make_async_copy(*pair, sems.at[k]) for k, pair in enumerate(pairs)]
    start_all(copies)
    wait_all(copies[4:7])
    nu = spread_species(diffuse, group)
    lane = lax.broadcasted_iota(jnp.int32, (EDGE, LANES), 1)
    codes = jnp.zeros((EDGE, LANES), f32)
    for k in range(classes.shape[0]):
        code = classes[k] + jnp.where(slots[k] >= 0, 4, 0)
        codes = jnp.where(lane == k, code.astype(f32), codes)
    for k in range(out.shape[0]):
        out[k, EDGE * group :, :] = codes
    wait_all(copies[:2])
    store_coefs(wx[...], wy[...], coef)
    wait_all(copies[2:4])
    three_sweeps(
        raw_access(raw), store_grouped(out, 0, group), coef, nu, one, two, rows, (18, 17, 16)
    )
    wait_all(copies[7:])


def edge_kernel(
    place,
    diffuse_in,
    conc,
    cx,
    cy,
    before,
    after,
    _log_table,
    _reac,
    _both,
    out,
    diffuse,
    raw,
    wx,
    wy,
    coef,
    one,
    two,
    sems,
):
    group, rows = raw.shape[2:4]
    total = conc.shape[1]
    own = rows - EDGE
    copies = []

    def copy(src, dst):
        copies.append(pltpu.make_async_copy(src, dst, sems.at[len(copies)]))

    copy(diffuse_in, diffuse)
    for slab, halo, own_first, own_at, halo_at in (
        (0, before, 0, EDGE, 0),
        (1, after, total - own, 0, own),
    ):
        for k, (wind, dst) in enumerate(((cx, wx), (cy, wy))):
            copy(wind.at[pl.ds(own_first, own)], dst.at[slab, pl.ds(own_at, own)])
            copy(halo.at[group + k], dst.at[slab, pl.ds(halo_at, EDGE)])
        for k in (0, 1):
            lanes = pl.ds(k * LANES, LANES)
            dst = raw.at[slab, k]
            copy(conc.at[:, pl.ds(own_first, own), lanes], dst.at[:, pl.ds(own_at, own)])
            copy(halo.at[pl.ds(0, group), :, lanes], dst.at[:, pl.ds(halo_at, EDGE)])
    start_all(copies)
    wait_all(copies)
    nu = spread_species(diffuse, group)

    @pl.loop(0, 2)
    def _(slab):
        store_coefs(wx[slab], wy[slab], coef)
        open_top = jnp.logical_and(slab == 0, place[0] == 0)
        open_end = jnp.logical_and(slab == 1, place[0] == place[1] - 1)

        def keep(row):
            outside = jnp.logical_or(
                jnp.logical_and(open_top, row < EDGE), jnp.logical_and(open_end, row >= own)
            )
            return jnp.where(outside, 0.0, 1.0)

        three_sweeps(
            raw_access(raw.at[slab]),
            store_grouped(out, slab * 4, group),
            coef,
            nu,
            one,
            two,
            rows,
            (10, 12, 16),
            keep,
        )


def split(x):
    high = x.astype(bf16)
    return high, (x - high.astype(f32)).astype(bf16)


def table_dot(table, x):
    high, low = split(x)
    return jnp.dot(table, high, preferred_element_type=f32) + jnp.dot(
        table, low, preferred_element_type=f32
    )


def euler(state, logs, step, reac, both):
    species = state.shape[0]
    g = state
    for _ in range(ITERS):
        rates = jnp.exp(logs + table_dot(reac, jnp.log(g)))
        made_lost = table_dot(both, rates)
        g = (state + step * made_lost[:species]) / (1.0 + step * made_lost[species:] / g)
    return g


def first_line(block, group):
    return block * group if isinstance(block, int) else pl.multiple_of(block * group, group)


def table_kernel(log_rate, reactants, products, log_table, reac, both):
    species, reactions = reactants.shape
    reactant = reactants[...].astype(f32)
    reac[...] = reactant.T.astype(bf16)
    both[:species] = products[...].astype(f32).T.astype(bf16)
    both[species:] = reactant.astype(bf16)
    for k in range(log_rate.shape[0]):
        log_table[k] = jnp.broadcast_to(log_rate[k : k + 1, :], (LANES, reactions)).T


def tables_of(log_rate, reactants, products):
    species, reactions = reactants.shape
    classes = log_rate.shape[0]
    vmem = pl.BlockSpec(memory_space=pltpu.VMEM)
    return pl.pallas_call(
        table_kernel,
        grid=(1,),
        out_shape=[
            pltpu.VMEM((classes, reactions, LANES), f32),
            pltpu.VMEM((reactions, species), bf16),
            pltpu.VMEM((2 * species, reactions), bf16),
        ],
        in_specs=[
            pl.BlockSpec((classes, reactions), lambda i: (0, 0)),
            pl.BlockSpec((species, reactions), lambda i: (0, 0)),
            pl.BlockSpec((reactions, species), lambda i: (0, 0)),
        ],
        out_specs=[vmem] * 3,
        compiler_params=pltpu.CompilerParams(vmem_limit_bytes=12 << 20),
        name="tables",
    )(log_rate, reactants, products)


def chemistry_kernel(info, start, x, log_table, reac, both, out, result, answer, listed, sem):
    peers, blocks = x.shape[0], EDGE
    species = reac.shape[1]
    group = species // peers
    codes = [info[start[b]] for b in range(blocks)]
    count = jnp.int32(0)
    for b in range(blocks):
        listed[1, b] = lax.bitwise_and(codes[b], 3)
        listed[2, b] = lax.shift_right_logical(codes[b], 2)
        listed[0, count] = b
        count = count + lax.shift_right_logical(codes[b], 2)

    def tile(chosen, first):
        states, logs, lengths = [], [], []
        for b in chosen:
            if first:
                states.append(jnp.maximum(x[:, pl.ds(first_line(b, group), group), :].reshape(species, LANES), FLOOR))
                length = jnp.where(listed[2, b] > 0, 1.0 / SUB, 1.0)
            else:
                states.append(result[b])
                length = 1.0 / SUB
            lengths.append(jnp.full((1, LANES), length, f32))
            logs.append(log_table[listed[1, b]])
        g = euler(
            jnp.concatenate(states, axis=1),
            jnp.concatenate(logs, axis=1),
            jnp.concatenate(lengths, axis=1),
            reac[...],
            both[...],
        )
        for i, b in enumerate(chosen):
            piece = g[:, i * LANES : (i + 1) * LANES]
            result[b] = piece
            for k in range(0, species, 8):
                answer[pl.ds(k * blocks + b, 8, stride=blocks), :] = piece[k : k + 8]

    @pl.loop(0, blocks // TILE)
    def _(i):
        tile([i * TILE + j for j in range(TILE)], True)

    for _ in range(SUB - 1):

        @pl.loop(0, (count + TILE - 1) // TILE)
        def _(i):
            tile([listed[0, jnp.minimum(i * TILE + j, count - 1)] for j in range(TILE)], False)


    copy = pltpu.make_async_copy(answer, out, sem)
    copy.start()
    copy.wait()


def chemistry(x, info, start, log_table, reac, both):
    species, blocks = reac.shape[1], EDGE
    vmem = pl.BlockSpec(memory_space=pltpu.VMEM)
    smem = pl.BlockSpec(memory_space=pltpu.SMEM)
    return pl.pallas_call(
        chemistry_kernel,
        out_shape=pltpu.HBM((species * blocks, LANES), f32),
        in_specs=[smem, smem, vmem, vmem, vmem, vmem],
        out_specs=pl.BlockSpec(memory_space=pltpu.HBM),
        scratch_shapes=[
            pltpu.VMEM((blocks, species, LANES), f32),
            pltpu.VMEM((species * blocks, LANES), f32),
            pltpu.SMEM((3, blocks), jnp.int32),
            pltpu.SemaphoreType.DMA,
        ],
        compiler_params=pltpu.CompilerParams(vmem_limit_bytes=14 << 20),
        name="chemistry",
    )(info, start, x, log_table, reac, both)


def place_kernel(firsts, parts, *rest):
    whole, stage, sems = rest[-3:]
    peers, group, blocks, _ = parts.shape
    count = blocks // len(firsts)
    rows = count * EDGE
    copies = []
    for k, first in enumerate(firsts):
        for side in (0, 1):
            for peer in range(side, peers, 2):
                for s in range(group):
                    at = pl.ds(s * rows + peer // 2, count, stride=EDGE)
                    stage[k, side, at, :] = parts[peer, s, k * count : (k + 1) * count]
            copy = pltpu.make_async_copy(
                stage.at[k, side].reshape(group, rows, LANES),
                whole.at[:, pl.ds(first, rows), pl.ds(side * LANES, LANES)],
                sems.at[2 * k + side],
            )
            copy.start()
            copies.append(copy)
    wait_all(copies)


def place_rows(parts, firsts, rows, *whole):
    peers, group, blocks, _ = parts.shape
    hbm = pl.BlockSpec(memory_space=pltpu.HBM)
    count = len(firsts)
    return pl.pallas_call(
        functools.partial(place_kernel, firsts),
        out_shape=pltpu.HBM((group, rows, 2 * LANES), f32),
        in_specs=[pl.BlockSpec(memory_space=pltpu.VMEM)] + [hbm] * len(whole),
        out_specs=hbm,
        scratch_shapes=[
            pltpu.VMEM((count, 2, group * blocks // count * EDGE, LANES), f32),
            pltpu.SemaphoreType.DMA((2 * count,)),
        ],
        input_output_aliases={1: 0} if whole else {},
        name="place",
    )(pltpu.with_memory_space_constraint(parts, pltpu.VMEM), *whole)


def per_device(
    concentrations,
    diffusion,
    courant_x,
    courant_y,
    log_rate,
    reactants,
    products,
    block_class,
    send_slot,
):
    group, rows, columns = concentrations.shape
    species, reactions = reactants.shape
    peers = species // group
    regions = lax.axis_size("region")
    up = [(i, (i + 1) % regions) for i in range(regions - 1)]
    down = [(j, i) for i, j in up]
    hbm = pl.BlockSpec(memory_space=pltpu.HBM)
    smem = pl.BlockSpec(memory_space=pltpu.SMEM)
    vmem = pl.BlockSpec(memory_space=pltpu.VMEM)
    places = rows // (2 * EDGE)
    lines = EDGE * group

    def buffers(slab_rows):
        row_buffer = pltpu.VMEM((slab_rows, group, columns), f32)
        return [pltpu.VMEM((10, slab_rows, LANES), f32), row_buffer, row_buffer]

    def in_hbm(*arrays):
        return [pltpu.with_memory_space_constraint(v, pltpu.HBM) for v in arrays]

    def in_vmem(*arrays):
        return [pltpu.with_memory_space_constraint(v, pltpu.VMEM) for v in arrays]

    fields = in_hbm(concentrations, courant_x, courant_y)
    slab_rows = rows // 2 + 2 * EDGE
    rim = pltpu.VMEM((group + 2, EDGE, columns), f32)
    middle, last, leading = pl.pallas_call(
        middle_kernel,
        grid=(1,),
        out_shape=(pltpu.HBM((peers, lines + EDGE, LANES), f32), rim, rim),
        in_specs=[hbm] * 6,
        out_specs=(pl.BlockSpec((peers, lines + EDGE, LANES), lambda i: (0, 0, 0)), vmem, vmem),
        scratch_shapes=[
            pltpu.SMEM((group,), f32),
            pltpu.SMEM((2 * EDGE,), jnp.int32),
            pltpu.SMEM((2 * EDGE,), jnp.int32),
            pltpu.VMEM((2, group, slab_rows, LANES), f32),
            pltpu.VMEM((slab_rows, columns), f32),
            pltpu.VMEM((slab_rows, columns), f32),
            *buffers(slab_rows),
            pltpu.SemaphoreType.DMA((13,)),
        ],
        compiler_params=pltpu.CompilerParams(vmem_limit_bytes=16 << 20),
        name="middle",
    )(*in_hbm(diffusion, block_class, send_slot), *fields)

    before = lax.ppermute(last, "region", up)
    after = lax.ppermute(leading, "region", down)
    tables = tables_of(*in_hbm(log_rate, reactants, products))
    place = jnp.stack([lax.axis_index("region"), jnp.int32(regions)]).astype(jnp.int32)
    slab_rows = rows // 4 + 2 * EDGE
    edges = pl.pallas_call(
        edge_kernel,
        grid=(1,),
        out_shape=pltpu.HBM((peers, lines, LANES), f32),
        in_specs=[smem] + [hbm] * 4 + [vmem] * 5,
        out_specs=pl.BlockSpec((peers, lines, LANES), lambda i: (0, 0, 0)),
        scratch_shapes=[
            pltpu.SMEM((group,), f32),
            pltpu.VMEM((2, 2, group, slab_rows, LANES), f32),
            pltpu.VMEM((2, slab_rows, columns), f32),
            pltpu.VMEM((2, slab_rows, columns), f32),
            *buffers(slab_rows),
            pltpu.SemaphoreType.DMA((17,)),
        ],
        compiler_params=pltpu.CompilerParams(vmem_limit_bytes=16 << 20),
        name="edges",
    )(place, *in_hbm(diffusion), *fields, *in_vmem(before, after), *in_vmem(*tables))

    mine = lax.axis_index("species").astype(jnp.int32)
    exchange = functools.partial(
        lax.all_to_all, axis_name="species", split_axis=0, concat_axis=0, tiled=True
    )
    info = None
    done = []
    order = jnp.arange(EDGE, dtype=jnp.int32)
    half = peers // 2
    for slab, source in (
        (middle, order + half // 2),
        (edges, jnp.where(order < half // 2, order, order + half)),
    ):
        gathered = exchange(slab)
        if info is None:
            info = gathered[:, lines, : 2 * EDGE].astype(jnp.int32).reshape(-1)
        start = source * 2 * EDGE + mine
        reacted = chemistry(*in_vmem(gathered), info, start, *in_vmem(*tables))
        done.append(exchange(reacted.reshape(peers, group, EDGE, LANES)))
    quarter = rows // 4
    filled = place_rows(done[0], (quarter,), rows)
    return place_rows(done[1], (0, 3 * quarter), rows, filled)


def solution(mesh):
    in_specs = (
        P("species", "region", None),
        P("species"),
        P("region", None),
        P("region", None),
        P(),
        P(),
        P(),
        P(("region", "species")),
        P(("region", "species")),
    )
    out_specs = P("species", "region", None)
    return jax.shard_map(
        per_device, mesh=mesh, in_specs=in_specs, out_specs=out_specs, check_vma=False
    )
```

```python
import functools

import jax
import jax.numpy as jnp
from jax import lax
from jax.experimental import pallas as pl
from jax.experimental.pallas import tpu as pltpu
from jax.sharding import PartitionSpec as P

STEPS = 3
ITERS = 2
SUB = 2
FLOOR = 0.05
EDGE = 8
LANES = 128
TILE = 4
bf16 = jnp.bfloat16
f32 = jnp.float32


def median0(p, r):
    return jnp.maximum(jnp.minimum(p, r), jnp.minimum(jnp.maximum(p, r), 0.0))


def shift_left(pair, lane):
    a, b = (pltpu.roll(v, LANES - 1, 1) for v in pair)
    last = lane == LANES - 1
    return jnp.where(last, b, a), jnp.where(last, 0.0, b)


def shift_right(pair, first, lane):
    a, b = (pltpu.roll(v, 1, 1) for v in pair)
    head = lane == 0
    return jnp.where(head, first, a), jnp.where(head, a, b)


def halves(v):
    return v[:, :LANES], v[:, LANES:]


def face_coefs(a):
    size = jnp.abs(a)
    return 0.5 * size * (1.0 - size)


def store_coefs(cx, cy, coef):
    ax = 0.5 * (cx + jnp.concatenate([cx[1:], cx[:1]], axis=0))
    edge = lax.broadcasted_iota(jnp.int32, cy.shape, 1) == 2 * LANES - 1
    ay = 0.5 * (cy + jnp.where(edge, 0.0, jnp.concatenate([cy[:, 1:], cy[:, :1]], axis=1)))
    al = 0.5 * cy[:, :LANES]
    al_weight = jnp.where(al < 0.0, face_coefs(al), 0.0)
    pairs = [halves(v) for v in (ax, face_coefs(ax), ay, face_coefs(ay))]
    pairs.append((jnp.minimum(al, 0.0), al_weight))
    for k, pair in enumerate(pairs):
        coef[2 * k] = pair[0]
        coef[2 * k + 1] = pair[1]


def one_flux(q, qn, d, m, mn, a, e, nu):
    up = a >= 0.0
    return a * jnp.where(up, q, qn) + e * jnp.where(up, m, mn) - nu * d


def sweep(load, store, coef, nu, lo, hi, unroll, keep=None):
    group = nu.shape[0]
    lane = lax.broadcasted_iota(jnp.int32, (group, LANES), 1)

    def spread(which, row):
        return tuple(coef[2 * which + k, pl.ds(row, group, stride=0), :] for k in (0, 1))

    def x_flux(row, q, qn, d, m, mn):
        a, e = spread(0, row), spread(1, row)
        return tuple(one_flux(q[i], qn[i], d[i], m[i], mn[i], a[i], e[i], nu) for i in (0, 1))

    def diff(q, qn):
        return tuple(y - x for x, y in zip(q, qn))

    def limited(p, r):
        return tuple(median0(x, y) for x, y in zip(p, r))

    qa, qb, qc, qd = (load(lo + k) for k in (-2, -1, 0, 1))
    da, db, dc = diff(qa, qb), diff(qb, qc), diff(qc, qd)
    mb, mc = limited(da, db), limited(db, dc)
    behind = x_flux(lo - 1, qb, qc, db, mb, mc)

    def row_step(row, carry):
        q, qn, d, m, behind = carry
        qnn = load(row + 2)
        dn = diff(qn, qnn)
        mn = limited(d, dn)
        fx = x_flux(row, q, qn, d, m, mn)
        right = shift_left(q, lane)
        g = diff(q, right)
        s = limited(shift_right(g, q[0], lane), g)
        sn = shift_left(s, lane)
        a, e = spread(2, row), spread(3, row)
        fy = tuple(one_flux(q[i], right[i], g[i], s[i], sn[i], a[i], e[i], nu) for i in (0, 1))
        la, le = spread(4, row)
        fl = shift_right(fy, (la - nu) * q[0] + le * s[0], lane)
        new = tuple(q[i] - (fx[i] - behind[i]) - (fy[i] - fl[i]) for i in (0, 1))
        if keep is not None:
            scale = keep(row)
            new = tuple(v * scale for v in new)
        store(row, new)
        return qn, qnn, dn, mn, fx

    def steps(i, carry):
        for k in range(unroll):
            carry = row_step(lo + i * unroll + k, carry)
        return carry

    count = hi - lo
    carry = lax.fori_loop(0, count // unroll, steps, (qc, qd, dc, mc, behind))
    for row in range(lo + count // unroll * unroll, hi):
        carry = row_step(row, carry)


def buffer_access(buf):
    def load(row):
        return buf[row, :, :LANES], buf[row, :, LANES:]

    def store(row, pair):
        buf[row, :, :LANES] = pair[0]
        buf[row, :, LANES:] = pair[1]

    return load, store


def start_all(copies):
    for copy in copies:
        copy.start()


def wait_all(copies):
    for copy in copies:
        copy.wait()


def spread_species(diffuse, group):
    lane = lax.broadcasted_iota(jnp.int32, (group, LANES), 0)
    nu = jnp.zeros((group, LANES), f32)
    for k in range(group):
        nu = jnp.where(lane == k, diffuse[k], nu)
    return nu


def raw_access(block):
    group, rows, _ = block.shape[1:]
    flat = [block.at[k].reshape(group * rows, LANES) for k in (0, 1)]

    def load(row):
        return tuple(part[pl.ds(row, group, stride=rows), :] for part in flat)

    return load


def three_sweeps(load, store, coef, nu, one, two, rows, unrolls, keep=None):
    load1, store1 = buffer_access(one)
    load2, store2 = buffer_access(two)
    sweep(load, store1, coef, nu, 4, rows - 4, unrolls[0], keep)
    sweep(load1, store2, coef, nu, 6, rows - 6, unrolls[1], keep)
    sweep(load2, store, coef, nu, 8, rows - 8, unrolls[2])


def store_grouped(out, base, group):
    def store(row, pair):
        at = row - EDGE
        line = pl.multiple_of((base + lax.shift_right_logical(at, 3)) * group, group)
        peer = 2 * lax.bitwise_and(at, EDGE - 1)
        out[peer, pl.ds(line, group), :] = pair[0]
        out[peer + 1, pl.ds(line, group), :] = pair[1]

    return store


def rim_kernel(conc, cx, cy, last, leading, sems):
    group, total, _ = conc.shape
    copies = []

    def copy(src, dst):
        copies.append(pltpu.make_async_copy(src, dst, sems.at[len(copies)]))

    for rim, at in ((last, total - EDGE), (leading, 0)):
        copy(conc.at[:, pl.ds(at, EDGE)], rim.at[pl.ds(0, group)])
        copy(cx.at[pl.ds(at, EDGE)], rim.at[group])
        copy(cy.at[pl.ds(at, EDGE)], rim.at[group + 1])
    start_all(copies)
    wait_all(copies)


def middle_kernel(
    diffuse_in,
    classes_in,
    slots_in,
    conc,
    cx,
    cy,
    out,
    token,
    diffuse,
    classes,
    slots,
    raw,
    wx,
    wy,
    coef,
    one,
    two,
    sems,
):
    group, rows = raw.shape[1:3]
    total = conc.shape[1]
    first = total // 4 - EDGE
    pairs = [(cx.at[pl.ds(first, rows)], wx), (cy.at[pl.ds(first, rows)], wy)]
    pairs += [
        (conc.at[:, pl.ds(first, rows), pl.ds(k * LANES, LANES)], raw.at[k]) for k in (0, 1)
    ]
    pairs += [(diffuse_in, diffuse), (classes_in, classes), (slots_in, slots)]
    copies = [pltpu.make_async_copy(*pair, sems.at[k]) for k, pair in enumerate(pairs)]
    start_all(copies)
    wait_all(copies[4:7])
    nu = spread_species(diffuse, group)
    lane = lax.broadcasted_iota(jnp.int32, (EDGE, LANES), 1)
    codes = jnp.zeros((EDGE, LANES), f32)
    for k in range(classes.shape[0]):
        code = classes[k] + jnp.where(slots[k] >= 0, 4, 0)
        codes = jnp.where(lane == k, code.astype(f32), codes)
    for k in range(out.shape[0]):
        out[k, EDGE * group :, :] = codes
    wait_all(copies[:2])
    store_coefs(wx[...], wy[...], coef)
    wait_all(copies[2:4])
    three_sweeps(
        raw_access(raw), store_grouped(out, 0, group), coef, nu, one, two, rows, (18, 17, 16)
    )
    token[...] = codes


def edge_kernel(
    place,
    diffuse_in,
    conc,
    cx,
    cy,
    before,
    after,
    _token,
    log_rate,
    reactants,
    products,
    out,
    log_table,
    reac,
    both,
    diffuse,
    raw,
    wx,
    wy,
    coef,
    one,
    two,
    sems,
):
    group, rows = raw.shape[2:4]
    total = conc.shape[1]
    own = rows - EDGE
    copies = []

    def copy(src, dst):
        copies.append(pltpu.make_async_copy(src, dst, sems.at[len(copies)]))

    copy(diffuse_in, diffuse)
    for slab, halo, own_first, own_at, halo_at in (
        (0, before, 0, EDGE, 0),
        (1, after, total - own, 0, own),
    ):
        for k, (wind, dst) in enumerate(((cx, wx), (cy, wy))):
            copy(wind.at[pl.ds(own_first, own)], dst.at[slab, pl.ds(own_at, own)])
            copy(halo.at[group + k], dst.at[slab, pl.ds(halo_at, EDGE)])
        for k in (0, 1):
            lanes = pl.ds(k * LANES, LANES)
            dst = raw.at[slab, k]
            copy(conc.at[:, pl.ds(own_first, own), lanes], dst.at[:, pl.ds(own_at, own)])
            copy(halo.at[pl.ds(0, group), :, lanes], dst.at[:, pl.ds(halo_at, EDGE)])
    start_all(copies)
    table_kernel(log_rate, reactants, products, log_table, reac, both)
    wait_all(copies)
    nu = spread_species(diffuse, group)

    @pl.loop(0, 2)
    def _(slab):
        store_coefs(wx[slab], wy[slab], coef)
        open_top = jnp.logical_and(slab == 0, place[0] == 0)
        open_end = jnp.logical_and(slab == 1, place[0] == place[1] - 1)

        def keep(row):
            outside = jnp.logical_or(
                jnp.logical_and(open_top, row < EDGE), jnp.logical_and(open_end, row >= own)
            )
            return jnp.where(outside, 0.0, 1.0)

        three_sweeps(
            raw_access(raw.at[slab]),
            store_grouped(out, slab * 4, group),
            coef,
            nu,
            one,
            two,
            rows,
            (10, 12, 16),
            keep,
        )


def split(x):
    high = x.astype(bf16)
    return high, (x - high.astype(f32)).astype(bf16)


def table_dot(table, x):
    high, low = split(x)
    return jnp.dot(table, high, preferred_element_type=f32) + jnp.dot(
        table, low, preferred_element_type=f32
    )


def euler(state, logs, step, reac, both):
    species = state.shape[0]
    g = state
    for _ in range(ITERS):
        rates = jnp.exp(logs + table_dot(reac, jnp.log(g)))
        made_lost = table_dot(both, rates)
        g = (state + step * made_lost[:species]) / (1.0 + step * made_lost[species:] / g)
    return g


def first_line(block, group):
    return block * group if isinstance(block, int) else pl.multiple_of(block * group, group)


def table_kernel(log_rate, reactants, products, log_table, reac, both):
    species, reactions = reactants.shape
    reactant = reactants[...].astype(f32)
    reac[...] = reactant.T.astype(bf16)
    both[:species] = products[...].astype(f32).T.astype(bf16)
    both[species:] = reactant.astype(bf16)
    for k in range(log_rate.shape[0]):
        log_table[k] = jnp.broadcast_to(log_rate[k : k + 1, :], (LANES, reactions)).T


def first_line(block, group):
    return block * group if isinstance(block, int) else pl.multiple_of(block * group, group)


def table_kernel(log_rate, reactants, products, log_table, reac, both):
    species, reactions = reactants.shape
    reactant = reactants[...].astype(f32)
    reac[...] = reactant.T.astype(bf16)
    both[:species] = products[...].astype(f32).T.astype(bf16)
    both[species:] = reactant.astype(bf16)
    for k in range(log_rate.shape[0]):
        log_table[k] = jnp.broadcast_to(log_rate[k : k + 1, :], (LANES, reactions)).T


def tables_of(log_rate, reactants, products):
    species, reactions = reactants.shape
    classes = log_rate.shape[0]
    vmem = pl.BlockSpec(memory_space=pltpu.VMEM)
    return pl.pallas_call(
        table_kernel,
        grid=(1,),
        out_shape=[
            pltpu.VMEM((classes, reactions, LANES), f32),
            pltpu.VMEM((reactions, species), bf16),
            pltpu.VMEM((2 * species, reactions), bf16),
        ],
        in_specs=[
            pl.BlockSpec((classes, reactions), lambda i: (0, 0)),
            pl.BlockSpec((species, reactions), lambda i: (0, 0)),
            pl.BlockSpec((reactions, species), lambda i: (0, 0)),
        ],
        out_specs=[vmem] * 3,
        compiler_params=pltpu.CompilerParams(vmem_limit_bytes=12 << 20),
        name="tables",
    )(log_rate, reactants, products)


def chemistry_kernel(info, start, x, log_table, reac, both, out, result, answer, listed, sem):
    peers, blocks = x.shape[0], EDGE
    species = reac.shape[1]
    group = species // peers
    codes = [info[start[b]] for b in range(blocks)]
    count = jnp.int32(0)
    for b in range(blocks):
        listed[1, b] = lax.bitwise_and(codes[b], 3)
        listed[2, b] = lax.shift_right_logical(codes[b], 2)
        listed[0, count] = b
        count = count + lax.shift_right_logical(codes[b], 2)

    def tile(chosen, first):
        states, logs, lengths = [], [], []
        for b in chosen:
            if first:
                states.append(jnp.maximum(x[:, pl.ds(first_line(b, group), group), :].reshape(species, LANES), FLOOR))
                length = jnp.where(listed[2, b] > 0, 1.0 / SUB, 1.0)
            else:
                states.append(result[b])
                length = 1.0 / SUB
            lengths.append(jnp.full((1, LANES), length, f32))
            logs.append(log_table[listed[1, b]])
        g = euler(
            jnp.concatenate(states, axis=1),
            jnp.concatenate(logs, axis=1),
            jnp.concatenate(lengths, axis=1),
            reac[...],
            both[...],
        )
        for i, b in enumerate(chosen):
            piece = g[:, i * LANES : (i + 1) * LANES]
            result[b] = piece
            for k in range(0, species, 8):
                answer[pl.ds(k * blocks + b, 8, stride=blocks), :] = piece[k : k + 8]

    @pl.loop(0, blocks // TILE)
    def _(i):
        tile([i * TILE + j for j in range(TILE)], True)

    for _ in range(SUB - 1):

        @pl.loop(0, (count + TILE - 1) // TILE)
        def _(i):
            tile([listed[0, jnp.minimum(i * TILE + j, count - 1)] for j in range(TILE)], False)


    copy = pltpu.make_async_copy(answer, out, sem)
    copy.start()
    copy.wait()


def chemistry(x, info, start, log_table, reac, both):
    species, blocks = reac.shape[1], EDGE
    vmem = pl.BlockSpec(memory_space=pltpu.VMEM)
    smem = pl.BlockSpec(memory_space=pltpu.SMEM)
    return pl.pallas_call(
        chemistry_kernel,
        out_shape=pltpu.HBM((species * blocks, LANES), f32),
        in_specs=[smem, smem, vmem, vmem, vmem, vmem],
        out_specs=pl.BlockSpec(memory_space=pltpu.HBM),
        scratch_shapes=[
            pltpu.VMEM((blocks, species, LANES), f32),
            pltpu.VMEM((species * blocks, LANES), f32),
            pltpu.SMEM((3, blocks), jnp.int32),
            pltpu.SemaphoreType.DMA,
        ],
        compiler_params=pltpu.CompilerParams(vmem_limit_bytes=14 << 20),
        name="chemistry",
    )(info, start, x, log_table, reac, both)


def place_kernel(firsts, parts, *rest):
    whole, stage, sems = rest[-3:]
    peers, group, blocks, _ = parts.shape
    count = blocks // len(firsts)
    rows = count * EDGE
    copies = []
    for k, first in enumerate(firsts):
        for side in (0, 1):
            for peer in range(side, peers, 2):
                for s in range(group):
                    at = pl.ds(s * rows + peer // 2, count, stride=EDGE)
                    stage[k, side, at, :] = parts[peer, s, k * count : (k + 1) * count]
            copy = pltpu.make_async_copy(
                stage.at[k, side].reshape(group, rows, LANES),
                whole.at[:, pl.ds(first, rows), pl.ds(side * LANES, LANES)],
                sems.at[2 * k + side],
            )
            copy.start()
            copies.append(copy)
    wait_all(copies)


def place_rows(parts, firsts, rows, *whole):
    peers, group, blocks, _ = parts.shape
    hbm = pl.BlockSpec(memory_space=pltpu.HBM)
    count = len(firsts)
    return pl.pallas_call(
        functools.partial(place_kernel, firsts),
        out_shape=pltpu.HBM((group, rows, 2 * LANES), f32),
        in_specs=[pl.BlockSpec(memory_space=pltpu.VMEM)] + [hbm] * len(whole),
        out_specs=hbm,
        scratch_shapes=[
            pltpu.VMEM((count, 2, group * blocks // count * EDGE, LANES), f32),
            pltpu.SemaphoreType.DMA((2 * count,)),
        ],
        input_output_aliases={1: 0} if whole else {},
        name="place",
    )(pltpu.with_memory_space_constraint(parts, pltpu.VMEM), *whole)


def per_device(
    concentrations,
    diffusion,
    courant_x,
    courant_y,
    log_rate,
    reactants,
    products,
    block_class,
    send_slot,
):
    group, rows, columns = concentrations.shape
    species, reactions = reactants.shape
    peers = species // group
    regions = lax.axis_size("region")
    up = [(i, (i + 1) % regions) for i in range(regions - 1)]
    down = [(j, i) for i, j in up]
    hbm = pl.BlockSpec(memory_space=pltpu.HBM)
    smem = pl.BlockSpec(memory_space=pltpu.SMEM)
    vmem = pl.BlockSpec(memory_space=pltpu.VMEM)
    places = rows // (2 * EDGE)
    lines = EDGE * group

    def buffers(slab_rows):
        row_buffer = pltpu.VMEM((slab_rows, group, columns), f32)
        return [pltpu.VMEM((10, slab_rows, LANES), f32), row_buffer, row_buffer]

    def in_hbm(*arrays):
        return [pltpu.with_memory_space_constraint(v, pltpu.HBM) for v in arrays]

    def in_vmem(*arrays):
        return [pltpu.with_memory_space_constraint(v, pltpu.VMEM) for v in arrays]

    fields = in_hbm(concentrations, courant_x, courant_y)
    slab_rows = rows // 2 + 2 * EDGE
    rim = pltpu.VMEM((group + 2, EDGE, columns), f32)
    last, leading = pl.pallas_call(
        rim_kernel,
        out_shape=(rim, rim),
        in_specs=[hbm] * 3,
        out_specs=(vmem, vmem),
        scratch_shapes=[pltpu.SemaphoreType.DMA((6,))],
        name="rims",
    )(*fields)
    before = lax.ppermute(last, "region", up)
    after = lax.ppermute(leading, "region", down)

    middle, token = pl.pallas_call(
        middle_kernel,
        grid=(1,),
        out_shape=(pltpu.HBM((peers, lines + EDGE, LANES), f32), pltpu.VMEM((EDGE, LANES), f32)),
        in_specs=[hbm] * 6,
        out_specs=(pl.BlockSpec((peers, lines + EDGE, LANES), lambda i: (0, 0, 0)), vmem),
        scratch_shapes=[
            pltpu.SMEM((group,), f32),
            pltpu.SMEM((2 * EDGE,), jnp.int32),
            pltpu.SMEM((2 * EDGE,), jnp.int32),
            pltpu.VMEM((2, group, slab_rows, LANES), f32),
            pltpu.VMEM((slab_rows, columns), f32),
            pltpu.VMEM((slab_rows, columns), f32),
            *buffers(slab_rows),
            pltpu.SemaphoreType.DMA((7,)),
        ],
        compiler_params=pltpu.CompilerParams(vmem_limit_bytes=16 << 20),
        name="middle",
    )(*in_hbm(diffusion, block_class, send_slot), *fields)

    place = jnp.stack([lax.axis_index("region"), jnp.int32(regions)]).astype(jnp.int32)
    slab_rows = rows // 4 + 2 * EDGE
    edges, *tables = pl.pallas_call(
        edge_kernel,
        grid=(1,),
        out_shape=(
            pltpu.HBM((peers, lines, LANES), f32),
            pltpu.VMEM((log_rate.shape[0], reactions, LANES), f32),
            pltpu.VMEM((reactions, species), bf16),
            pltpu.VMEM((2 * species, reactions), bf16),
        ),
        in_specs=[smem] + [hbm] * 4 + [vmem] * 3 + [
            pl.BlockSpec(v.shape, lambda i: (0, 0)) for v in (log_rate, reactants, products)
        ],
        out_specs=(pl.BlockSpec((peers, lines, LANES), lambda i: (0, 0, 0)), vmem, vmem, vmem),
        scratch_shapes=[
            pltpu.SMEM((group,), f32),
            pltpu.VMEM((2, 2, group, slab_rows, LANES), f32),
            pltpu.VMEM((2, slab_rows, columns), f32),
            pltpu.VMEM((2, slab_rows, columns), f32),
            *buffers(slab_rows),
            pltpu.SemaphoreType.DMA((17,)),
        ],
        compiler_params=pltpu.CompilerParams(vmem_limit_bytes=24 << 20),
        cost_estimate=pl.CostEstimate(
            flops=20 * 10**9, transcendentals=0, bytes_accessed=10 << 20
        ),
        name="edges",
    )(place, *in_hbm(diffusion), *fields, *in_vmem(before, after), *in_vmem(token), *in_hbm(log_rate, reactants, products))

    mine = lax.axis_index("species").astype(jnp.int32)
    exchange = functools.partial(
        lax.all_to_all, axis_name="species", split_axis=0, concat_axis=0, tiled=True
    )
    info = None
    done = []
    order = jnp.arange(EDGE, dtype=jnp.int32)
    half = peers // 2
    for slab, source in (
        (middle, order + half // 2),
        (edges, jnp.where(order < half // 2, order, order + half)),
    ):
        gathered = exchange(slab)
        if info is None:
            info = gathered[:, lines, : 2 * EDGE].astype(jnp.int32).reshape(-1)
        start = source * 2 * EDGE + mine
        reacted = chemistry(*in_vmem(gathered), info, start, *in_vmem(*tables))
        done.append(exchange(reacted.reshape(peers, group, EDGE, LANES)))
    quarter = rows // 4
    filled = place_rows(done[0], (quarter,), rows)
    return place_rows(done[1], (0, 3 * quarter), rows, filled)


def solution(mesh):
    in_specs = (
        P("species", "region", None),
        P("species"),
        P("region", None),
        P("region", None),
        P(),
        P(),
        P(),
        P(("region", "species")),
        P(("region", "species")),
    )
    out_specs = P("species", "region", None)
    return jax.shard_map(
        per_device, mesh=mesh, in_specs=in_specs, out_specs=out_specs, check_vma=False
    )
```

```python
import functools

import jax
import jax.numpy as jnp
from jax import lax
from jax.experimental import pallas as pl
from jax.experimental.pallas import tpu as pltpu
from jax.sharding import PartitionSpec as P

STEPS = 3
ITERS = 2
SUB = 2
FLOOR = 0.05
EDGE = 8
LANES = 128
TILE = 4
bf16 = jnp.bfloat16
f32 = jnp.float32


def median0(p, r):
    return jnp.maximum(jnp.minimum(p, r), jnp.minimum(jnp.maximum(p, r), 0.0))


def shift_left(pair, lane):
    a, b = (pltpu.roll(v, LANES - 1, 1) for v in pair)
    last = lane == LANES - 1
    return jnp.where(last, b, a), jnp.where(last, 0.0, b)


def shift_right(pair, first, lane):
    a, b = (pltpu.roll(v, 1, 1) for v in pair)
    head = lane == 0
    return jnp.where(head, first, a), jnp.where(head, a, b)


def halves(v):
    return v[:, :LANES], v[:, LANES:]


def face_coefs(a):
    size = jnp.abs(a)
    return 0.5 * size * (1.0 - size)


def store_coefs(cx, cy, coef):
    ax = 0.5 * (cx + jnp.concatenate([cx[1:], cx[:1]], axis=0))
    edge = lax.broadcasted_iota(jnp.int32, cy.shape, 1) == 2 * LANES - 1
    ay = 0.5 * (cy + jnp.where(edge, 0.0, jnp.concatenate([cy[:, 1:], cy[:, :1]], axis=1)))
    al = 0.5 * cy[:, :LANES]
    al_weight = jnp.where(al < 0.0, face_coefs(al), 0.0)
    pairs = [halves(v) for v in (ax, face_coefs(ax), ay, face_coefs(ay))]
    pairs.append((jnp.minimum(al, 0.0), al_weight))
    for k, pair in enumerate(pairs):
        coef[2 * k] = pair[0]
        coef[2 * k + 1] = pair[1]


def one_flux(q, qn, d, m, mn, a, e, nu):
    up = a >= 0.0
    return a * jnp.where(up, q, qn) + e * jnp.where(up, m, mn) - nu * d


def sweep(load, store, coef, nu, lo, hi, unroll, keep=None):
    group = nu.shape[0]
    lane = lax.broadcasted_iota(jnp.int32, (group, LANES), 1)

    def spread(which, row):
        return tuple(coef[2 * which + k, pl.ds(row, group, stride=0), :] for k in (0, 1))

    def x_flux(row, q, qn, d, m, mn):
        a, e = spread(0, row), spread(1, row)
        return tuple(one_flux(q[i], qn[i], d[i], m[i], mn[i], a[i], e[i], nu) for i in (0, 1))

    def diff(q, qn):
        return tuple(y - x for x, y in zip(q, qn))

    def limited(p, r):
        return tuple(median0(x, y) for x, y in zip(p, r))

    qa, qb, qc, qd = (load(lo + k) for k in (-2, -1, 0, 1))
    da, db, dc = diff(qa, qb), diff(qb, qc), diff(qc, qd)
    mb, mc = limited(da, db), limited(db, dc)
    behind = x_flux(lo - 1, qb, qc, db, mb, mc)

    def row_step(row, carry):
        q, qn, d, m, behind = carry
        qnn = load(row + 2)
        dn = diff(qn, qnn)
        mn = limited(d, dn)
        fx = x_flux(row, q, qn, d, m, mn)
        right = shift_left(q, lane)
        g = diff(q, right)
        s = limited(shift_right(g, q[0], lane), g)
        sn = shift_left(s, lane)
        a, e = spread(2, row), spread(3, row)
        fy = tuple(one_flux(q[i], right[i], g[i], s[i], sn[i], a[i], e[i], nu) for i in (0, 1))
        la, le = spread(4, row)
        fl = shift_right(fy, (la - nu) * q[0] + le * s[0], lane)
        new = tuple(q[i] - (fx[i] - behind[i]) - (fy[i] - fl[i]) for i in (0, 1))
        if keep is not None:
            scale = keep(row)
            new = tuple(v * scale for v in new)
        store(row, new)
        return qn, qnn, dn, mn, fx

    def steps(i, carry):
        for k in range(unroll):
            carry = row_step(lo + i * unroll + k, carry)
        return carry

    count = hi - lo
    carry = lax.fori_loop(0, count // unroll, steps, (qc, qd, dc, mc, behind))
    for row in range(lo + count // unroll * unroll, hi):
        carry = row_step(row, carry)


def buffer_access(buf):
    def load(row):
        return buf[row, :, :LANES], buf[row, :, LANES:]

    def store(row, pair):
        buf[row, :, :LANES] = pair[0]
        buf[row, :, LANES:] = pair[1]

    return load, store


def start_all(copies):
    for copy in copies:
        copy.start()


def wait_all(copies):
    for copy in copies:
        copy.wait()


def spread_species(diffuse, group):
    lane = lax.broadcasted_iota(jnp.int32, (group, LANES), 0)
    nu = jnp.zeros((group, LANES), f32)
    for k in range(group):
        nu = jnp.where(lane == k, diffuse[k], nu)
    return nu


def raw_access(block):
    group, rows, _ = block.shape[1:]
    flat = [block.at[k].reshape(group * rows, LANES) for k in (0, 1)]

    def load(row):
        return tuple(part[pl.ds(row, group, stride=rows), :] for part in flat)

    return load


def three_sweeps(load, store, coef, nu, one, two, rows, unrolls, keep=None):
    load1, store1 = buffer_access(one)
    load2, store2 = buffer_access(two)
    sweep(load, store1, coef, nu, 4, rows - 4, unrolls[0], keep)
    sweep(load1, store2, coef, nu, 6, rows - 6, unrolls[1], keep)
    sweep(load2, store, coef, nu, 8, rows - 8, unrolls[2])


def store_grouped(out, base, group):
    def store(row, pair):
        at = row - EDGE
        line = pl.multiple_of((base + lax.shift_right_logical(at, 3)) * group, group)
        peer = 2 * lax.bitwise_and(at, EDGE - 1)
        out[peer, pl.ds(line, group), :] = pair[0]
        out[peer + 1, pl.ds(line, group), :] = pair[1]

    return store


def rim_kernel(conc, cx, cy, last, leading, sems):
    group, total, _ = conc.shape
    copies = []

    def copy(src, dst):
        copies.append(pltpu.make_async_copy(src, dst, sems.at[len(copies)]))

    for rim, at in ((last, total - EDGE), (leading, 0)):
        copy(conc.at[:, pl.ds(at, EDGE)], rim.at[pl.ds(0, group)])
        copy(cx.at[pl.ds(at, EDGE)], rim.at[group])
        copy(cy.at[pl.ds(at, EDGE)], rim.at[group + 1])
    start_all(copies)
    wait_all(copies)


def middle_kernel(
    diffuse_in,
    classes_in,
    slots_in,
    conc,
    cx,
    cy,
    out,
    token,
    diffuse,
    classes,
    slots,
    raw,
    wx,
    wy,
    coef,
    one,
    two,
    sems,
):
    group, rows = raw.shape[1:3]
    total = conc.shape[1]
    first = total // 4 - EDGE
    pairs = [(cx.at[pl.ds(first, rows)], wx), (cy.at[pl.ds(first, rows)], wy)]
    pairs += [
        (conc.at[:, pl.ds(first, rows), pl.ds(k * LANES, LANES)], raw.at[k]) for k in (0, 1)
    ]
    pairs += [(diffuse_in, diffuse), (classes_in, classes), (slots_in, slots)]
    copies = [pltpu.make_async_copy(*pair, sems.at[k]) for k, pair in enumerate(pairs)]
    start_all(copies)
    wait_all(copies[4:7])
    nu = spread_species(diffuse, group)
    lane = lax.broadcasted_iota(jnp.int32, (EDGE, LANES), 1)
    codes = jnp.zeros((EDGE, LANES), f32)
    for k in range(classes.shape[0]):
        code = classes[k] + jnp.where(slots[k] >= 0, 4, 0)
        codes = jnp.where(lane == k, code.astype(f32), codes)
    for k in range(out.shape[0]):
        out[k, EDGE * group :, :] = codes
    wait_all(copies[:2])
    store_coefs(wx[...], wy[...], coef)
    wait_all(copies[2:4])
    three_sweeps(
        raw_access(raw), store_grouped(out, 0, group), coef, nu, one, two, rows, (18, 17, 16)
    )
    token[...] = codes


def edge_kernel(
    place,
    diffuse_in,
    conc,
    cx,
    cy,
    before,
    after,
    _token,
    log_rate,
    reactants,
    products,
    out,
    log_table,
    both,
    diffuse,
    raw,
    wx,
    wy,
    coef,
    one,
    two,
    sems,
):
    group, rows = raw.shape[2:4]
    total = conc.shape[1]
    own = rows - EDGE
    copies = []

    def copy(src, dst):
        copies.append(pltpu.make_async_copy(src, dst, sems.at[len(copies)]))

    copy(diffuse_in, diffuse)
    for slab, halo, own_first, own_at, halo_at in (
        (0, before, 0, EDGE, 0),
        (1, after, total - own, 0, own),
    ):
        for k, (wind, dst) in enumerate(((cx, wx), (cy, wy))):
            copy(wind.at[pl.ds(own_first, own)], dst.at[slab, pl.ds(own_at, own)])
            copy(halo.at[group + k], dst.at[slab, pl.ds(halo_at, EDGE)])
        for k in (0, 1):
            lanes = pl.ds(k * LANES, LANES)
            dst = raw.at[slab, k]
            copy(conc.at[:, pl.ds(own_first, own), lanes], dst.at[:, pl.ds(own_at, own)])
            copy(halo.at[pl.ds(0, group), :, lanes], dst.at[:, pl.ds(halo_at, EDGE)])
    start_all(copies)
    table_kernel(log_rate, reactants, products, log_table, both)
    wait_all(copies)
    nu = spread_species(diffuse, group)

    @pl.loop(0, 2)
    def _(slab):
        store_coefs(wx[slab], wy[slab], coef)
        open_top = jnp.logical_and(slab == 0, place[0] == 0)
        open_end = jnp.logical_and(slab == 1, place[0] == place[1] - 1)

        def keep(row):
            outside = jnp.logical_or(
                jnp.logical_and(open_top, row < EDGE), jnp.logical_and(open_end, row >= own)
            )
            return jnp.where(outside, 0.0, 1.0)

        three_sweeps(
            raw_access(raw.at[slab]),
            store_grouped(out, slab * 4, group),
            coef,
            nu,
            one,
            two,
            rows,
            (10, 12, 16),
            keep,
        )


def split(x):
    high = x.astype(bf16)
    return high, (x - high.astype(f32)).astype(bf16)


def table_dot(table, x):
    high, low = split(x)
    return jnp.dot(table, high, preferred_element_type=f32) + jnp.dot(
        table, low, preferred_element_type=f32
    )


def blocks_dot(blocks, x):
    size = x.shape[0]
    high, low = split(x)
    parts = [blocks[:, k : k + size] for k in range(0, blocks.shape[1], size)]
    return jnp.concatenate(
        [
            jnp.dot(part, high, preferred_element_type=f32)
            + jnp.dot(part, low, preferred_element_type=f32)
            for part in parts
        ],
        axis=0,
    )


def euler(state, logs, step, both):
    species = state.shape[0]
    reac = both[2 * species :]
    both = both[: 2 * species]
    g = state
    for _ in range(ITERS):
        rates = jnp.exp(logs + blocks_dot(reac, jnp.log(g)))
        made_lost = table_dot(both, rates)
        g = (state + step * made_lost[:species]) / (1.0 + step * made_lost[species:] / g)
    return g


def first_line(block, group):
    return block * group if isinstance(block, int) else pl.multiple_of(block * group, group)


def table_kernel(log_rate, reactants, products, log_table, both):
    species, reactions = reactants.shape
    reactant = reactants[...].astype(f32)
    both[:species] = products[...].astype(f32).T.astype(bf16)
    both[species : 2 * species] = reactant.astype(bf16)
    for k in range(0, reactions, species):
        both[2 * species :, k : k + species] = reactant[:, k : k + species].T.astype(bf16)
    for k in range(log_rate.shape[0]):
        log_table[k] = jnp.broadcast_to(log_rate[k : k + 1, :], (LANES, reactions)).T


def first_line(block, group):
    return block * group if isinstance(block, int) else pl.multiple_of(block * group, group)


def table_kernel(log_rate, reactants, products, log_table, both):
    species, reactions = reactants.shape
    reactant = reactants[...].astype(f32)
    both[:species] = products[...].astype(f32).T.astype(bf16)
    both[species : 2 * species] = reactant.astype(bf16)
    for k in range(0, reactions, species):
        both[2 * species :, k : k + species] = reactant[:, k : k + species].T.astype(bf16)
    for k in range(log_rate.shape[0]):
        log_table[k] = jnp.broadcast_to(log_rate[k : k + 1, :], (LANES, reactions)).T


def tables_of(log_rate, reactants, products):
    species, reactions = reactants.shape
    classes = log_rate.shape[0]
    vmem = pl.BlockSpec(memory_space=pltpu.VMEM)
    return pl.pallas_call(
        table_kernel,
        grid=(1,),
        out_shape=[
            pltpu.VMEM((classes, reactions, LANES), f32),
            pltpu.VMEM((3 * species, reactions), bf16),
        ],
        in_specs=[
            pl.BlockSpec((classes, reactions), lambda i: (0, 0)),
            pl.BlockSpec((species, reactions), lambda i: (0, 0)),
            pl.BlockSpec((reactions, species), lambda i: (0, 0)),
        ],
        out_specs=[vmem] * 3,
        compiler_params=pltpu.CompilerParams(vmem_limit_bytes=12 << 20),
        name="tables",
    )(log_rate, reactants, products)


def chemistry_kernel(info, start, x, log_table, both, out, result, answer, listed, sem):
    peers, blocks = x.shape[0], EDGE
    species = both.shape[0] // 3
    group = species // peers
    codes = [info[start[b]] for b in range(blocks)]
    count = jnp.int32(0)
    for b in range(blocks):
        listed[1, b] = lax.bitwise_and(codes[b], 3)
        listed[2, b] = lax.shift_right_logical(codes[b], 2)
        listed[0, count] = b
        count = count + lax.shift_right_logical(codes[b], 2)

    def tile(chosen, first):
        states, logs, lengths = [], [], []
        for b in chosen:
            if first:
                states.append(jnp.maximum(x[:, pl.ds(first_line(b, group), group), :].reshape(species, LANES), FLOOR))
                length = jnp.where(listed[2, b] > 0, 1.0 / SUB, 1.0)
            else:
                states.append(result[b])
                length = 1.0 / SUB
            lengths.append(jnp.full((1, LANES), length, f32))
            logs.append(log_table[listed[1, b]])
        g = euler(
            jnp.concatenate(states, axis=1),
            jnp.concatenate(logs, axis=1),
            jnp.concatenate(lengths, axis=1),
            both[...],
        )
        for i, b in enumerate(chosen):
            piece = g[:, i * LANES : (i + 1) * LANES]
            result[b] = piece
            for k in range(0, species, 8):
                answer[pl.ds(k * blocks + b, 8, stride=blocks), :] = piece[k : k + 8]

    @pl.loop(0, blocks // TILE)
    def _(i):
        tile([i * TILE + j for j in range(TILE)], True)

    for _ in range(SUB - 1):

        @pl.loop(0, (count + TILE - 1) // TILE)
        def _(i):
            tile([listed[0, jnp.minimum(i * TILE + j, count - 1)] for j in range(TILE)], False)


    copy = pltpu.make_async_copy(answer, out, sem)
    copy.start()
    copy.wait()


def chemistry(x, info, start, log_table, both):
    species, blocks = both.shape[0] // 3, EDGE
    vmem = pl.BlockSpec(memory_space=pltpu.VMEM)
    smem = pl.BlockSpec(memory_space=pltpu.SMEM)
    return pl.pallas_call(
        chemistry_kernel,
        out_shape=pltpu.HBM((species * blocks, LANES), f32),
        in_specs=[smem, smem, vmem, vmem, vmem],
        out_specs=pl.BlockSpec(memory_space=pltpu.HBM),
        scratch_shapes=[
            pltpu.VMEM((blocks, species, LANES), f32),
            pltpu.VMEM((species * blocks, LANES), f32),
            pltpu.SMEM((3, blocks), jnp.int32),
            pltpu.SemaphoreType.DMA,
        ],
        compiler_params=pltpu.CompilerParams(vmem_limit_bytes=14 << 20),
        name="chemistry",
    )(info, start, x, log_table, both)


def place_kernel(firsts, parts, *rest):
    whole, stage, sems = rest[-3:]
    peers, group, blocks, _ = parts.shape
    count = blocks // len(firsts)
    rows = count * EDGE
    copies = []
    for k, first in enumerate(firsts):
        for side in (0, 1):
            for peer in range(side, peers, 2):
                for s in range(group):
                    at = pl.ds(s * rows + peer // 2, count, stride=EDGE)
                    stage[k, side, at, :] = parts[peer, s, k * count : (k + 1) * count]
            copy = pltpu.make_async_copy(
                stage.at[k, side].reshape(group, rows, LANES),
                whole.at[:, pl.ds(first, rows), pl.ds(side * LANES, LANES)],
                sems.at[2 * k + side],
            )
            copy.start()
            copies.append(copy)
    wait_all(copies)


def place_rows(parts, firsts, rows, *whole):
    peers, group, blocks, _ = parts.shape
    hbm = pl.BlockSpec(memory_space=pltpu.HBM)
    count = len(firsts)
    return pl.pallas_call(
        functools.partial(place_kernel, firsts),
        out_shape=pltpu.HBM((group, rows, 2 * LANES), f32),
        in_specs=[pl.BlockSpec(memory_space=pltpu.VMEM)] + [hbm] * len(whole),
        out_specs=hbm,
        scratch_shapes=[
            pltpu.VMEM((count, 2, group * blocks // count * EDGE, LANES), f32),
            pltpu.SemaphoreType.DMA((2 * count,)),
        ],
        input_output_aliases={1: 0} if whole else {},
        name="place",
    )(pltpu.with_memory_space_constraint(parts, pltpu.VMEM), *whole)


def per_device(
    concentrations,
    diffusion,
    courant_x,
    courant_y,
    log_rate,
    reactants,
    products,
    block_class,
    send_slot,
):
    group, rows, columns = concentrations.shape
    species, reactions = reactants.shape
    peers = species // group
    regions = lax.axis_size("region")
    up = [(i, (i + 1) % regions) for i in range(regions - 1)]
    down = [(j, i) for i, j in up]
    hbm = pl.BlockSpec(memory_space=pltpu.HBM)
    smem = pl.BlockSpec(memory_space=pltpu.SMEM)
    vmem = pl.BlockSpec(memory_space=pltpu.VMEM)
    places = rows // (2 * EDGE)
    lines = EDGE * group

    def buffers(slab_rows):
        row_buffer = pltpu.VMEM((slab_rows, group, columns), f32)
        return [pltpu.VMEM((10, slab_rows, LANES), f32), row_buffer, row_buffer]

    def in_hbm(*arrays):
        return [pltpu.with_memory_space_constraint(v, pltpu.HBM) for v in arrays]

    def in_vmem(*arrays):
        return [pltpu.with_memory_space_constraint(v, pltpu.VMEM) for v in arrays]

    fields = in_hbm(concentrations, courant_x, courant_y)
    slab_rows = rows // 2 + 2 * EDGE
    rim = pltpu.VMEM((group + 2, EDGE, columns), f32)
    last, leading = pl.pallas_call(
        rim_kernel,
        out_shape=(rim, rim),
        in_specs=[hbm] * 3,
        out_specs=(vmem, vmem),
        scratch_shapes=[pltpu.SemaphoreType.DMA((6,))],
        name="rims",
    )(*fields)
    before = lax.ppermute(last, "region", up)
    after = lax.ppermute(leading, "region", down)

    middle, token = pl.pallas_call(
        middle_kernel,
        grid=(1,),
        out_shape=(pltpu.HBM((peers, lines + EDGE, LANES), f32), pltpu.VMEM((EDGE, LANES), f32)),
        in_specs=[hbm] * 6,
        out_specs=(pl.BlockSpec((peers, lines + EDGE, LANES), lambda i: (0, 0, 0)), vmem),
        scratch_shapes=[
            pltpu.SMEM((group,), f32),
            pltpu.SMEM((2 * EDGE,), jnp.int32),
            pltpu.SMEM((2 * EDGE,), jnp.int32),
            pltpu.VMEM((2, group, slab_rows, LANES), f32),
            pltpu.VMEM((slab_rows, columns), f32),
            pltpu.VMEM((slab_rows, columns), f32),
            *buffers(slab_rows),
            pltpu.SemaphoreType.DMA((7,)),
        ],
        compiler_params=pltpu.CompilerParams(vmem_limit_bytes=16 << 20),
        name="middle",
    )(*in_hbm(diffusion, block_class, send_slot), *fields)

    place = jnp.stack([lax.axis_index("region"), jnp.int32(regions)]).astype(jnp.int32)
    slab_rows = rows // 4 + 2 * EDGE
    edges, *tables = pl.pallas_call(
        edge_kernel,
        grid=(1,),
        out_shape=(
            pltpu.HBM((peers, lines, LANES), f32),
            pltpu.VMEM((log_rate.shape[0], reactions, LANES), f32),
            pltpu.VMEM((3 * species, reactions), bf16),
        ),
        in_specs=[smem] + [hbm] * 4 + [vmem] * 3 + [
            pl.BlockSpec(v.shape, lambda i: (0, 0)) for v in (log_rate, reactants, products)
        ],
        out_specs=(pl.BlockSpec((peers, lines, LANES), lambda i: (0, 0, 0)), vmem, vmem),
        scratch_shapes=[
            pltpu.SMEM((group,), f32),
            pltpu.VMEM((2, 2, group, slab_rows, LANES), f32),
            pltpu.VMEM((2, slab_rows, columns), f32),
            pltpu.VMEM((2, slab_rows, columns), f32),
            *buffers(slab_rows),
            pltpu.SemaphoreType.DMA((17,)),
        ],
        compiler_params=pltpu.CompilerParams(vmem_limit_bytes=24 << 20),
        cost_estimate=pl.CostEstimate(
            flops=20 * 10**9, transcendentals=0, bytes_accessed=10 << 20
        ),
        name="edges",
    )(place, *in_hbm(diffusion), *fields, before, after, *in_vmem(token), *in_hbm(log_rate, reactants, products))

    mine = lax.axis_index("species").astype(jnp.int32)
    exchange = functools.partial(
        lax.all_to_all, axis_name="species", split_axis=0, concat_axis=0, tiled=True
    )
    info = None
    done = []
    order = jnp.arange(EDGE, dtype=jnp.int32)
    half = peers // 2
    for slab, source in (
        (middle, order + half // 2),
        (edges, jnp.where(order < half // 2, order, order + half)),
    ):
        gathered = exchange(slab)
        if info is None:
            info = gathered[:, lines, : 2 * EDGE].astype(jnp.int32).reshape(-1)
        start = source * 2 * EDGE + mine
        reacted = chemistry(*in_vmem(gathered), info, start, *in_vmem(*tables))
        done.append(exchange(reacted.reshape(peers, group, EDGE, LANES)))
    quarter = rows // 4
    filled = place_rows(done[0], (quarter,), rows)
    return place_rows(done[1], (0, 3 * quarter), rows, filled)


def solution(mesh):
    in_specs = (
        P("species", "region", None),
        P("species"),
        P("region", None),
        P("region", None),
        P(),
        P(),
        P(),
        P(("region", "species")),
        P(("region", "species")),
    )
    out_specs = P("species", "region", None)
    return jax.shard_map(
        per_device, mesh=mesh, in_specs=in_specs, out_specs=out_specs, check_vma=False
    )
```

```python
import functools

import jax
import jax.numpy as jnp
from jax import lax
from jax.experimental import pallas as pl
from jax.experimental.pallas import tpu as pltpu
from jax.sharding import PartitionSpec as P

STEPS = 3
ITERS = 2
SUB = 2
FLOOR = 0.05
EDGE = 8
LANES = 128
TILE = 4
bf16 = jnp.bfloat16
f32 = jnp.float32


def median0(p, r):
    return jnp.maximum(jnp.minimum(p, r), jnp.minimum(jnp.maximum(p, r), 0.0))


def shift_left(pair, lane):
    a, b = (pltpu.roll(v, LANES - 1, 1) for v in pair)
    last = lane == LANES - 1
    return jnp.where(last, b, a), jnp.where(last, 0.0, b)


def shift_right(pair, first, lane):
    a, b = (pltpu.roll(v, 1, 1) for v in pair)
    head = lane == 0
    return jnp.where(head, first, a), jnp.where(head, a, b)


def halves(v):
    return v[:, :LANES], v[:, LANES:]


def face_coefs(a):
    size = jnp.abs(a)
    return 0.5 * size * (1.0 - size)


def store_coefs(cx, cy, coef):
    ax = 0.5 * (cx + jnp.concatenate([cx[1:], cx[:1]], axis=0))
    edge = lax.broadcasted_iota(jnp.int32, cy.shape, 1) == 2 * LANES - 1
    ay = 0.5 * (cy + jnp.where(edge, 0.0, jnp.concatenate([cy[:, 1:], cy[:, :1]], axis=1)))
    al = 0.5 * cy[:, :LANES]
    al_weight = jnp.where(al < 0.0, face_coefs(al), 0.0)
    pairs = [halves(v) for v in (ax, face_coefs(ax), ay, face_coefs(ay))]
    pairs.append((jnp.minimum(al, 0.0), al_weight))
    for k, pair in enumerate(pairs):
        coef[2 * k] = pair[0]
        coef[2 * k + 1] = pair[1]


def one_flux(q, qn, d, m, mn, a, e, nu):
    up = a >= 0.0
    return a * jnp.where(up, q, qn) + e * jnp.where(up, m, mn) - nu * d


def sweep(load, store, coef, nu, lo, hi, unroll, keep=None):
    group = nu.shape[0]
    lane = lax.broadcasted_iota(jnp.int32, (group, LANES), 1)

    def spread(which, row):
        return tuple(coef[2 * which + k, pl.ds(row, group, stride=0), :] for k in (0, 1))

    def x_flux(row, q, qn, d, m, mn):
        a, e = spread(0, row), spread(1, row)
        return tuple(one_flux(q[i], qn[i], d[i], m[i], mn[i], a[i], e[i], nu) for i in (0, 1))

    def diff(q, qn):
        return tuple(y - x for x, y in zip(q, qn))

    def limited(p, r):
        return tuple(median0(x, y) for x, y in zip(p, r))

    qa, qb, qc, qd = (load(lo + k) for k in (-2, -1, 0, 1))
    da, db, dc = diff(qa, qb), diff(qb, qc), diff(qc, qd)
    mb, mc = limited(da, db), limited(db, dc)
    behind = x_flux(lo - 1, qb, qc, db, mb, mc)

    def row_step(row, carry):
        q, qn, d, m, behind = carry
        qnn = load(row + 2)
        dn = diff(qn, qnn)
        mn = limited(d, dn)
        fx = x_flux(row, q, qn, d, m, mn)
        right = shift_left(q, lane)
        g = diff(q, right)
        s = limited(shift_right(g, q[0], lane), g)
        sn = shift_left(s, lane)
        a, e = spread(2, row), spread(3, row)
        fy = tuple(one_flux(q[i], right[i], g[i], s[i], sn[i], a[i], e[i], nu) for i in (0, 1))
        la, le = spread(4, row)
        fl = shift_right(fy, (la - nu) * q[0] + le * s[0], lane)
        new = tuple(q[i] - (fx[i] - behind[i]) - (fy[i] - fl[i]) for i in (0, 1))
        if keep is not None:
            scale = keep(row)
            new = tuple(v * scale for v in new)
        store(row, new)
        return qn, qnn, dn, mn, fx

    def steps(i, carry):
        for k in range(unroll):
            carry = row_step(lo + i * unroll + k, carry)
        return carry

    count = hi - lo
    carry = lax.fori_loop(0, count // unroll, steps, (qc, qd, dc, mc, behind))
    for row in range(lo + count // unroll * unroll, hi):
        carry = row_step(row, carry)


def buffer_access(buf):
    def load(row):
        return buf[row, :, :LANES], buf[row, :, LANES:]

    def store(row, pair):
        buf[row, :, :LANES] = pair[0]
        buf[row, :, LANES:] = pair[1]

    return load, store


def start_all(copies):
    for copy in copies:
        copy.start()


def wait_all(copies):
    for copy in copies:
        copy.wait()


def spread_species(diffuse, group):
    lane = lax.broadcasted_iota(jnp.int32, (group, LANES), 0)
    nu = jnp.zeros((group, LANES), f32)
    for k in range(group):
        nu = jnp.where(lane == k, diffuse[k], nu)
    return nu


def raw_access(block):
    group, rows, _ = block.shape[1:]
    flat = [block.at[k].reshape(group * rows, LANES) for k in (0, 1)]

    def load(row):
        return tuple(part[pl.ds(row, group, stride=rows), :] for part in flat)

    return load


def three_sweeps(load, store, coef, nu, one, two, rows, unrolls, keep=None):
    load1, store1 = buffer_access(one)
    load2, store2 = buffer_access(two)
    sweep(load, store1, coef, nu, 4, rows - 4, unrolls[0], keep)
    sweep(load1, store2, coef, nu, 6, rows - 6, unrolls[1], keep)
    sweep(load2, store, coef, nu, 8, rows - 8, unrolls[2])


def store_grouped(out, base, group):
    def store(row, pair):
        at = row - EDGE
        line = pl.multiple_of((base + lax.shift_right_logical(at, 3)) * group, group)
        peer = 2 * lax.bitwise_and(at, EDGE - 1)
        out[peer, pl.ds(line, group), :] = pair[0]
        out[peer + 1, pl.ds(line, group), :] = pair[1]

    return store


def rim_kernel(conc, cx, cy, last, leading, sems):
    group, total, _ = conc.shape
    copies = []

    def copy(src, dst):
        copies.append(pltpu.make_async_copy(src, dst, sems.at[len(copies)]))

    for rim, at in ((last, total - EDGE), (leading, 0)):
        copy(conc.at[:, pl.ds(at, EDGE)], rim.at[pl.ds(0, group)])
        copy(cx.at[pl.ds(at, EDGE)], rim.at[group])
        copy(cy.at[pl.ds(at, EDGE)], rim.at[group + 1])
    start_all(copies)
    wait_all(copies)


def middle_kernel(
    diffuse_in,
    classes_in,
    slots_in,
    conc,
    cx,
    cy,
    out,
    token,
    diffuse,
    classes,
    slots,
    raw,
    wx,
    wy,
    coef,
    one,
    two,
    sems,
):
    group, rows = raw.shape[1:3]
    total = conc.shape[1]
    first = total // 4 - EDGE
    pairs = [(cx.at[pl.ds(first, rows)], wx), (cy.at[pl.ds(first, rows)], wy)]
    pairs += [
        (conc.at[:, pl.ds(first, rows), pl.ds(k * LANES, LANES)], raw.at[k]) for k in (0, 1)
    ]
    pairs += [(diffuse_in, diffuse), (classes_in, classes), (slots_in, slots)]
    copies = [pltpu.make_async_copy(*pair, sems.at[k]) for k, pair in enumerate(pairs)]
    start_all(copies)
    wait_all(copies[4:7])
    nu = spread_species(diffuse, group)
    lane = lax.broadcasted_iota(jnp.int32, (EDGE, LANES), 1)
    codes = jnp.zeros((EDGE, LANES), f32)
    for k in range(classes.shape[0]):
        code = classes[k] + jnp.where(slots[k] >= 0, 4, 0)
        codes = jnp.where(lane == k, code.astype(f32), codes)
    for k in range(out.shape[0]):
        out[k, EDGE * group :, :] = codes
    wait_all(copies[:2])
    store_coefs(wx[...], wy[...], coef)
    wait_all(copies[2:4])
    three_sweeps(
        raw_access(raw), store_grouped(out, 0, group), coef, nu, one, two, rows, (18, 17, 16)
    )
    token[...] = codes


def edge_kernel(
    place,
    diffuse_in,
    conc,
    cx,
    cy,
    before,
    after,
    _token,
    log_rate,
    reactants,
    products,
    out,
    log_table,
    both,
    diffuse,
    raw,
    wx,
    wy,
    coef,
    one,
    two,
    sems,
):
    group, rows = raw.shape[2:4]
    total = conc.shape[1]
    own = rows - EDGE
    copies = []

    def copy(src, dst):
        copies.append(pltpu.make_async_copy(src, dst, sems.at[len(copies)]))

    copy(diffuse_in, diffuse)
    for slab, halo, own_first, own_at, halo_at in (
        (0, before, 0, EDGE, 0),
        (1, after, total - own, 0, own),
    ):
        for k, (wind, dst) in enumerate(((cx, wx), (cy, wy))):
            copy(wind.at[pl.ds(own_first, own)], dst.at[slab, pl.ds(own_at, own)])
            copy(halo.at[group + k], dst.at[slab, pl.ds(halo_at, EDGE)])
        for k in (0, 1):
            lanes = pl.ds(k * LANES, LANES)
            dst = raw.at[slab, k]
            copy(conc.at[:, pl.ds(own_first, own), lanes], dst.at[:, pl.ds(own_at, own)])
            copy(halo.at[pl.ds(0, group), :, lanes], dst.at[:, pl.ds(halo_at, EDGE)])
    start_all(copies)
    table_kernel(log_rate, reactants, products, log_table, both)
    wait_all(copies)
    nu = spread_species(diffuse, group)

    @pl.loop(0, 2)
    def _(slab):
        store_coefs(wx[slab], wy[slab], coef)
        open_top = jnp.logical_and(slab == 0, place[0] == 0)
        open_end = jnp.logical_and(slab == 1, place[0] == place[1] - 1)

        def keep(row):
            outside = jnp.logical_or(
                jnp.logical_and(open_top, row < EDGE), jnp.logical_and(open_end, row >= own)
            )
            return jnp.where(outside, 0.0, 1.0)

        three_sweeps(
            raw_access(raw.at[slab]),
            store_grouped(out, slab * 4, group),
            coef,
            nu,
            one,
            two,
            rows,
            (10, 12, 16),
            keep,
        )


def split(x):
    high = x.astype(bf16)
    return high, (x - high.astype(f32)).astype(bf16)


def table_dot(table, x):
    high, low = split(x)
    return jnp.dot(table, high, preferred_element_type=f32) + jnp.dot(
        table, low, preferred_element_type=f32
    )


def blocks_dot(blocks, x):
    size = x.shape[0]
    high, low = split(x)
    parts = [blocks[:, k : k + size] for k in range(0, blocks.shape[1], size)]
    return jnp.concatenate(
        [
            jnp.dot(part, high, preferred_element_type=f32)
            + jnp.dot(part, low, preferred_element_type=f32)
            for part in parts
        ],
        axis=0,
    )


def euler(state, logs, step, both):
    species = state.shape[0]
    reac = both[2 * species :]
    both = both[: 2 * species]
    g = state
    for _ in range(ITERS):
        rates = jnp.exp(logs + blocks_dot(reac, jnp.log(g)))
        made_lost = table_dot(both, rates)
        g = (state + step * made_lost[:species]) / (1.0 + step * made_lost[species:] / g)
    return g


def first_line(block, group):
    return block * group if isinstance(block, int) else pl.multiple_of(block * group, group)


def table_kernel(log_rate, reactants, products, log_table, both):
    species, reactions = reactants.shape
    reactant = reactants[...].astype(f32)
    both[:species] = products[...].astype(f32).T.astype(bf16)
    both[species : 2 * species] = reactant.astype(bf16)
    for k in range(0, reactions, species):
        both[2 * species :, k : k + species] = reactant[:, k : k + species].T.astype(bf16)
    for k in range(log_rate.shape[0]):
        log_table[k] = jnp.broadcast_to(log_rate[k : k + 1, :], (LANES, reactions)).T


def first_line(block, group):
    return block * group if isinstance(block, int) else pl.multiple_of(block * group, group)


def table_kernel(log_rate, reactants, products, log_table, both):
    species, reactions = reactants.shape
    reactant = reactants[...].astype(f32)
    both[:species] = products[...].astype(f32).T.astype(bf16)
    both[species : 2 * species] = reactant.astype(bf16)
    for k in range(0, reactions, species):
        both[2 * species :, k : k + species] = reactant[:, k : k + species].T.astype(bf16)
    for k in range(log_rate.shape[0]):
        log_table[k] = jnp.broadcast_to(log_rate[k : k + 1, :], (LANES, reactions)).T


def tables_of(log_rate, reactants, products):
    species, reactions = reactants.shape
    classes = log_rate.shape[0]
    vmem = pl.BlockSpec(memory_space=pltpu.VMEM)
    return pl.pallas_call(
        table_kernel,
        grid=(1,),
        out_shape=[
            pltpu.VMEM((classes, reactions, LANES), f32),
            pltpu.VMEM((3 * species, reactions), bf16),
        ],
        in_specs=[
            pl.BlockSpec((classes, reactions), lambda i: (0, 0)),
            pl.BlockSpec((species, reactions), lambda i: (0, 0)),
            pl.BlockSpec((reactions, species), lambda i: (0, 0)),
        ],
        out_specs=[vmem] * 3,
        compiler_params=pltpu.CompilerParams(vmem_limit_bytes=12 << 20),
        name="tables",
    )(log_rate, reactants, products)


def chemistry_kernel(info, start, x, log_table, both, out, result, answer, listed, sem):
    peers, blocks = x.shape[0], EDGE
    species = both.shape[0] // 3
    group = species // peers
    codes = [info[start[b]] for b in range(blocks)]
    count = jnp.int32(0)
    for b in range(blocks):
        listed[1, b] = lax.bitwise_and(codes[b], 3)
        listed[2, b] = lax.shift_right_logical(codes[b], 2)
        listed[0, count] = b
        count = count + lax.shift_right_logical(codes[b], 2)

    def tile(chosen, first):
        states, logs, lengths = [], [], []
        for b in chosen:
            if first:
                states.append(jnp.maximum(x[:, pl.ds(first_line(b, group), group), :].reshape(species, LANES), FLOOR))
                length = jnp.where(listed[2, b] > 0, 1.0 / SUB, 1.0)
            else:
                states.append(result[b])
                length = 1.0 / SUB
            lengths.append(jnp.full((1, LANES), length, f32))
            logs.append(log_table[listed[1, b]])
        g = euler(
            jnp.concatenate(states, axis=1),
            jnp.concatenate(logs, axis=1),
            jnp.concatenate(lengths, axis=1),
            both[...],
        )
        for i, b in enumerate(chosen):
            piece = g[:, i * LANES : (i + 1) * LANES]
            result[b] = piece
            for k in range(0, species, 8):
                answer[pl.ds(k * blocks + b, 8, stride=blocks), :] = piece[k : k + 8]

    @pl.loop(0, blocks // TILE)
    def _(i):
        tile([i * TILE + j for j in range(TILE)], True)

    for _ in range(SUB - 1):

        @pl.loop(0, (count + TILE - 1) // TILE)
        def _(i):
            tile([listed[0, jnp.minimum(i * TILE + j, count - 1)] for j in range(TILE)], False)


    copy = pltpu.make_async_copy(answer, out, sem)
    copy.start()
    copy.wait()


def chemistry(x, info, start, log_table, both):
    species, blocks = both.shape[0] // 3, EDGE
    vmem = pl.BlockSpec(memory_space=pltpu.VMEM)
    smem = pl.BlockSpec(memory_space=pltpu.SMEM)
    return pl.pallas_call(
        chemistry_kernel,
        out_shape=pltpu.HBM((species * blocks, LANES), f32),
        in_specs=[smem, smem, vmem, vmem, vmem],
        out_specs=pl.BlockSpec(memory_space=pltpu.HBM),
        scratch_shapes=[
            pltpu.VMEM((blocks, species, LANES), f32),
            pltpu.VMEM((species * blocks, LANES), f32),
            pltpu.SMEM((3, blocks), jnp.int32),
            pltpu.SemaphoreType.DMA,
        ],
        compiler_params=pltpu.CompilerParams(vmem_limit_bytes=14 << 20),
        name="chemistry",
    )(info, start, x, log_table, both)


def place_kernel(firsts, parts, *rest):
    whole, stage, sems = rest[-3:]
    peers, group, blocks, _ = parts.shape
    count = blocks // len(firsts)
    rows = count * EDGE
    copies = []
    for k, first in enumerate(firsts):
        for side in (0, 1):
            for peer in range(side, peers, 2):
                for s in range(group):
                    at = pl.ds(s * rows + peer // 2, count, stride=EDGE)
                    stage[k, side, at, :] = parts[peer, s, k * count : (k + 1) * count]
            copy = pltpu.make_async_copy(
                stage.at[k, side].reshape(group, rows, LANES),
                whole.at[:, pl.ds(first, rows), pl.ds(side * LANES, LANES)],
                sems.at[2 * k + side],
            )
            copy.start()
            copies.append(copy)
    wait_all(copies)


def place_rows(parts, firsts, rows, *whole):
    peers, group, blocks, _ = parts.shape
    hbm = pl.BlockSpec(memory_space=pltpu.HBM)
    count = len(firsts)
    return pl.pallas_call(
        functools.partial(place_kernel, firsts),
        out_shape=pltpu.HBM((group, rows, 2 * LANES), f32),
        in_specs=[pl.BlockSpec(memory_space=pltpu.VMEM)] + [hbm] * len(whole),
        out_specs=hbm,
        scratch_shapes=[
            pltpu.VMEM((count, 2, group * blocks // count * EDGE, LANES), f32),
            pltpu.SemaphoreType.DMA((2 * count,)),
        ],
        input_output_aliases={1: 0} if whole else {},
        name="place",
    )(pltpu.with_memory_space_constraint(parts, pltpu.VMEM), *whole)


def per_device(
    concentrations,
    diffusion,
    courant_x,
    courant_y,
    log_rate,
    reactants,
    products,
    block_class,
    send_slot,
):
    group, rows, columns = concentrations.shape
    species, reactions = reactants.shape
    peers = species // group
    regions = lax.axis_size("region")
    up = [(i, (i + 1) % regions) for i in range(regions - 1)]
    down = [(j, i) for i, j in up]
    hbm = pl.BlockSpec(memory_space=pltpu.HBM)
    smem = pl.BlockSpec(memory_space=pltpu.SMEM)
    vmem = pl.BlockSpec(memory_space=pltpu.VMEM)
    places = rows // (2 * EDGE)
    lines = EDGE * group

    def buffers(slab_rows):
        row_buffer = pltpu.VMEM((slab_rows, group, columns), f32)
        return [pltpu.VMEM((10, slab_rows, LANES), f32), row_buffer, row_buffer]

    def in_hbm(*arrays):
        return [pltpu.with_memory_space_constraint(v, pltpu.HBM) for v in arrays]

    def in_vmem(*arrays):
        return [pltpu.with_memory_space_constraint(v, pltpu.VMEM) for v in arrays]

    fields = in_hbm(concentrations, courant_x, courant_y)
    slab_rows = rows // 2 + 2 * EDGE
    rim = pltpu.VMEM((group + 2, EDGE, columns), f32)
    last, leading = pl.pallas_call(
        rim_kernel,
        out_shape=(rim, rim),
        in_specs=[hbm] * 3,
        out_specs=(vmem, vmem),
        scratch_shapes=[pltpu.SemaphoreType.DMA((6,))],
        name="rims",
    )(*fields)
    before = lax.ppermute(last, "region", up)
    after = lax.ppermute(leading, "region", down)

    middle, token = pl.pallas_call(
        middle_kernel,
        grid=(1,),
        out_shape=(pltpu.HBM((peers, lines + EDGE, LANES), f32), pltpu.VMEM((EDGE, LANES), f32)),
        in_specs=[hbm] * 6,
        out_specs=(pl.BlockSpec((peers, lines + EDGE, LANES), lambda i: (0, 0, 0)), vmem),
        scratch_shapes=[
            pltpu.SMEM((group,), f32),
            pltpu.SMEM((2 * EDGE,), jnp.int32),
            pltpu.SMEM((2 * EDGE,), jnp.int32),
            pltpu.VMEM((2, group, slab_rows, LANES), f32),
            pltpu.VMEM((slab_rows, columns), f32),
            pltpu.VMEM((slab_rows, columns), f32),
            *buffers(slab_rows),
            pltpu.SemaphoreType.DMA((7,)),
        ],
        compiler_params=pltpu.CompilerParams(vmem_limit_bytes=16 << 20),
        name="middle",
    )(*in_hbm(diffusion, block_class, send_slot), *fields)

    turn = lax.ppermute(token, "region", [(k, k + 1) for k in range(0, regions - 1, 2)])
    first_part, turn = lax.optimization_barrier((middle, turn))
    place = jnp.stack([lax.axis_index("region"), jnp.int32(regions)]).astype(jnp.int32)
    slab_rows = rows // 4 + 2 * EDGE
    edges, *tables = pl.pallas_call(
        edge_kernel,
        grid=(1,),
        out_shape=(
            pltpu.HBM((peers, lines, LANES), f32),
            pltpu.VMEM((log_rate.shape[0], reactions, LANES), f32),
            pltpu.VMEM((3 * species, reactions), bf16),
        ),
        in_specs=[smem] + [hbm] * 4 + [vmem] * 3 + [
            pl.BlockSpec(v.shape, lambda i: (0, 0)) for v in (log_rate, reactants, products)
        ],
        out_specs=(pl.BlockSpec((peers, lines, LANES), lambda i: (0, 0, 0)), vmem, vmem),
        scratch_shapes=[
            pltpu.SMEM((group,), f32),
            pltpu.VMEM((2, 2, group, slab_rows, LANES), f32),
            pltpu.VMEM((2, slab_rows, columns), f32),
            pltpu.VMEM((2, slab_rows, columns), f32),
            *buffers(slab_rows),
            pltpu.SemaphoreType.DMA((17,)),
        ],
        compiler_params=pltpu.CompilerParams(vmem_limit_bytes=24 << 20),
        cost_estimate=pl.CostEstimate(
            flops=20 * 10**9, transcendentals=0, bytes_accessed=10 << 20
        ),
        name="edges",
    )(place, *in_hbm(diffusion), *fields, before, after, turn, *in_hbm(log_rate, reactants, products))

    mine = lax.axis_index("species").astype(jnp.int32)
    exchange = functools.partial(
        lax.all_to_all, axis_name="species", split_axis=0, concat_axis=0, tiled=True
    )
    info = None
    done = []
    order = jnp.arange(EDGE, dtype=jnp.int32)
    half = peers // 2
    for slab, source in (
        (first_part, order + half // 2),
        (edges, jnp.where(order < half // 2, order, order + half)),
    ):
        gathered = exchange(slab)
        if info is None:
            info = gathered[:, lines, : 2 * EDGE].astype(jnp.int32).reshape(-1)
        start = source * 2 * EDGE + mine
        reacted = chemistry(*in_vmem(gathered), info, start, *in_vmem(*tables))
        done.append(exchange(reacted.reshape(peers, group, EDGE, LANES)))
    quarter = rows // 4
    filled = place_rows(done[0], (quarter,), rows)
    return place_rows(done[1], (0, 3 * quarter), rows, filled)


def solution(mesh):
    in_specs = (
        P("species", "region", None),
        P("species"),
        P("region", None),
        P("region", None),
        P(),
        P(),
        P(),
        P(("region", "species")),
        P(("region", "species")),
    )
    out_specs = P("species", "region", None)
    return jax.shard_map(
        per_device, mesh=mesh, in_specs=in_specs, out_specs=out_specs, check_vma=False
    )
```

```python
import functools

import jax
import jax.numpy as jnp
from jax import lax
from jax.experimental import pallas as pl
from jax.experimental.pallas import tpu as pltpu
from jax.sharding import PartitionSpec as P

STEPS = 3
ITERS = 2
SUB = 2
FLOOR = 0.05
EDGE = 8
LANES = 128
TILE = 4
bf16 = jnp.bfloat16
f32 = jnp.float32


def median0(p, r):
    return jnp.maximum(jnp.minimum(p, r), jnp.minimum(jnp.maximum(p, r), 0.0))


def shift_left(pair, lane):
    a, b = (pltpu.roll(v, LANES - 1, 1) for v in pair)
    last = lane == LANES - 1
    return jnp.where(last, b, a), jnp.where(last, 0.0, b)


def shift_right(pair, first, lane):
    a, b = (pltpu.roll(v, 1, 1) for v in pair)
    head = lane == 0
    return jnp.where(head, first, a), jnp.where(head, a, b)


def halves(v):
    return v[:, :LANES], v[:, LANES:]


def face_coefs(a):
    size = jnp.abs(a)
    return 0.5 * size * (1.0 - size)


def store_coefs(cx, cy, coef):
    ax = 0.5 * (cx + jnp.concatenate([cx[1:], cx[:1]], axis=0))
    edge = lax.broadcasted_iota(jnp.int32, cy.shape, 1) == 2 * LANES - 1
    ay = 0.5 * (cy + jnp.where(edge, 0.0, jnp.concatenate([cy[:, 1:], cy[:, :1]], axis=1)))
    al = 0.5 * cy[:, :LANES]
    al_weight = jnp.where(al < 0.0, face_coefs(al), 0.0)
    pairs = [halves(v) for v in (ax, face_coefs(ax), ay, face_coefs(ay))]
    pairs.append((jnp.minimum(al, 0.0), al_weight))
    for k, pair in enumerate(pairs):
        coef[2 * k] = pair[0]
        coef[2 * k + 1] = pair[1]


def one_flux(q, qn, d, m, mn, a, e, nu):
    up = a >= 0.0
    return a * jnp.where(up, q, qn) + e * jnp.where(up, m, mn) - nu * d


def sweep(load, store, coef, nu, lo, hi, unroll, keep=None):
    group = nu.shape[0]
    lane = lax.broadcasted_iota(jnp.int32, (group, LANES), 1)

    def spread(which, row):
        return tuple(coef[2 * which + k, pl.ds(row, group, stride=0), :] for k in (0, 1))

    def x_flux(row, q, qn, d, m, mn):
        a, e = spread(0, row), spread(1, row)
        return tuple(one_flux(q[i], qn[i], d[i], m[i], mn[i], a[i], e[i], nu) for i in (0, 1))

    def diff(q, qn):
        return tuple(y - x for x, y in zip(q, qn))

    def limited(p, r):
        return tuple(median0(x, y) for x, y in zip(p, r))

    qa, qb, qc, qd = (load(lo + k) for k in (-2, -1, 0, 1))
    da, db, dc = diff(qa, qb), diff(qb, qc), diff(qc, qd)
    mb, mc = limited(da, db), limited(db, dc)
    behind = x_flux(lo - 1, qb, qc, db, mb, mc)

    def row_step(row, carry):
        q, qn, d, m, behind = carry
        qnn = load(row + 2)
        dn = diff(qn, qnn)
        mn = limited(d, dn)
        fx = x_flux(row, q, qn, d, m, mn)
        right = shift_left(q, lane)
        g = diff(q, right)
        s = limited(shift_right(g, q[0], lane), g)
        sn = shift_left(s, lane)
        a, e = spread(2, row), spread(3, row)
        fy = tuple(one_flux(q[i], right[i], g[i], s[i], sn[i], a[i], e[i], nu) for i in (0, 1))
        la, le = spread(4, row)
        fl = shift_right(fy, (la - nu) * q[0] + le * s[0], lane)
        new = tuple(q[i] - (fx[i] - behind[i]) - (fy[i] - fl[i]) for i in (0, 1))
        if keep is not None:
            scale = keep(row)
            new = tuple(v * scale for v in new)
        store(row, new)
        return qn, qnn, dn, mn, fx

    def steps(i, carry):
        for k in range(unroll):
            carry = row_step(lo + i * unroll + k, carry)
        return carry

    count = hi - lo
    carry = lax.fori_loop(0, count // unroll, steps, (qc, qd, dc, mc, behind))
    for row in range(lo + count // unroll * unroll, hi):
        carry = row_step(row, carry)


def buffer_access(buf):
    def load(row):
        return buf[row, :, :LANES], buf[row, :, LANES:]

    def store(row, pair):
        buf[row, :, :LANES] = pair[0]
        buf[row, :, LANES:] = pair[1]

    return load, store


def start_all(copies):
    for copy in copies:
        copy.start()


def wait_all(copies):
    for copy in copies:
        copy.wait()


def spread_species(diffuse, group):
    lane = lax.broadcasted_iota(jnp.int32, (group, LANES), 0)
    nu = jnp.zeros((group, LANES), f32)
    for k in range(group):
        nu = jnp.where(lane == k, diffuse[k], nu)
    return nu


def raw_access(block):
    group, rows, _ = block.shape[1:]
    flat = [block.at[k].reshape(group * rows, LANES) for k in (0, 1)]

    def load(row):
        return tuple(part[pl.ds(row, group, stride=rows), :] for part in flat)

    return load


def three_sweeps(load, store, coef, nu, one, two, rows, unrolls, keep=None):
    load1, store1 = buffer_access(one)
    load2, store2 = buffer_access(two)
    sweep(load, store1, coef, nu, 4, rows - 4, unrolls[0], keep)
    sweep(load1, store2, coef, nu, 6, rows - 6, unrolls[1], keep)
    sweep(load2, store, coef, nu, 8, rows - 8, unrolls[2])


def store_grouped(out, base, group):
    def store(row, pair):
        at = row - EDGE
        line = pl.multiple_of((base + lax.shift_right_logical(at, 3)) * group, group)
        peer = 2 * lax.bitwise_and(at, EDGE - 1)
        out[peer, pl.ds(line, group), :] = pair[0]
        out[peer + 1, pl.ds(line, group), :] = pair[1]

    return store


def rim_kernel(conc, cx, cy, last, leading, sems):
    group, total, _ = conc.shape
    copies = []

    def copy(src, dst):
        copies.append(pltpu.make_async_copy(src, dst, sems.at[len(copies)]))

    for rim, at in ((last, total - EDGE), (leading, 0)):
        copy(conc.at[:, pl.ds(at, EDGE)], rim.at[pl.ds(0, group)])
        copy(cx.at[pl.ds(at, EDGE)], rim.at[group])
        copy(cy.at[pl.ds(at, EDGE)], rim.at[group + 1])
    start_all(copies)
    wait_all(copies)


def middle_kernel(
    diffuse_in,
    classes_in,
    slots_in,
    conc,
    cx,
    cy,
    out,
    token,
    diffuse,
    classes,
    slots,
    raw,
    wx,
    wy,
    coef,
    one,
    two,
    sems,
):
    group, rows = raw.shape[1:3]
    total = conc.shape[1]
    first = total // 4 - EDGE
    pairs = [(cx.at[pl.ds(first, rows)], wx), (cy.at[pl.ds(first, rows)], wy)]
    pairs += [
        (conc.at[:, pl.ds(first, rows), pl.ds(k * LANES, LANES)], raw.at[k]) for k in (0, 1)
    ]
    pairs += [(diffuse_in, diffuse), (classes_in, classes), (slots_in, slots)]
    copies = [pltpu.make_async_copy(*pair, sems.at[k]) for k, pair in enumerate(pairs)]
    start_all(copies)
    wait_all(copies[4:7])
    nu = spread_species(diffuse, group)
    lane = lax.broadcasted_iota(jnp.int32, (EDGE, LANES), 1)
    codes = jnp.zeros((EDGE, LANES), f32)
    for k in range(classes.shape[0]):
        code = classes[k] + jnp.where(slots[k] >= 0, 4, 0)
        codes = jnp.where(lane == k, code.astype(f32), codes)
    for k in range(out.shape[0]):
        out[k, EDGE * group :, :] = codes
    wait_all(copies[:2])
    store_coefs(wx[...], wy[...], coef)
    wait_all(copies[2:4])
    three_sweeps(
        raw_access(raw), store_grouped(out, 0, group), coef, nu, one, two, rows, (18, 17, 16)
    )
    token[...] = codes


def edge_kernel(
    place,
    diffuse_in,
    conc,
    cx,
    cy,
    before,
    after,
    _token,
    log_rate,
    reactants,
    products,
    out,
    log_table,
    both,
    diffuse,
    raw,
    wx,
    wy,
    coef,
    one,
    two,
    sems,
):
    group, rows = raw.shape[2:4]
    total = conc.shape[1]
    own = rows - EDGE
    copies = []

    def copy(src, dst):
        copies.append(pltpu.make_async_copy(src, dst, sems.at[len(copies)]))

    copy(diffuse_in, diffuse)
    for slab, halo, own_first, own_at, halo_at in (
        (0, before, 0, EDGE, 0),
        (1, after, total - own, 0, own),
    ):
        for k, (wind, dst) in enumerate(((cx, wx), (cy, wy))):
            copy(wind.at[pl.ds(own_first, own)], dst.at[slab, pl.ds(own_at, own)])
            copy(halo.at[group + k], dst.at[slab, pl.ds(halo_at, EDGE)])
        for k in (0, 1):
            lanes = pl.ds(k * LANES, LANES)
            dst = raw.at[slab, k]
            copy(conc.at[:, pl.ds(own_first, own), lanes], dst.at[:, pl.ds(own_at, own)])
            copy(halo.at[pl.ds(0, group), :, lanes], dst.at[:, pl.ds(halo_at, EDGE)])
    start_all(copies)
    table_kernel(log_rate, reactants, products, log_table, both)
    wait_all(copies)
    nu = spread_species(diffuse, group)

    @pl.loop(0, 2)
    def _(slab):
        store_coefs(wx[slab], wy[slab], coef)
        open_top = jnp.logical_and(slab == 0, place[0] == 0)
        open_end = jnp.logical_and(slab == 1, place[0] == place[1] - 1)

        def keep(row):
            outside = jnp.logical_or(
                jnp.logical_and(open_top, row < EDGE), jnp.logical_and(open_end, row >= own)
            )
            return jnp.where(outside, 0.0, 1.0)

        three_sweeps(
            raw_access(raw.at[slab]),
            store_grouped(out, slab * 4, group),
            coef,
            nu,
            one,
            two,
            rows,
            (10, 12, 16),
            keep,
        )


def split(x):
    high = x.astype(bf16)
    return high, (x - high.astype(f32)).astype(bf16)


def table_dot(table, x):
    high, low = split(x)
    return jnp.dot(table, high, preferred_element_type=f32) + jnp.dot(
        table, low, preferred_element_type=f32
    )


def blocks_dot(blocks, x):
    size = x.shape[0]
    high, low = split(x)
    parts = [blocks[:, k : k + size] for k in range(0, blocks.shape[1], size)]
    return jnp.concatenate(
        [
            jnp.dot(part, high, preferred_element_type=f32)
            + jnp.dot(part, low, preferred_element_type=f32)
            for part in parts
        ],
        axis=0,
    )


def euler(state, logs, step, both):
    species = state.shape[0]
    reac = both[2 * species :]
    both = both[: 2 * species]
    g = state
    for _ in range(ITERS):
        rates = jnp.exp(logs + blocks_dot(reac, jnp.log(g)))
        made_lost = table_dot(both, rates)
        g = (state + step * made_lost[:species]) / (1.0 + step * made_lost[species:] / g)
    return g


def first_line(block, group):
    return block * group if isinstance(block, int) else pl.multiple_of(block * group, group)


def table_kernel(log_rate, reactants, products, log_table, both):
    species, reactions = reactants.shape
    reactant = reactants[...].astype(f32)
    both[:species] = products[...].astype(f32).T.astype(bf16)
    both[species : 2 * species] = reactant.astype(bf16)
    for k in range(0, reactions, species):
        both[2 * species :, k : k + species] = reactant[:, k : k + species].T.astype(bf16)
    for k in range(log_rate.shape[0]):
        log_table[k] = jnp.broadcast_to(log_rate[k : k + 1, :], (LANES, reactions)).T


def first_line(block, group):
    return block * group if isinstance(block, int) else pl.multiple_of(block * group, group)


def table_kernel(log_rate, reactants, products, log_table, both):
    species, reactions = reactants.shape
    reactant = reactants[...].astype(f32)
    both[:species] = products[...].astype(f32).T.astype(bf16)
    both[species : 2 * species] = reactant.astype(bf16)
    for k in range(0, reactions, species):
        both[2 * species :, k : k + species] = reactant[:, k : k + species].T.astype(bf16)
    for k in range(log_rate.shape[0]):
        log_table[k] = jnp.broadcast_to(log_rate[k : k + 1, :], (LANES, reactions)).T


def tables_of(log_rate, reactants, products):
    species, reactions = reactants.shape
    classes = log_rate.shape[0]
    vmem = pl.BlockSpec(memory_space=pltpu.VMEM)
    return pl.pallas_call(
        table_kernel,
        grid=(1,),
        out_shape=[
            pltpu.VMEM((classes, reactions, LANES), f32),
            pltpu.VMEM((3 * species, reactions), bf16),
        ],
        in_specs=[
            pl.BlockSpec((classes, reactions), lambda i: (0, 0)),
            pl.BlockSpec((species, reactions), lambda i: (0, 0)),
            pl.BlockSpec((reactions, species), lambda i: (0, 0)),
        ],
        out_specs=[vmem] * 3,
        compiler_params=pltpu.CompilerParams(vmem_limit_bytes=12 << 20),
        name="tables",
    )(log_rate, reactants, products)


def code_class(code):
    return sum((code >= float(k)).astype(jnp.int32) for k in (5, 6, 7))


def chemistry_kernel(
    sources, mine, x_in, coded, log_table, both, out, x, codes, result, answer, listed, sems
):
    peers, lines, _ = x.shape
    blocks = EDGE
    group = lines // blocks
    species = peers * group
    size = TILE * group

    def part(i):
        at = pl.ds(first_line(i, size), size)
        return pltpu.make_async_copy(x_in.at[:, at, :], x.at[:, at, :], sems.at[i])

    copies = []
    for first, count, at in sources:
        copies.append(
            pltpu.make_async_copy(
                coded.at[pl.ds(first, count), pl.ds(lines, EDGE), :],
                codes.at[pl.ds(at, count)],
                sems.at[blocks // TILE + len(copies)],
            )
        )
    start_all(copies + [part(i) for i in range(blocks // TILE)])
    wait_all(copies)
    count = jnp.int32(0)
    for b in range(blocks):
        code = codes[b, 0, mine[0]]
        stiff = (code >= 4.0).astype(jnp.int32)
        lower = sum((code >= float(k)).astype(jnp.int32) for k in (1, 2, 3))
        listed[1, b] = jnp.where(code >= 4.0, code_class(code), lower)
        listed[2, b] = stiff
        listed[0, count] = b
        count = count + stiff

    def tile(chosen, first):
        states, logs, lengths = [], [], []
        for b in chosen:
            if first:
                states.append(jnp.maximum(x[:, pl.ds(first_line(b, group), group), :].reshape(species, LANES), FLOOR))
                length = jnp.where(listed[2, b] > 0, 1.0 / SUB, 1.0)
            else:
                states.append(result[b])
                length = 1.0 / SUB
            lengths.append(jnp.full((1, LANES), length, f32))
            logs.append(log_table[listed[1, b]])
        g = euler(
            jnp.concatenate(states, axis=1),
            jnp.concatenate(logs, axis=1),
            jnp.concatenate(lengths, axis=1),
            both[...],
        )
        for i, b in enumerate(chosen):
            piece = g[:, i * LANES : (i + 1) * LANES]
            result[b] = piece
            for k in range(0, species, 8):
                answer[pl.ds(k * blocks + b, 8, stride=blocks), :] = piece[k : k + 8]

    @pl.loop(0, blocks // TILE)
    def _(i):
        part(i).wait()
        tile([i * TILE + j for j in range(TILE)], True)

    for _ in range(SUB - 1):

        @pl.loop(0, (count + TILE - 1) // TILE)
        def _(i):
            tile([listed[0, jnp.minimum(i * TILE + j, count - 1)] for j in range(TILE)], False)


    copy = pltpu.make_async_copy(answer, out, sems.at[0])
    copy.start()
    copy.wait()


def chemistry(x, coded, sources, mine, log_table, both):
    peers = x.shape[0]
    species, blocks = both.shape[0] // 3, EDGE
    vmem = pl.BlockSpec(memory_space=pltpu.VMEM)
    smem = pl.BlockSpec(memory_space=pltpu.SMEM)
    hbm = pl.BlockSpec(memory_space=pltpu.HBM)
    return pl.pallas_call(
        functools.partial(chemistry_kernel, sources),
        out_shape=pltpu.HBM((species * blocks, LANES), f32),
        in_specs=[smem, hbm, hbm, vmem, vmem],
        out_specs=hbm,
        scratch_shapes=[
            pltpu.VMEM((peers, species // peers * blocks, LANES), f32),
            pltpu.SMEM((blocks, EDGE, LANES), f32),
            pltpu.VMEM((blocks, species, LANES), f32),
            pltpu.VMEM((species * blocks, LANES), f32),
            pltpu.SMEM((3, blocks), jnp.int32),
            pltpu.SemaphoreType.DMA((blocks // TILE + len(sources),)),
        ],
        compiler_params=pltpu.CompilerParams(vmem_limit_bytes=14 << 20),
        name="chemistry",
    )(mine, x, coded, log_table, both)


def place_kernel(firsts, parts, *rest):
    whole, stage, sems = rest[-3:]
    peers, group, blocks, _ = parts.shape
    count = blocks // len(firsts)
    rows = count * EDGE
    copies = []
    for k, first in enumerate(firsts):
        for side in (0, 1):
            for peer in range(side, peers, 2):
                for s in range(group):
                    at = pl.ds(s * rows + peer // 2, count, stride=EDGE)
                    stage[k, side, at, :] = parts[peer, s, k * count : (k + 1) * count]
            copy = pltpu.make_async_copy(
                stage.at[k, side].reshape(group, rows, LANES),
                whole.at[:, pl.ds(first, rows), pl.ds(side * LANES, LANES)],
                sems.at[2 * k + side],
            )
            copy.start()
            copies.append(copy)
    wait_all(copies)


def place_rows(parts, firsts, rows, *whole):
    peers, group, blocks, _ = parts.shape
    hbm = pl.BlockSpec(memory_space=pltpu.HBM)
    count = len(firsts)
    return pl.pallas_call(
        functools.partial(place_kernel, firsts),
        out_shape=pltpu.HBM((group, rows, 2 * LANES), f32),
        in_specs=[pl.BlockSpec(memory_space=pltpu.VMEM)] + [hbm] * len(whole),
        out_specs=hbm,
        scratch_shapes=[
            pltpu.VMEM((count, 2, group * blocks // count * EDGE, LANES), f32),
            pltpu.SemaphoreType.DMA((2 * count,)),
        ],
        input_output_aliases={1: 0} if whole else {},
        name="place",
    )(pltpu.with_memory_space_constraint(parts, pltpu.VMEM), *whole)


def per_device(
    concentrations,
    diffusion,
    courant_x,
    courant_y,
    log_rate,
    reactants,
    products,
    block_class,
    send_slot,
):
    group, rows, columns = concentrations.shape
    species, reactions = reactants.shape
    peers = species // group
    regions = lax.axis_size("region")
    up = [(i, (i + 1) % regions) for i in range(regions - 1)]
    down = [(j, i) for i, j in up]
    hbm = pl.BlockSpec(memory_space=pltpu.HBM)
    smem = pl.BlockSpec(memory_space=pltpu.SMEM)
    vmem = pl.BlockSpec(memory_space=pltpu.VMEM)
    places = rows // (2 * EDGE)
    lines = EDGE * group

    def buffers(slab_rows):
        row_buffer = pltpu.VMEM((slab_rows, group, columns), f32)
        return [pltpu.VMEM((10, slab_rows, LANES), f32), row_buffer, row_buffer]

    def in_hbm(*arrays):
        return [pltpu.with_memory_space_constraint(v, pltpu.HBM) for v in arrays]

    def in_vmem(*arrays):
        return [pltpu.with_memory_space_constraint(v, pltpu.VMEM) for v in arrays]

    fields = in_hbm(concentrations, courant_x, courant_y)
    slab_rows = rows // 2 + 2 * EDGE
    rim = pltpu.VMEM((group + 2, EDGE, columns), f32)
    last, leading = pl.pallas_call(
        rim_kernel,
        out_shape=(rim, rim),
        in_specs=[hbm] * 3,
        out_specs=(vmem, vmem),
        scratch_shapes=[pltpu.SemaphoreType.DMA((6,))],
        name="rims",
    )(*fields)
    before = lax.ppermute(last, "region", up)
    after = lax.ppermute(leading, "region", down)

    middle, token = pl.pallas_call(
        middle_kernel,
        grid=(1,),
        out_shape=(pltpu.HBM((peers, lines + EDGE, LANES), f32), pltpu.VMEM((EDGE, LANES), f32)),
        in_specs=[hbm] * 6,
        out_specs=(pl.BlockSpec((peers, lines + EDGE, LANES), lambda i: (0, 0, 0)), vmem),
        scratch_shapes=[
            pltpu.SMEM((group,), f32),
            pltpu.SMEM((2 * EDGE,), jnp.int32),
            pltpu.SMEM((2 * EDGE,), jnp.int32),
            pltpu.VMEM((2, group, slab_rows, LANES), f32),
            pltpu.VMEM((slab_rows, columns), f32),
            pltpu.VMEM((slab_rows, columns), f32),
            *buffers(slab_rows),
            pltpu.SemaphoreType.DMA((7,)),
        ],
        compiler_params=pltpu.CompilerParams(vmem_limit_bytes=16 << 20),
        name="middle",
    )(*in_hbm(diffusion, block_class, send_slot), *fields)

    turn = lax.ppermute(token, "region", [(k, k + 1) for k in range(0, regions - 1, 2)])
    first_part, turn = lax.optimization_barrier((middle, turn))
    place = jnp.stack([lax.axis_index("region"), jnp.int32(regions)]).astype(jnp.int32)
    slab_rows = rows // 4 + 2 * EDGE
    edges, *tables = pl.pallas_call(
        edge_kernel,
        grid=(1,),
        out_shape=(
            pltpu.HBM((peers, lines, LANES), f32),
            pltpu.VMEM((log_rate.shape[0], reactions, LANES), f32),
            pltpu.VMEM((3 * species, reactions), bf16),
        ),
        in_specs=[smem] + [hbm] * 4 + [vmem] * 3 + [
            pl.BlockSpec(v.shape, lambda i: (0, 0)) for v in (log_rate, reactants, products)
        ],
        out_specs=(pl.BlockSpec((peers, lines, LANES), lambda i: (0, 0, 0)), vmem, vmem),
        scratch_shapes=[
            pltpu.SMEM((group,), f32),
            pltpu.VMEM((2, 2, group, slab_rows, LANES), f32),
            pltpu.VMEM((2, slab_rows, columns), f32),
            pltpu.VMEM((2, slab_rows, columns), f32),
            *buffers(slab_rows),
            pltpu.SemaphoreType.DMA((17,)),
        ],
        compiler_params=pltpu.CompilerParams(vmem_limit_bytes=24 << 20),
        cost_estimate=pl.CostEstimate(
            flops=20 * 10**9, transcendentals=0, bytes_accessed=10 << 20
        ),
        name="edges",
    )(place, *in_hbm(diffusion), *fields, before, after, turn, *in_hbm(log_rate, reactants, products))

    mine = lax.axis_index("species").astype(jnp.int32).reshape(1)
    exchange = functools.partial(
        lax.all_to_all, axis_name="species", split_axis=0, concat_axis=0, tiled=True
    )
    done = []
    coded = None
    half = peers // 2
    quarter = half // 2
    for slab, sources in (
        (first_part, ((quarter, half, 0),)),
        (edges, ((0, quarter, 0), (half + quarter, quarter, quarter))),
    ):
        (gathered,) = in_hbm(exchange(slab))
        coded = gathered if coded is None else coded
        reacted = chemistry(gathered, coded, sources, mine, *in_vmem(*tables))
        done.append(exchange(reacted.reshape(peers, group, EDGE, LANES)))
    quarter = rows // 4
    filled = place_rows(done[0], (quarter,), rows)
    return place_rows(done[1], (0, 3 * quarter), rows, filled)


def solution(mesh):
    in_specs = (
        P("species", "region", None),
        P("species"),
        P("region", None),
        P("region", None),
        P(),
        P(),
        P(),
        P(("region", "species")),
        P(("region", "species")),
    )
    out_specs = P("species", "region", None)
    return jax.shard_map(
        per_device, mesh=mesh, in_specs=in_specs, out_specs=out_specs, check_vma=False
    )
```

```python
import functools

import jax
import jax.numpy as jnp
from jax import lax
from jax.experimental import pallas as pl
from jax.experimental.pallas import tpu as pltpu
from jax.sharding import PartitionSpec as P

STEPS = 3
ITERS = 2
SUB = 2
FLOOR = 0.05
EDGE = 8
LANES = 128
TILE = 4
bf16 = jnp.bfloat16
f32 = jnp.float32


def median0(p, r):
    return jnp.maximum(jnp.minimum(p, r), jnp.minimum(jnp.maximum(p, r), 0.0))


def shift_left(pair, lane):
    a, b = (pltpu.roll(v, LANES - 1, 1) for v in pair)
    last = lane == LANES - 1
    return jnp.where(last, b, a), jnp.where(last, 0.0, b)


def shift_right(pair, first, lane):
    a, b = (pltpu.roll(v, 1, 1) for v in pair)
    head = lane == 0
    return jnp.where(head, first, a), jnp.where(head, a, b)


def halves(v):
    return v[:, :LANES], v[:, LANES:]


def face_coefs(a):
    size = jnp.abs(a)
    return 0.5 * size * (1.0 - size)


def store_coefs(cx, cy, coef):
    ax = 0.5 * (cx + jnp.concatenate([cx[1:], cx[:1]], axis=0))
    edge = lax.broadcasted_iota(jnp.int32, cy.shape, 1) == 2 * LANES - 1
    ay = 0.5 * (cy + jnp.where(edge, 0.0, jnp.concatenate([cy[:, 1:], cy[:, :1]], axis=1)))
    al = 0.5 * cy[:, :LANES]
    al_weight = jnp.where(al < 0.0, face_coefs(al), 0.0)
    pairs = [halves(v) for v in (ax, face_coefs(ax), ay, face_coefs(ay))]
    pairs.append((jnp.minimum(al, 0.0), al_weight))
    for k, pair in enumerate(pairs):
        coef[2 * k] = pair[0]
        coef[2 * k + 1] = pair[1]


def one_flux(q, qn, d, m, mn, a, e, nu):
    up = a >= 0.0
    return a * jnp.where(up, q, qn) + e * jnp.where(up, m, mn) - nu * d


def sweep(load, store, coef, nu, lo, hi, unroll, keep=None):
    group = nu.shape[0]
    lane = lax.broadcasted_iota(jnp.int32, (group, LANES), 1)

    def spread(which, row):
        return tuple(coef[2 * which + k, pl.ds(row, group, stride=0), :] for k in (0, 1))

    def x_flux(row, q, qn, d, m, mn):
        a, e = spread(0, row), spread(1, row)
        return tuple(one_flux(q[i], qn[i], d[i], m[i], mn[i], a[i], e[i], nu) for i in (0, 1))

    def diff(q, qn):
        return tuple(y - x for x, y in zip(q, qn))

    def limited(p, r):
        return tuple(median0(x, y) for x, y in zip(p, r))

    qa, qb, qc, qd = (load(lo + k) for k in (-2, -1, 0, 1))
    da, db, dc = diff(qa, qb), diff(qb, qc), diff(qc, qd)
    mb, mc = limited(da, db), limited(db, dc)
    behind = x_flux(lo - 1, qb, qc, db, mb, mc)

    def row_step(row, carry):
        q, qn, d, m, behind = carry
        qnn = load(row + 2)
        dn = diff(qn, qnn)
        mn = limited(d, dn)
        fx = x_flux(row, q, qn, d, m, mn)
        right = shift_left(q, lane)
        g = diff(q, right)
        s = limited(shift_right(g, q[0], lane), g)
        sn = shift_left(s, lane)
        a, e = spread(2, row), spread(3, row)
        fy = tuple(one_flux(q[i], right[i], g[i], s[i], sn[i], a[i], e[i], nu) for i in (0, 1))
        la, le = spread(4, row)
        fl = shift_right(fy, (la - nu) * q[0] + le * s[0], lane)
        new = tuple(q[i] - (fx[i] - behind[i]) - (fy[i] - fl[i]) for i in (0, 1))
        if keep is not None:
            scale = keep(row)
            new = tuple(v * scale for v in new)
        store(row, new)
        return qn, qnn, dn, mn, fx

    def steps(i, carry):
        for k in range(unroll):
            carry = row_step(lo + i * unroll + k, carry)
        return carry

    count = hi - lo
    carry = lax.fori_loop(0, count // unroll, steps, (qc, qd, dc, mc, behind))
    for row in range(lo + count // unroll * unroll, hi):
        carry = row_step(row, carry)


def buffer_access(buf):
    def load(row):
        return buf[row, :, :LANES], buf[row, :, LANES:]

    def store(row, pair):
        buf[row, :, :LANES] = pair[0]
        buf[row, :, LANES:] = pair[1]

    return load, store


def start_all(copies):
    for copy in copies:
        copy.start()


def wait_all(copies):
    for copy in copies:
        copy.wait()


def spread_species(diffuse, group):
    lane = lax.broadcasted_iota(jnp.int32, (group, LANES), 0)
    nu = jnp.zeros((group, LANES), f32)
    for k in range(group):
        nu = jnp.where(lane == k, diffuse[k], nu)
    return nu


def raw_access(block):
    group, rows, _ = block.shape[1:]
    flat = [block.at[k].reshape(group * rows, LANES) for k in (0, 1)]

    def load(row):
        return tuple(part[pl.ds(row, group, stride=rows), :] for part in flat)

    return load


def three_sweeps(load, store, coef, nu, one, two, rows, unrolls, keep=None):
    load1, store1 = buffer_access(one)
    load2, store2 = buffer_access(two)
    sweep(load, store1, coef, nu, 4, rows - 4, unrolls[0], keep)
    sweep(load1, store2, coef, nu, 6, rows - 6, unrolls[1], keep)
    sweep(load2, store, coef, nu, 8, rows - 8, unrolls[2])


def store_grouped(out, base, group):
    def store(row, pair):
        at = row - EDGE
        line = pl.multiple_of((base + lax.shift_right_logical(at, 3)) * group, group)
        peer = 2 * lax.bitwise_and(at, EDGE - 1)
        out[peer, pl.ds(line, group), :] = pair[0]
        out[peer + 1, pl.ds(line, group), :] = pair[1]

    return store


def rim_kernel(conc, cx, cy, last, leading, sems):
    group, total, _ = conc.shape
    copies = []

    def copy(src, dst):
        copies.append(pltpu.make_async_copy(src, dst, sems.at[len(copies)]))

    for rim, at in ((last, total - EDGE), (leading, 0)):
        copy(conc.at[:, pl.ds(at, EDGE)], rim.at[pl.ds(0, group)])
        copy(cx.at[pl.ds(at, EDGE)], rim.at[group])
        copy(cy.at[pl.ds(at, EDGE)], rim.at[group + 1])
    start_all(copies)
    wait_all(copies)


def middle_kernel(
    diffuse_in,
    classes_in,
    slots_in,
    conc,
    cx,
    cy,
    out,
    token,
    diffuse,
    classes,
    slots,
    raw,
    wx,
    wy,
    coef,
    one,
    two,
    sems,
):
    group, rows = raw.shape[1:3]
    total = conc.shape[1]
    first = total // 4 - EDGE
    pairs = [(cx.at[pl.ds(first, rows)], wx), (cy.at[pl.ds(first, rows)], wy)]
    pairs += [
        (conc.at[:, pl.ds(first, rows), pl.ds(k * LANES, LANES)], raw.at[k]) for k in (0, 1)
    ]
    pairs += [(diffuse_in, diffuse), (classes_in, classes), (slots_in, slots)]
    copies = [pltpu.make_async_copy(*pair, sems.at[k]) for k, pair in enumerate(pairs)]
    start_all(copies)
    wait_all(copies[4:7])
    nu = spread_species(diffuse, group)
    lane = lax.broadcasted_iota(jnp.int32, (EDGE, LANES), 1)
    codes = jnp.zeros((EDGE, LANES), f32)
    for k in range(classes.shape[0]):
        code = classes[k] + jnp.where(slots[k] >= 0, 4, 0)
        codes = jnp.where(lane == k, code.astype(f32), codes)
    for k in range(out.shape[0]):
        out[k, EDGE * group :, :] = codes
    wait_all(copies[:2])
    store_coefs(wx[...], wy[...], coef)
    wait_all(copies[2:4])
    three_sweeps(
        raw_access(raw), store_grouped(out, 0, group), coef, nu, one, two, rows, (18, 17, 16)
    )
    token[...] = codes


def edge_kernel(
    place,
    diffuse_in,
    conc,
    cx,
    cy,
    before,
    after,
    _token,
    log_rate,
    reactants,
    products,
    early_log_table,
    early_both,
    out,
    log_table,
    both,
    diffuse,
    raw,
    wx,
    wy,
    coef,
    one,
    two,
    sems,
):
    group, rows = raw.shape[2:4]
    total = conc.shape[1]
    own = rows - EDGE
    copies = []

    def copy(src, dst):
        copies.append(pltpu.make_async_copy(src, dst, sems.at[len(copies)]))

    copy(diffuse_in, diffuse)
    for slab, halo, own_first, own_at, halo_at in (
        (0, before, 0, EDGE, 0),
        (1, after, total - own, 0, own),
    ):
        for k, (wind, dst) in enumerate(((cx, wx), (cy, wy))):
            copy(wind.at[pl.ds(own_first, own)], dst.at[slab, pl.ds(own_at, own)])
            copy(halo.at[group + k], dst.at[slab, pl.ds(halo_at, EDGE)])
        for k in (0, 1):
            lanes = pl.ds(k * LANES, LANES)
            dst = raw.at[slab, k]
            copy(conc.at[:, pl.ds(own_first, own), lanes], dst.at[:, pl.ds(own_at, own)])
            copy(halo.at[pl.ds(0, group), :, lanes], dst.at[:, pl.ds(halo_at, EDGE)])
    start_all(copies)

    @pl.when(lax.rem(place[0], 2) == 1)
    def _():
        table_kernel(log_rate, reactants, products, log_table, both)

    @pl.when(lax.rem(place[0], 2) == 0)
    def _():
        early = [
            pltpu.make_async_copy(src, dst, sems.at[len(copies) + k])
            for k, (src, dst) in enumerate(((early_log_table, log_table), (early_both, both)))
        ]
        start_all(early)
        wait_all(early)

    wait_all(copies)
    nu = spread_species(diffuse, group)

    @pl.loop(0, 2)
    def _(slab):
        store_coefs(wx[slab], wy[slab], coef)
        open_top = jnp.logical_and(slab == 0, place[0] == 0)
        open_end = jnp.logical_and(slab == 1, place[0] == place[1] - 1)

        def keep(row):
            outside = jnp.logical_or(
                jnp.logical_and(open_top, row < EDGE), jnp.logical_and(open_end, row >= own)
            )
            return jnp.where(outside, 0.0, 1.0)

        three_sweeps(
            raw_access(raw.at[slab]),
            store_grouped(out, slab * 4, group),
            coef,
            nu,
            one,
            two,
            rows,
            (10, 12, 16),
            keep,
        )


def split(x):
    high = x.astype(bf16)
    return high, (x - high.astype(f32)).astype(bf16)


def table_dot(table, x):
    high, low = split(x)
    return jnp.dot(table, high, preferred_element_type=f32) + jnp.dot(
        table, low, preferred_element_type=f32
    )


def blocks_dot(blocks, x):
    size = x.shape[0]
    high, low = split(x)
    parts = [blocks[:, k : k + size] for k in range(0, blocks.shape[1], size)]
    return jnp.concatenate(
        [
            jnp.dot(part, high, preferred_element_type=f32)
            + jnp.dot(part, low, preferred_element_type=f32)
            for part in parts
        ],
        axis=0,
    )


def euler(state, logs, step, both):
    species = state.shape[0]
    reac = both[2 * species :]
    both = both[: 2 * species]
    g = state
    for _ in range(ITERS):
        rates = jnp.exp(logs + blocks_dot(reac, jnp.log(g)))
        made_lost = table_dot(both, rates)
        g = (state + step * made_lost[:species]) / (1.0 + step * made_lost[species:] / g)
    return g


def turn_kernel(place, _turn, log_rate_in, reactants_in, products_in, log_table, both, *rest):
    buffers, made, sems = rest[:3], rest[3:5], rest[5]

    @pl.when(lax.rem(place[0], 2) == 0)
    def _():
        copies = [
            pltpu.make_async_copy(src, dst, sems.at[k])
            for k, (src, dst) in enumerate(
                zip((log_rate_in, reactants_in, products_in), buffers)
            )
        ]
        start_all(copies)
        wait_all(copies)
        table_kernel(*buffers, *made)
        copies = [
            pltpu.make_async_copy(src, dst, sems.at[k])
            for k, (src, dst) in enumerate(zip(made, (log_table, both)))
        ]
        start_all(copies)
        wait_all(copies)


def first_line(block, group):
    return block * group if isinstance(block, int) else pl.multiple_of(block * group, group)


def table_kernel(log_rate, reactants, products, log_table, both):
    species, reactions = reactants.shape
    reactant = reactants[...].astype(f32)
    both[:species] = products[...].astype(f32).T.astype(bf16)
    both[species : 2 * species] = reactant.astype(bf16)
    for k in range(0, reactions, species):
        both[2 * species :, k : k + species] = reactant[:, k : k + species].T.astype(bf16)
    for k in range(log_rate.shape[0]):
        log_table[k] = jnp.broadcast_to(log_rate[k : k + 1, :], (LANES, reactions)).T


def turn_kernel(place, _turn, log_rate_in, reactants_in, products_in, log_table, both, *rest):
    buffers, made, sems = rest[:3], rest[3:5], rest[5]

    @pl.when(lax.rem(place[0], 2) == 0)
    def _():
        copies = [
            pltpu.make_async_copy(src, dst, sems.at[k])
            for k, (src, dst) in enumerate(
                zip((log_rate_in, reactants_in, products_in), buffers)
            )
        ]
        start_all(copies)
        wait_all(copies)
        table_kernel(*buffers, *made)
        copies = [
            pltpu.make_async_copy(src, dst, sems.at[k])
            for k, (src, dst) in enumerate(zip(made, (log_table, both)))
        ]
        start_all(copies)
        wait_all(copies)


def first_line(block, group):
    return block * group if isinstance(block, int) else pl.multiple_of(block * group, group)


def table_kernel(log_rate, reactants, products, log_table, both):
    species, reactions = reactants.shape
    reactant = reactants[...].astype(f32)
    both[:species] = products[...].astype(f32).T.astype(bf16)
    both[species : 2 * species] = reactant.astype(bf16)
    for k in range(0, reactions, species):
        both[2 * species :, k : k + species] = reactant[:, k : k + species].T.astype(bf16)
    for k in range(log_rate.shape[0]):
        log_table[k] = jnp.broadcast_to(log_rate[k : k + 1, :], (LANES, reactions)).T


def tables_of(log_rate, reactants, products):
    species, reactions = reactants.shape
    classes = log_rate.shape[0]
    vmem = pl.BlockSpec(memory_space=pltpu.VMEM)
    return pl.pallas_call(
        table_kernel,
        grid=(1,),
        out_shape=[
            pltpu.VMEM((classes, reactions, LANES), f32),
            pltpu.VMEM((3 * species, reactions), bf16),
        ],
        in_specs=[
            pl.BlockSpec((classes, reactions), lambda i: (0, 0)),
            pl.BlockSpec((species, reactions), lambda i: (0, 0)),
            pl.BlockSpec((reactions, species), lambda i: (0, 0)),
        ],
        out_specs=[vmem] * 3,
        compiler_params=pltpu.CompilerParams(vmem_limit_bytes=12 << 20),
        name="tables",
    )(log_rate, reactants, products)


def code_class(code):
    return sum((code >= float(k)).astype(jnp.int32) for k in (5, 6, 7))


def chemistry_kernel(
    sources, mine, x_in, coded, log_table, both, out, x, codes, result, answer, listed, sems
):
    peers, lines, _ = x.shape
    blocks = EDGE
    group = lines // blocks
    species = peers * group
    size = TILE * group

    def part(i):
        at = pl.ds(first_line(i, size), size)
        return pltpu.make_async_copy(x_in.at[:, at, :], x.at[:, at, :], sems.at[i])

    copies = []
    for first, count, at in sources:
        copies.append(
            pltpu.make_async_copy(
                coded.at[pl.ds(first, count), pl.ds(lines, EDGE), :],
                codes.at[pl.ds(at, count)],
                sems.at[blocks // TILE + len(copies)],
            )
        )
    start_all(copies + [part(i) for i in range(blocks // TILE)])
    wait_all(copies)
    count = jnp.int32(0)
    for b in range(blocks):
        code = codes[b, 0, mine[0]]
        stiff = (code >= 4.0).astype(jnp.int32)
        lower = sum((code >= float(k)).astype(jnp.int32) for k in (1, 2, 3))
        listed[1, b] = jnp.where(code >= 4.0, code_class(code), lower)
        listed[2, b] = stiff
        listed[0, count] = b
        count = count + stiff

    def tile(chosen, first):
        states, logs, lengths = [], [], []
        for b in chosen:
            if first:
                states.append(jnp.maximum(x[:, pl.ds(first_line(b, group), group), :].reshape(species, LANES), FLOOR))
                length = jnp.where(listed[2, b] > 0, 1.0 / SUB, 1.0)
            else:
                states.append(result[b])
                length = 1.0 / SUB
            lengths.append(jnp.full((1, LANES), length, f32))
            logs.append(log_table[listed[1, b]])
        g = euler(
            jnp.concatenate(states, axis=1),
            jnp.concatenate(logs, axis=1),
            jnp.concatenate(lengths, axis=1),
            both[...],
        )
        for i, b in enumerate(chosen):
            piece = g[:, i * LANES : (i + 1) * LANES]
            result[b] = piece
            for k in range(0, species, 8):
                answer[pl.ds(k * blocks + b, 8, stride=blocks), :] = piece[k : k + 8]

    @pl.loop(0, blocks // TILE)
    def _(i):
        part(i).wait()
        tile([i * TILE + j for j in range(TILE)], True)

    for _ in range(SUB - 1):

        @pl.loop(0, (count + TILE - 1) // TILE)
        def _(i):
            tile([listed[0, jnp.minimum(i * TILE + j, count - 1)] for j in range(TILE)], False)


    copy = pltpu.make_async_copy(answer, out, sems.at[0])
    copy.start()
    copy.wait()


def chemistry(x, coded, sources, mine, log_table, both):
    peers = x.shape[0]
    species, blocks = both.shape[0] // 3, EDGE
    vmem = pl.BlockSpec(memory_space=pltpu.VMEM)
    smem = pl.BlockSpec(memory_space=pltpu.SMEM)
    hbm = pl.BlockSpec(memory_space=pltpu.HBM)
    return pl.pallas_call(
        functools.partial(chemistry_kernel, sources),
        out_shape=pltpu.HBM((species * blocks, LANES), f32),
        in_specs=[smem, hbm, hbm, vmem, vmem],
        out_specs=hbm,
        scratch_shapes=[
            pltpu.VMEM((peers, species // peers * blocks, LANES), f32),
            pltpu.SMEM((blocks, EDGE, LANES), f32),
            pltpu.VMEM((blocks, species, LANES), f32),
            pltpu.VMEM((species * blocks, LANES), f32),
            pltpu.SMEM((3, blocks), jnp.int32),
            pltpu.SemaphoreType.DMA((blocks // TILE + len(sources),)),
        ],
        compiler_params=pltpu.CompilerParams(vmem_limit_bytes=14 << 20),
        name="chemistry",
    )(mine, x, coded, log_table, both)


def place_kernel(firsts, parts, *rest):
    whole, stage, sems = rest[-3:]
    peers, group, blocks, _ = parts.shape
    count = blocks // len(firsts)
    rows = count * EDGE
    copies = []
    for k, first in enumerate(firsts):
        for side in (0, 1):
            for peer in range(side, peers, 2):
                for s in range(group):
                    at = pl.ds(s * rows + peer // 2, count, stride=EDGE)
                    stage[k, side, at, :] = parts[peer, s, k * count : (k + 1) * count]
            copy = pltpu.make_async_copy(
                stage.at[k, side].reshape(group, rows, LANES),
                whole.at[:, pl.ds(first, rows), pl.ds(side * LANES, LANES)],
                sems.at[2 * k + side],
            )
            copy.start()
            copies.append(copy)
    wait_all(copies)


def place_rows(parts, firsts, rows, *whole):
    peers, group, blocks, _ = parts.shape
    hbm = pl.BlockSpec(memory_space=pltpu.HBM)
    count = len(firsts)
    return pl.pallas_call(
        functools.partial(place_kernel, firsts),
        out_shape=pltpu.HBM((group, rows, 2 * LANES), f32),
        in_specs=[pl.BlockSpec(memory_space=pltpu.VMEM)] + [hbm] * len(whole),
        out_specs=hbm,
        scratch_shapes=[
            pltpu.VMEM((count, 2, group * blocks // count * EDGE, LANES), f32),
            pltpu.SemaphoreType.DMA((2 * count,)),
        ],
        input_output_aliases={1: 0} if whole else {},
        name="place",
    )(pltpu.with_memory_space_constraint(parts, pltpu.VMEM), *whole)


def per_device(
    concentrations,
    diffusion,
    courant_x,
    courant_y,
    log_rate,
    reactants,
    products,
    block_class,
    send_slot,
):
    group, rows, columns = concentrations.shape
    species, reactions = reactants.shape
    peers = species // group
    regions = lax.axis_size("region")
    up = [(i, (i + 1) % regions) for i in range(regions - 1)]
    down = [(j, i) for i, j in up]
    hbm = pl.BlockSpec(memory_space=pltpu.HBM)
    smem = pl.BlockSpec(memory_space=pltpu.SMEM)
    vmem = pl.BlockSpec(memory_space=pltpu.VMEM)
    places = rows // (2 * EDGE)
    lines = EDGE * group

    def buffers(slab_rows):
        row_buffer = pltpu.VMEM((slab_rows, group, columns), f32)
        return [pltpu.VMEM((10, slab_rows, LANES), f32), row_buffer, row_buffer]

    def in_hbm(*arrays):
        return [pltpu.with_memory_space_constraint(v, pltpu.HBM) for v in arrays]

    def in_vmem(*arrays):
        return [pltpu.with_memory_space_constraint(v, pltpu.VMEM) for v in arrays]

    fields = in_hbm(concentrations, courant_x, courant_y)
    slab_rows = rows // 2 + 2 * EDGE
    rim = pltpu.VMEM((group + 2, EDGE, columns), f32)
    last, leading = pl.pallas_call(
        rim_kernel,
        out_shape=(rim, rim),
        in_specs=[hbm] * 3,
        out_specs=(vmem, vmem),
        scratch_shapes=[pltpu.SemaphoreType.DMA((6,))],
        name="rims",
    )(*fields)
    before = lax.ppermute(last, "region", up)
    after = lax.ppermute(leading, "region", down)

    middle, token = pl.pallas_call(
        middle_kernel,
        grid=(1,),
        out_shape=(pltpu.HBM((peers, lines + EDGE, LANES), f32), pltpu.VMEM((EDGE, LANES), f32)),
        in_specs=[hbm] * 6,
        out_specs=(pl.BlockSpec((peers, lines + EDGE, LANES), lambda i: (0, 0, 0)), vmem),
        scratch_shapes=[
            pltpu.SMEM((group,), f32),
            pltpu.SMEM((2 * EDGE,), jnp.int32),
            pltpu.SMEM((2 * EDGE,), jnp.int32),
            pltpu.VMEM((2, group, slab_rows, LANES), f32),
            pltpu.VMEM((slab_rows, columns), f32),
            pltpu.VMEM((slab_rows, columns), f32),
            *buffers(slab_rows),
            pltpu.SemaphoreType.DMA((7,)),
        ],
        compiler_params=pltpu.CompilerParams(vmem_limit_bytes=16 << 20),
        name="middle",
    )(*in_hbm(diffusion, block_class, send_slot), *fields)

    turn = lax.ppermute(token, "region", [(k + 1, k) for k in range(0, regions - 1, 2)])
    place = jnp.stack([lax.axis_index("region"), jnp.int32(regions)]).astype(jnp.int32)
    table_inputs = in_hbm(log_rate, reactants, products)
    table_shapes = (
        pltpu.VMEM((log_rate.shape[0], reactions, LANES), f32),
        pltpu.VMEM((3 * species, reactions), bf16),
    )
    early = pl.pallas_call(
        turn_kernel,
        out_shape=(
            pltpu.HBM((log_rate.shape[0], reactions, LANES), f32),
            pltpu.HBM((3 * species, reactions), bf16),
        ),
        in_specs=[smem, vmem, hbm, hbm, hbm],
        out_specs=(hbm, hbm),
        scratch_shapes=[
            *[pltpu.VMEM(v.shape, v.dtype) for v in (log_rate, reactants, products)],
            *table_shapes,
            pltpu.SemaphoreType.DMA((3,)),
        ],
        name="turn",
    )(place, *in_vmem(turn), *table_inputs)
    first_part, *early = lax.optimization_barrier((middle, *early))
    slab_rows = rows // 4 + 2 * EDGE
    edges, *tables = pl.pallas_call(
        edge_kernel,
        grid=(1,),
        out_shape=(
            pltpu.HBM((peers, lines, LANES), f32),
            *table_shapes,
        ),
        in_specs=[smem] + [hbm] * 4 + [vmem] * 3 + [
            pl.BlockSpec(v.shape, lambda i: (0, 0)) for v in (log_rate, reactants, products)
        ] + [hbm, hbm],
        out_specs=(pl.BlockSpec((peers, lines, LANES), lambda i: (0, 0, 0)), vmem, vmem),
        scratch_shapes=[
            pltpu.SMEM((group,), f32),
            pltpu.VMEM((2, 2, group, slab_rows, LANES), f32),
            pltpu.VMEM((2, slab_rows, columns), f32),
            pltpu.VMEM((2, slab_rows, columns), f32),
            *buffers(slab_rows),
            pltpu.SemaphoreType.DMA((19,)),
        ],
        compiler_params=pltpu.CompilerParams(vmem_limit_bytes=24 << 20),
        cost_estimate=pl.CostEstimate(
            flops=20 * 10**9, transcendentals=0, bytes_accessed=10 << 20
        ),
        name="edges",
    )(place, *in_hbm(diffusion), *fields, before, after, token, *table_inputs, *in_hbm(*early))

    mine = lax.axis_index("species").astype(jnp.int32).reshape(1)
    exchange = functools.partial(
        lax.all_to_all, axis_name="species", split_axis=0, concat_axis=0, tiled=True
    )
    done = []
    coded = None
    half = peers // 2
    quarter = half // 2
    for slab, sources in (
        (first_part, ((quarter, half, 0),)),
        (edges, ((0, quarter, 0), (half + quarter, quarter, quarter))),
    ):
        (gathered,) = in_hbm(exchange(slab))
        coded = gathered if coded is None else coded
        reacted = chemistry(gathered, coded, sources, mine, *in_vmem(*tables))
        done.append(exchange(reacted.reshape(peers, group, EDGE, LANES)))
    quarter = rows // 4
    filled = place_rows(done[0], (quarter,), rows)
    return place_rows(done[1], (0, 3 * quarter), rows, filled)


def solution(mesh):
    in_specs = (
        P("species", "region", None),
        P("species"),
        P("region", None),
        P("region", None),
        P(),
        P(),
        P(),
        P(("region", "species")),
        P(("region", "species")),
    )
    out_specs = P("species", "region", None)
    return jax.shard_map(
        per_device, mesh=mesh, in_specs=in_specs, out_specs=out_specs, check_vma=False
    )
```

```python
import functools

import jax
import jax.numpy as jnp
from jax import lax
from jax.experimental import pallas as pl
from jax.experimental.pallas import tpu as pltpu
from jax.sharding import PartitionSpec as P

STEPS = 3
ITERS = 2
SUB = 2
FLOOR = 0.05
EDGE = 8
LANES = 128
TILE = 4
bf16 = jnp.bfloat16
f32 = jnp.float32


def median0(p, r):
    return jnp.maximum(jnp.minimum(p, r), jnp.minimum(jnp.maximum(p, r), 0.0))


def shift_left(pair, lane):
    a, b = (pltpu.roll(v, LANES - 1, 1) for v in pair)
    last = lane == LANES - 1
    return jnp.where(last, b, a), jnp.where(last, 0.0, b)


def shift_right(pair, first, lane):
    a, b = (pltpu.roll(v, 1, 1) for v in pair)
    head = lane == 0
    return jnp.where(head, first, a), jnp.where(head, a, b)


def halves(v):
    return v[:, :LANES], v[:, LANES:]


def face_coefs(a):
    size = jnp.abs(a)
    return 0.5 * size * (1.0 - size)


def store_coefs(cx, cy, coef):
    ax = 0.5 * (cx + jnp.concatenate([cx[1:], cx[:1]], axis=0))
    edge = lax.broadcasted_iota(jnp.int32, cy.shape, 1) == 2 * LANES - 1
    ay = 0.5 * (cy + jnp.where(edge, 0.0, jnp.concatenate([cy[:, 1:], cy[:, :1]], axis=1)))
    al = 0.5 * cy[:, :LANES]
    al_weight = jnp.where(al < 0.0, face_coefs(al), 0.0)
    pairs = [halves(v) for v in (ax, face_coefs(ax), ay, face_coefs(ay))]
    pairs.append((jnp.minimum(al, 0.0), al_weight))
    for k, pair in enumerate(pairs):
        coef[2 * k] = pair[0]
        coef[2 * k + 1] = pair[1]


def one_flux(q, qn, d, m, mn, a, e, nu):
    up = a >= 0.0
    return a * jnp.where(up, q, qn) + e * jnp.where(up, m, mn) - nu * d


def sweep(load, store, coef, nu, lo, hi, unroll, keep=None):
    group = nu.shape[0]
    lane = lax.broadcasted_iota(jnp.int32, (group, LANES), 1)

    def spread(which, row):
        return tuple(coef[2 * which + k, pl.ds(row, group, stride=0), :] for k in (0, 1))

    def x_flux(row, q, qn, d, m, mn):
        a, e = spread(0, row), spread(1, row)
        return tuple(one_flux(q[i], qn[i], d[i], m[i], mn[i], a[i], e[i], nu) for i in (0, 1))

    def diff(q, qn):
        return tuple(y - x for x, y in zip(q, qn))

    def limited(p, r):
        return tuple(median0(x, y) for x, y in zip(p, r))

    qa, qb, qc, qd = (load(lo + k) for k in (-2, -1, 0, 1))
    da, db, dc = diff(qa, qb), diff(qb, qc), diff(qc, qd)
    mb, mc = limited(da, db), limited(db, dc)
    behind = x_flux(lo - 1, qb, qc, db, mb, mc)

    def row_step(row, carry):
        q, qn, d, m, behind = carry
        qnn = load(row + 2)
        dn = diff(qn, qnn)
        mn = limited(d, dn)
        fx = x_flux(row, q, qn, d, m, mn)
        right = shift_left(q, lane)
        g = diff(q, right)
        s = limited(shift_right(g, q[0], lane), g)
        sn = shift_left(s, lane)
        a, e = spread(2, row), spread(3, row)
        fy = tuple(one_flux(q[i], right[i], g[i], s[i], sn[i], a[i], e[i], nu) for i in (0, 1))
        la, le = spread(4, row)
        fl = shift_right(fy, (la - nu) * q[0] + le * s[0], lane)
        new = tuple(q[i] - (fx[i] - behind[i]) - (fy[i] - fl[i]) for i in (0, 1))
        if keep is not None:
            scale = keep(row)
            new = tuple(v * scale for v in new)
        store(row, new)
        return qn, qnn, dn, mn, fx

    def steps(i, carry):
        for k in range(unroll):
            carry = row_step(lo + i * unroll + k, carry)
        return carry

    count = hi - lo
    carry = lax.fori_loop(0, count // unroll, steps, (qc, qd, dc, mc, behind))
    for row in range(lo + count // unroll * unroll, hi):
        carry = row_step(row, carry)


def buffer_access(buf):
    def load(row):
        return buf[row, :, :LANES], buf[row, :, LANES:]

    def store(row, pair):
        buf[row, :, :LANES] = pair[0]
        buf[row, :, LANES:] = pair[1]

    return load, store


def start_all(copies):
    for copy in copies:
        copy.start()


def wait_all(copies):
    for copy in copies:
        copy.wait()


def spread_species(diffuse, group):
    lane = lax.broadcasted_iota(jnp.int32, (group, LANES), 0)
    nu = jnp.zeros((group, LANES), f32)
    for k in range(group):
        nu = jnp.where(lane == k, diffuse[k], nu)
    return nu


def raw_access(block):
    group, rows, _ = block.shape[1:]
    flat = [block.at[k].reshape(group * rows, LANES) for k in (0, 1)]

    def load(row):
        return tuple(part[pl.ds(row, group, stride=rows), :] for part in flat)

    return load


def three_sweeps(load, store, coef, nu, one, two, rows, unrolls, keep=None):
    load1, store1 = buffer_access(one)
    load2, store2 = buffer_access(two)
    sweep(load, store1, coef, nu, 4, rows - 4, unrolls[0], keep)
    sweep(load1, store2, coef, nu, 6, rows - 6, unrolls[1], keep)
    sweep(load2, store, coef, nu, 8, rows - 8, unrolls[2])


def store_grouped(out, base, group):
    def store(row, pair):
        at = row - EDGE
        line = pl.multiple_of((base + lax.shift_right_logical(at, 3)) * group, group)
        peer = 2 * lax.bitwise_and(at, EDGE - 1)
        out[peer, pl.ds(line, group), :] = pair[0]
        out[peer + 1, pl.ds(line, group), :] = pair[1]

    return store


def rim_kernel(conc, cx, cy, last, leading, sems):
    group, total, _ = conc.shape
    copies = []

    def copy(src, dst):
        copies.append(pltpu.make_async_copy(src, dst, sems.at[len(copies)]))

    for rim, at in ((last, total - EDGE), (leading, 0)):
        copy(conc.at[:, pl.ds(at, EDGE)], rim.at[pl.ds(0, group)])
        copy(cx.at[pl.ds(at, EDGE)], rim.at[group])
        copy(cy.at[pl.ds(at, EDGE)], rim.at[group + 1])
    start_all(copies)
    wait_all(copies)


def middle_kernel(
    diffuse_in,
    classes_in,
    slots_in,
    conc,
    cx,
    cy,
    out,
    token,
    diffuse,
    classes,
    slots,
    raw,
    wx,
    wy,
    coef,
    one,
    two,
    sems,
):
    group, rows = raw.shape[1:3]
    total = conc.shape[1]
    first = total // 4 - EDGE
    pairs = [(cx.at[pl.ds(first, rows)], wx), (cy.at[pl.ds(first, rows)], wy)]
    pairs += [
        (conc.at[:, pl.ds(first, rows), pl.ds(k * LANES, LANES)], raw.at[k]) for k in (0, 1)
    ]
    pairs += [(diffuse_in, diffuse), (classes_in, classes), (slots_in, slots)]
    copies = [pltpu.make_async_copy(*pair, sems.at[k]) for k, pair in enumerate(pairs)]
    start_all(copies)
    wait_all(copies[4:7])
    nu = spread_species(diffuse, group)
    lane = lax.broadcasted_iota(jnp.int32, (EDGE, LANES), 1)
    codes = jnp.zeros((EDGE, LANES), f32)
    for k in range(classes.shape[0]):
        code = classes[k] + jnp.where(slots[k] >= 0, 4, 0)
        codes = jnp.where(lane == k, code.astype(f32), codes)
    for k in range(out.shape[0]):
        out[k, EDGE * group :, :] = codes
    wait_all(copies[:2])
    store_coefs(wx[...], wy[...], coef)
    wait_all(copies[2:4])
    three_sweeps(
        raw_access(raw), store_grouped(out, 0, group), coef, nu, one, two, rows, (18, 17, 16)
    )
    token[...] = codes


def edge_kernel(
    place,
    diffuse_in,
    conc,
    cx,
    cy,
    before,
    after,
    _token,
    log_rate_in,
    reactants_in,
    products_in,
    early_log_table,
    early_both,
    out,
    log_table,
    both,
    log_rate,
    reactants,
    products,
    diffuse,
    raw,
    wx,
    wy,
    coef,
    one,
    two,
    sems,
):
    group, rows = raw.shape[2:4]
    total = conc.shape[1]
    own = rows - EDGE
    copies = []

    def copy(src, dst):
        copies.append(pltpu.make_async_copy(src, dst, sems.at[len(copies)]))

    copy(diffuse_in, diffuse)
    for slab, halo, own_first, own_at, halo_at in (
        (0, before, 0, EDGE, 0),
        (1, after, total - own, 0, own),
    ):
        for k, (wind, dst) in enumerate(((cx, wx), (cy, wy))):
            copy(wind.at[pl.ds(own_first, own)], dst.at[slab, pl.ds(own_at, own)])
            copy(halo.at[group + k], dst.at[slab, pl.ds(halo_at, EDGE)])
        for k in (0, 1):
            lanes = pl.ds(k * LANES, LANES)
            dst = raw.at[slab, k]
            copy(conc.at[:, pl.ds(own_first, own), lanes], dst.at[:, pl.ds(own_at, own)])
            copy(halo.at[pl.ds(0, group), :, lanes], dst.at[:, pl.ds(halo_at, EDGE)])
    start_all(copies)

    @pl.when(lax.rem(place[0], 2) == 1)
    def _():
        inputs = [
            pltpu.make_async_copy(src, dst, sems.at[len(copies) + k])
            for k, (src, dst) in enumerate(
                ((log_rate_in, log_rate), (reactants_in, reactants), (products_in, products))
            )
        ]
        start_all(inputs)
        wait_all(inputs)
        table_kernel(log_rate, reactants, products, log_table, both)

    @pl.when(lax.rem(place[0], 2) == 0)
    def _():
        early = [
            pltpu.make_async_copy(src, dst, sems.at[len(copies) + k])
            for k, (src, dst) in enumerate(((early_log_table, log_table), (early_both, both)))
        ]
        start_all(early)
        wait_all(early)

    wait_all(copies)
    nu = spread_species(diffuse, group)

    @pl.loop(0, 2)
    def _(slab):
        store_coefs(wx[slab], wy[slab], coef)
        open_top = jnp.logical_and(slab == 0, place[0] == 0)
        open_end = jnp.logical_and(slab == 1, place[0] == place[1] - 1)

        def keep(row):
            outside = jnp.logical_or(
                jnp.logical_and(open_top, row < EDGE), jnp.logical_and(open_end, row >= own)
            )
            return jnp.where(outside, 0.0, 1.0)

        three_sweeps(
            raw_access(raw.at[slab]),
            store_grouped(out, slab * 4, group),
            coef,
            nu,
            one,
            two,
            rows,
            (10, 12, 16),
            keep,
        )


def split(x):
    high = x.astype(bf16)
    return high, (x - high.astype(f32)).astype(bf16)


def table_dot(table, x):
    high, low = split(x)
    return jnp.dot(table, high, preferred_element_type=f32) + jnp.dot(
        table, low, preferred_element_type=f32
    )


def blocks_dot(blocks, x):
    size = x.shape[0]
    high, low = split(x)
    parts = [blocks[:, k : k + size] for k in range(0, blocks.shape[1], size)]
    return jnp.concatenate(
        [
            jnp.dot(part, high, preferred_element_type=f32)
            + jnp.dot(part, low, preferred_element_type=f32)
            for part in parts
        ],
        axis=0,
    )


def euler(state, logs, step, both):
    species = state.shape[0]
    reac = both[2 * species :]
    both = both[: 2 * species]
    g = state
    for _ in range(ITERS):
        rates = jnp.exp(logs + blocks_dot(reac, jnp.log(g)))
        made_lost = table_dot(both, rates)
        g = (state + step * made_lost[:species]) / (1.0 + step * made_lost[species:] / g)
    return g


def turn_kernel(place, _turn, log_rate_in, reactants_in, products_in, log_table, both, *rest):
    buffers, made, sems = rest[:3], rest[3:5], rest[5]

    @pl.when(lax.rem(place[0], 2) == 0)
    def _():
        copies = [
            pltpu.make_async_copy(src, dst, sems.at[k])
            for k, (src, dst) in enumerate(
                zip((log_rate_in, reactants_in, products_in), buffers)
            )
        ]
        start_all(copies)
        wait_all(copies)
        table_kernel(*buffers, *made)
        copies = [
            pltpu.make_async_copy(src, dst, sems.at[k])
            for k, (src, dst) in enumerate(zip(made, (log_table, both)))
        ]
        start_all(copies)
        wait_all(copies)


def first_line(block, group):
    return block * group if isinstance(block, int) else pl.multiple_of(block * group, group)


def table_kernel(log_rate, reactants, products, log_table, both):
    species, reactions = reactants.shape
    reactant = reactants[...].astype(f32)
    both[:species] = products[...].astype(f32).T.astype(bf16)
    both[species : 2 * species] = reactant.astype(bf16)
    for k in range(0, reactions, species):
        both[2 * species :, k : k + species] = reactant[:, k : k + species].T.astype(bf16)
    for k in range(log_rate.shape[0]):
        log_table[k] = jnp.broadcast_to(log_rate[k : k + 1, :], (LANES, reactions)).T


def turn_kernel(place, _turn, log_rate_in, reactants_in, products_in, log_table, both, *rest):
    buffers, made, sems = rest[:3], rest[3:5], rest[5]

    @pl.when(lax.rem(place[0], 2) == 0)
    def _():
        copies = [
            pltpu.make_async_copy(src, dst, sems.at[k])
            for k, (src, dst) in enumerate(
                zip((log_rate_in, reactants_in, products_in), buffers)
            )
        ]
        start_all(copies)
        wait_all(copies)
        table_kernel(*buffers, *made)
        copies = [
            pltpu.make_async_copy(src, dst, sems.at[k])
            for k, (src, dst) in enumerate(zip(made, (log_table, both)))
        ]
        start_all(copies)
        wait_all(copies)


def first_line(block, group):
    return block * group if isinstance(block, int) else pl.multiple_of(block * group, group)


def table_kernel(log_rate, reactants, products, log_table, both):
    species, reactions = reactants.shape
    reactant = reactants[...].astype(f32)
    both[:species] = products[...].astype(f32).T.astype(bf16)
    both[species : 2 * species] = reactant.astype(bf16)
    for k in range(0, reactions, species):
        both[2 * species :, k : k + species] = reactant[:, k : k + species].T.astype(bf16)
    for k in range(log_rate.shape[0]):
        log_table[k] = jnp.broadcast_to(log_rate[k : k + 1, :], (LANES, reactions)).T


def tables_of(log_rate, reactants, products):
    species, reactions = reactants.shape
    classes = log_rate.shape[0]
    vmem = pl.BlockSpec(memory_space=pltpu.VMEM)
    return pl.pallas_call(
        table_kernel,
        grid=(1,),
        out_shape=[
            pltpu.VMEM((classes, reactions, LANES), f32),
            pltpu.VMEM((3 * species, reactions), bf16),
        ],
        in_specs=[
            pl.BlockSpec((classes, reactions), lambda i: (0, 0)),
            pl.BlockSpec((species, reactions), lambda i: (0, 0)),
            pl.BlockSpec((reactions, species), lambda i: (0, 0)),
        ],
        out_specs=[vmem] * 3,
        compiler_params=pltpu.CompilerParams(vmem_limit_bytes=12 << 20),
        name="tables",
    )(log_rate, reactants, products)


def code_class(code):
    return sum((code >= float(k)).astype(jnp.int32) for k in (5, 6, 7))


def chemistry_kernel(
    sources, mine, x_in, coded, log_table, both, out, x, codes, result, answer, listed, sems
):
    peers, lines, _ = x.shape
    blocks = EDGE
    group = lines // blocks
    species = peers * group
    size = TILE * group

    def part(i):
        at = pl.ds(first_line(i, size), size)
        return pltpu.make_async_copy(x_in.at[:, at, :], x.at[:, at, :], sems.at[i])

    copies = []
    for first, count, at in sources:
        copies.append(
            pltpu.make_async_copy(
                coded.at[pl.ds(first, count), pl.ds(lines, EDGE), :],
                codes.at[pl.ds(at, count)],
                sems.at[blocks // TILE + len(copies)],
            )
        )
    start_all(copies + [part(i) for i in range(blocks // TILE)])
    wait_all(copies)
    count = jnp.int32(0)
    for b in range(blocks):
        code = codes[b, 0, mine[0]]
        stiff = (code >= 4.0).astype(jnp.int32)
        lower = sum((code >= float(k)).astype(jnp.int32) for k in (1, 2, 3))
        listed[1, b] = jnp.where(code >= 4.0, code_class(code), lower)
        listed[2, b] = stiff
        listed[0, count] = b
        count = count + stiff

    def tile(chosen, first):
        states, logs, lengths = [], [], []
        for b in chosen:
            if first:
                states.append(jnp.maximum(x[:, pl.ds(first_line(b, group), group), :].reshape(species, LANES), FLOOR))
                length = jnp.where(listed[2, b] > 0, 1.0 / SUB, 1.0)
            else:
                states.append(result[b])
                length = 1.0 / SUB
            lengths.append(jnp.full((1, LANES), length, f32))
            logs.append(log_table[listed[1, b]])
        g = euler(
            jnp.concatenate(states, axis=1),
            jnp.concatenate(logs, axis=1),
            jnp.concatenate(lengths, axis=1),
            both[...],
        )
        for i, b in enumerate(chosen):
            piece = g[:, i * LANES : (i + 1) * LANES]
            result[b] = piece
            for k in range(0, species, 8):
                answer[pl.ds(k * blocks + b, 8, stride=blocks), :] = piece[k : k + 8]

    @pl.loop(0, blocks // TILE)
    def _(i):
        part(i).wait()
        tile([i * TILE + j for j in range(TILE)], True)

    for _ in range(SUB - 1):

        @pl.loop(0, (count + TILE - 1) // TILE)
        def _(i):
            tile([listed[0, jnp.minimum(i * TILE + j, count - 1)] for j in range(TILE)], False)


    copy = pltpu.make_async_copy(answer, out, sems.at[0])
    copy.start()
    copy.wait()


def chemistry(x, coded, sources, mine, log_table, both):
    peers = x.shape[0]
    species, blocks = both.shape[0] // 3, EDGE
    vmem = pl.BlockSpec(memory_space=pltpu.VMEM)
    smem = pl.BlockSpec(memory_space=pltpu.SMEM)
    hbm = pl.BlockSpec(memory_space=pltpu.HBM)
    return pl.pallas_call(
        functools.partial(chemistry_kernel, sources),
        out_shape=pltpu.HBM((species * blocks, LANES), f32),
        in_specs=[smem, hbm, hbm, vmem, vmem],
        out_specs=hbm,
        scratch_shapes=[
            pltpu.VMEM((peers, species // peers * blocks, LANES), f32),
            pltpu.SMEM((blocks, EDGE, LANES), f32),
            pltpu.VMEM((blocks, species, LANES), f32),
            pltpu.VMEM((species * blocks, LANES), f32),
            pltpu.SMEM((3, blocks), jnp.int32),
            pltpu.SemaphoreType.DMA((blocks // TILE + len(sources),)),
        ],
        compiler_params=pltpu.CompilerParams(vmem_limit_bytes=14 << 20),
        name="chemistry",
    )(mine, x, coded, log_table, both)


def place_kernel(firsts, parts, *rest):
    whole, stage, sems = rest[-3:]
    peers, group, blocks, _ = parts.shape
    count = blocks // len(firsts)
    rows = count * EDGE
    copies = []
    for k, first in enumerate(firsts):
        for side in (0, 1):
            for peer in range(side, peers, 2):
                for s in range(group):
                    at = pl.ds(s * rows + peer // 2, count, stride=EDGE)
                    stage[k, side, at, :] = parts[peer, s, k * count : (k + 1) * count]
            copy = pltpu.make_async_copy(
                stage.at[k, side].reshape(group, rows, LANES),
                whole.at[:, pl.ds(first, rows), pl.ds(side * LANES, LANES)],
                sems.at[2 * k + side],
            )
            copy.start()
            copies.append(copy)
    wait_all(copies)


def place_rows(parts, firsts, rows, *whole):
    peers, group, blocks, _ = parts.shape
    hbm = pl.BlockSpec(memory_space=pltpu.HBM)
    count = len(firsts)
    return pl.pallas_call(
        functools.partial(place_kernel, firsts),
        out_shape=pltpu.HBM((group, rows, 2 * LANES), f32),
        in_specs=[pl.BlockSpec(memory_space=pltpu.VMEM)] + [hbm] * len(whole),
        out_specs=hbm,
        scratch_shapes=[
            pltpu.VMEM((count, 2, group * blocks // count * EDGE, LANES), f32),
            pltpu.SemaphoreType.DMA((2 * count,)),
        ],
        input_output_aliases={1: 0} if whole else {},
        name="place",
    )(pltpu.with_memory_space_constraint(parts, pltpu.VMEM), *whole)


def per_device(
    concentrations,
    diffusion,
    courant_x,
    courant_y,
    log_rate,
    reactants,
    products,
    block_class,
    send_slot,
):
    group, rows, columns = concentrations.shape
    species, reactions = reactants.shape
    peers = species // group
    regions = lax.axis_size("region")
    up = [(i, (i + 1) % regions) for i in range(regions - 1)]
    down = [(j, i) for i, j in up]
    hbm = pl.BlockSpec(memory_space=pltpu.HBM)
    smem = pl.BlockSpec(memory_space=pltpu.SMEM)
    vmem = pl.BlockSpec(memory_space=pltpu.VMEM)
    places = rows // (2 * EDGE)
    lines = EDGE * group

    def buffers(slab_rows):
        row_buffer = pltpu.VMEM((slab_rows, group, columns), f32)
        return [pltpu.VMEM((10, slab_rows, LANES), f32), row_buffer, row_buffer]

    def in_hbm(*arrays):
        return [pltpu.with_memory_space_constraint(v, pltpu.HBM) for v in arrays]

    def in_vmem(*arrays):
        return [pltpu.with_memory_space_constraint(v, pltpu.VMEM) for v in arrays]

    fields = in_hbm(concentrations, courant_x, courant_y)
    slab_rows = rows // 2 + 2 * EDGE
    rim = pltpu.VMEM((group + 2, EDGE, columns), f32)
    last, leading = pl.pallas_call(
        rim_kernel,
        out_shape=(rim, rim),
        in_specs=[hbm] * 3,
        out_specs=(vmem, vmem),
        scratch_shapes=[pltpu.SemaphoreType.DMA((6,))],
        name="rims",
    )(*fields)
    before = lax.ppermute(last, "region", up)
    after = lax.ppermute(leading, "region", down)

    middle, token = pl.pallas_call(
        middle_kernel,
        grid=(1,),
        out_shape=(pltpu.HBM((peers, lines + EDGE, LANES), f32), pltpu.VMEM((EDGE, LANES), f32)),
        in_specs=[hbm] * 6,
        out_specs=(pl.BlockSpec((peers, lines + EDGE, LANES), lambda i: (0, 0, 0)), vmem),
        scratch_shapes=[
            pltpu.SMEM((group,), f32),
            pltpu.SMEM((2 * EDGE,), jnp.int32),
            pltpu.SMEM((2 * EDGE,), jnp.int32),
            pltpu.VMEM((2, group, slab_rows, LANES), f32),
            pltpu.VMEM((slab_rows, columns), f32),
            pltpu.VMEM((slab_rows, columns), f32),
            *buffers(slab_rows),
            pltpu.SemaphoreType.DMA((7,)),
        ],
        compiler_params=pltpu.CompilerParams(vmem_limit_bytes=16 << 20),
        name="middle",
    )(*in_hbm(diffusion, block_class, send_slot), *fields)

    turn = lax.ppermute(token, "region", [(k + 1, k) for k in range(0, regions - 1, 2)])
    place = jnp.stack([lax.axis_index("region"), jnp.int32(regions)]).astype(jnp.int32)
    table_inputs = in_hbm(log_rate, reactants, products)
    table_shapes = (
        pltpu.VMEM((log_rate.shape[0], reactions, LANES), f32),
        pltpu.VMEM((3 * species, reactions), bf16),
    )
    early = pl.pallas_call(
        turn_kernel,
        out_shape=(
            pltpu.HBM((log_rate.shape[0], reactions, LANES), f32),
            pltpu.HBM((3 * species, reactions), bf16),
        ),
        in_specs=[smem, vmem, hbm, hbm, hbm],
        out_specs=(hbm, hbm),
        scratch_shapes=[
            *[pltpu.VMEM(v.shape, v.dtype) for v in (log_rate, reactants, products)],
            *table_shapes,
            pltpu.SemaphoreType.DMA((3,)),
        ],
        name="turn",
    )(place, *in_vmem(turn), *table_inputs)
    first_part, *early = lax.optimization_barrier((middle, *early))
    slab_rows = rows // 4 + 2 * EDGE
    edges, *tables = pl.pallas_call(
        edge_kernel,
        grid=(1,),
        out_shape=(
            pltpu.HBM((peers, lines, LANES), f32),
            *table_shapes,
        ),
        in_specs=[smem] + [hbm] * 4 + [vmem] * 3 + [hbm] * 5,
        out_specs=(pl.BlockSpec((peers, lines, LANES), lambda i: (0, 0, 0)), vmem, vmem),
        scratch_shapes=[
            *[pltpu.VMEM(v.shape, v.dtype) for v in (log_rate, reactants, products)],
            pltpu.SMEM((group,), f32),
            pltpu.VMEM((2, 2, group, slab_rows, LANES), f32),
            pltpu.VMEM((2, slab_rows, columns), f32),
            pltpu.VMEM((2, slab_rows, columns), f32),
            *buffers(slab_rows),
            pltpu.SemaphoreType.DMA((20,)),
        ],
        compiler_params=pltpu.CompilerParams(vmem_limit_bytes=24 << 20),
        cost_estimate=pl.CostEstimate(
            flops=20 * 10**9, transcendentals=0, bytes_accessed=10 << 20
        ),
        name="edges",
    )(place, *in_hbm(diffusion), *fields, before, after, token, *table_inputs, *in_hbm(*early))

    mine = lax.axis_index("species").astype(jnp.int32).reshape(1)
    exchange = functools.partial(
        lax.all_to_all, axis_name="species", split_axis=0, concat_axis=0, tiled=True
    )
    done = []
    coded = None
    half = peers // 2
    quarter = half // 2
    for slab, sources in (
        (first_part, ((quarter, half, 0),)),
        (edges, ((0, quarter, 0), (half + quarter, quarter, quarter))),
    ):
        (gathered,) = in_hbm(exchange(slab))
        coded = gathered if coded is None else coded
        reacted = chemistry(gathered, coded, sources, mine, *in_vmem(*tables))
        done.append(exchange(reacted.reshape(peers, group, EDGE, LANES)))
    quarter = rows // 4
    filled = place_rows(done[0], (quarter,), rows)
    return place_rows(done[1], (0, 3 * quarter), rows, filled)


def solution(mesh):
    in_specs = (
        P("species", "region", None),
        P("species"),
        P("region", None),
        P("region", None),
        P(),
        P(),
        P(),
        P(("region", "species")),
        P(("region", "species")),
    )
    out_specs = P("species", "region", None)
    return jax.shard_map(
        per_device, mesh=mesh, in_specs=in_specs, out_specs=out_specs, check_vma=False
    )
```
